32 devices in a mesh: batch: 8 (over z, x), tp: 4 (over y, core).
Axes of the slice: x: 2, y: 2, z: 4, core: 2. Of those that a mesh axis runs over, the one named last changes fastest.
Arguments:
- tokens: bfloat16 [12288, 768], P('batch'), may hold values from -6 to 6
- w_query: bfloat16 [768, 768], P(None, 'tp'), may hold values from -0.3125 to 0.3125
- b_query: float32 [768], P('tp'), may hold values from -3 to 3
- w_key: bfloat16 [768, 768], P(None, 'tp'), may hold values from -0.3125 to 0.3125
- w_value: bfloat16 [768, 768], P(None, 'tp'), may hold values from -0.21875 to 0.21875
- b_value: float32 [768], P('tp'), may hold values from -2 to 2
- w_attn_out: bfloat16 [768, 768], P('tp'), may hold values from -0.875 to 0.875
- b_attn_out: float32 [768], replicated, may hold values from -3 to 3
- gain_one: float32 [768], replicated, may hold values from 0.5 to 1.5
- bias_one: float32 [768], replicated, may hold values from -3 to 3
- w_in: bfloat16 [768, 3072], P(None, 'tp'), may hold values from -0.21875 to 0.21875
- b_in: float32 [3072], P('tp'), may hold values from -3 to 3
- w_out: bfloat16 [3072, 768], P('tp'), may hold values from -0.15625 to 0.15625
- b_out: float32 [768], replicated, may hold values from -3 to 3
- gain_two: float32 [768], replicated, may hold values from 0.5 to 1.5
- bias_two: float32 [768], replicated, may hold values from -3 to 3
- lengths: int32 [24], P('batch'), may hold values from 8 to 512, as said below
- grad_out: bfloat16 [12288, 768], P('batch'), may hold values from -6 to 6
Outputs:
- layer_out: bfloat16 [12288, 768], P(('batch', 'tp'))
- pooled: float32 [24, 1728], P('batch')
- grad_tokens: bfloat16 [12288, 768], P(('batch', 'tp'))
- grad_w_query: float32 [768, 768], P(None, 'tp')
- grad_b_query: float32 [768], P('tp')
- grad_w_key: float32 [768, 768], P(None, 'tp')
- grad_w_value: float32 [768, 768], P(None, 'tp')
- grad_b_value: float32 [768], P('tp')
- grad_w_attn_out: float32 [768, 768], P('tp')
- grad_b_attn_out: float32 [768], replicated
- grad_gain_one: float32 [768], replicated
- grad_bias_one: float32 [768], replicated
- grad_w_in: float32 [768, 3072], P(None, 'tp')
- grad_b_in: float32 [3072], P('tp')
- grad_w_out: float32 [3072, 768], P('tp')
- grad_b_out: float32 [768], replicated
- grad_gain_two: float32 [768], replicated
- grad_bias_two: float32 [768], replicated
The draws below stay inside these ranges and needn't reach their ends.
Inputs may be any that keep to these rules, and one draw needn't show every extreme that they name: `lengths`: some sentence has exactly 512 tokens and some has exactly 8.
All inputs are finite; a program needn't handle non-finite values.
Results may differ from the reference program's by a relative error of at most 0.02.
The reference program's roundings to bfloat16 on the way count: a program that leaves them out, or rounds other values in their place, can miss the bound.
Values may be sent and summed in bfloat16 or wider, within the bound.
A program may use at most 128 MiB of HBM per device.

```python
import jax
import jax.numpy as jnp
from jax import lax

D = 768
HEADS = 12
HEAD = 64
FF = 3072
SEQ_LEN = 512
SEQS = 24
TOKENS = 12288


def draw_lengths(key, part):
    key_left, key_right, key_long, key_short = jax.random.split(key, 4)
    length_span = SEQ_LEN - 8
    left_draw = jax.random.randint(key_left, (SEQS,), 0, length_span + 1)
    right_draw = jax.random.randint(key_right, (SEQS,), 0, length_span + 1)
    drawn = SEQ_LEN - left_draw * right_draw // length_span
    long_place = jax.random.randint(key_long, (), 0, SEQS)
    short_place = (long_place + 1 + jax.random.randint(key_short, (), 0, SEQS - 1)) % SEQS
    places = jnp.arange(SEQS, dtype=jnp.int32)
    drawn = jnp.where(places == long_place, SEQ_LEN, drawn)
    drawn = jnp.where(places == short_place, 8, drawn)
    return drawn.astype(jnp.int32)


def shard_levels(stream_key, shape, shards, least, high):
    def one(axis_at, shards_of):
        draws = jax.random.uniform(jax.random.fold_in(jax.random.fold_in(stream_key, 6), axis_at), (shards_of,), jnp.float32, least / len(shards), high / len(shards))
        return jnp.repeat(jnp.exp(draws), shape[axis_at] // shards_of).reshape((-1,) + (1,) * (len(shape) - axis_at - 1))

    level = one(*shards[0])
    for cut in shards[1:]:
        level = level * one(*cut)
    return level


def noise(rng, dims, deviation, reach, cuts=(), kind=jnp.bfloat16):
    loudness = shard_levels(rng, dims, cuts, -0.22, 0.18) if cuts else 1.0
    values = jax.random.normal(rng, dims, jnp.float32) * deviation * loudness
    return jnp.minimum(jnp.maximum(values, -reach), reach).astype(kind)


def setup_inputs(seed: int = 0) -> dict:
    seeds = jax.random.split(jax.random.key(seed), 19)
    tokens = noise(seeds[0], (TOKENS, D), 1.0, 6.0, ((0, 8),))
    w_query = noise(seeds[1], (D, D), (D // 2) ** -0.5, 0.3125, ((1, 4),))
    b_query = noise(seeds[2], (D,), 0.5, 3.0, ((0, 4),), jnp.float32)
    w_key = noise(seeds[3], (D, D), (D // 2) ** -0.5, 0.3125, ((1, 4),))
    w_value = noise(seeds[4], (D, D), D ** -0.5, 0.21875, ((1, 4),))
    b_value = noise(seeds[5], (D,), 0.3, 2.0, ((0, 4),), jnp.float32)
    w_attn_out = noise(seeds[6], (D, D), (D // 16) ** -0.5, 0.875, ((0, 4),))
    b_attn_out = noise(seeds[7], (D,), 0.5, 3.0, (), jnp.float32)
    gain_one = jnp.clip(1.0 + 0.1 * jax.random.normal(seeds[8], (D,), jnp.float32), 0.5, 1.5)
    bias_one = noise(seeds[9], (D,), 0.5, 3.0, (), jnp.float32)
    w_in = noise(seeds[10], (D, FF), D ** -0.5, 0.21875, ((1, 4),))
    b_in = noise(seeds[11], (FF,), 0.5, 3.0, ((0, 4),), jnp.float32)
    w_out = noise(seeds[12], (FF, D), (FF // 2) ** -0.5, 0.15625, ((0, 4),))
    b_out = noise(seeds[13], (D,), 0.5, 3.0, (), jnp.float32)
    gain_two = jnp.clip(1.0 + 0.1 * jax.random.normal(seeds[14], (D,), jnp.float32), 0.5, 1.5)
    bias_two = noise(seeds[15], (D,), 0.5, 3.0, (), jnp.float32)
    lengths = draw_lengths(jax.random.fold_in(seeds[18], 71), 0)
    grad_out = noise(seeds[17], (TOKENS, D), 1.0, 6.0, ((0, 8),))
    return dict(tokens=tokens, w_query=w_query, b_query=b_query, w_key=w_key, w_value=w_value, b_value=b_value, w_attn_out=w_attn_out, b_attn_out=b_attn_out, gain_one=gain_one, bias_one=bias_one, w_in=w_in, b_in=b_in, w_out=w_out, b_out=b_out, gain_two=gain_two, bias_two=bias_two, lengths=lengths, grad_out=grad_out)


@jax.custom_vjp
def low(v):
    return lax.optimization_barrier(v.astype(jnp.bfloat16)).astype(jnp.float32)

@jax.custom_vjp
def low_back(v):
    return v

def low_keep(v):
    return (low(v), None)

def low_pass(kept, grad):
    return (grad,)

def back_keep(v):
    return (v, None)

def back_low(kept, grad):
    return (low(grad),)
low.defvjp(low_keep, low_pass)
low_back.defvjp(back_keep, back_low)
EPSILON = 1e-06

def highest_dot(left_side, right_side):
    return jnp.dot(left_side, right_side, precision=lax.Precision.HIGHEST, preferred_element_type=jnp.float32)

def layer_norm(residual, gain_vec, bias_vec):
    average = lax.optimization_barrier(jnp.mean(residual, axis=-1, keepdims=True))
    centred = residual - average
    spread = lax.optimization_barrier(jnp.mean(centred * centred, axis=-1, keepdims=True))
    return centred * lax.rsqrt(spread + EPSILON) * gain_vec + bias_vec

def attend_sentence(pieces):
    queries, key_rows, value_rows, seq_length = pieces
    query_heads = queries.reshape(SEQ_LEN, HEADS, HEAD)
    key_heads = key_rows.reshape(SEQ_LEN, HEADS, HEAD)
    value_heads = value_rows.reshape(SEQ_LEN, HEADS, HEAD)
    raw_scores = jnp.einsum('qhd,khd->hqk', query_heads, key_heads, precision=lax.Precision.HIGHEST) * HEAD ** (-0.5)
    raw_scores = low_back(raw_scores)
    allowed = jnp.arange(SEQ_LEN, dtype=jnp.int32) < seq_length
    scores = jnp.where(allowed[None, None, :], raw_scores, -1e+30)
    shares = low(jax.nn.softmax(scores, axis=-1))
    context = jnp.einsum('hqk,khd->qhd', shares, value_heads, precision=lax.Precision.HIGHEST)
    return context.reshape(SEQ_LEN, D)

def forward(inputs, w_query, b_query, w_key, w_value, b_value, w_attn_out, b_attn_out, gain_one, bias_one, w_in, b_in, w_out, b_out, gain_two, bias_two, lengths):
    queries = low(low_back(highest_dot(inputs, w_query) + b_query))
    key_rows = low(low_back(highest_dot(inputs, w_key)))
    value_rows = low(low_back(highest_dot(inputs, w_value) + b_value))
    shape_seq = (SEQS, SEQ_LEN, D)
    context = lax.map(jax.checkpoint(attend_sentence), (queries.reshape(shape_seq), key_rows.reshape(shape_seq), value_rows.reshape(shape_seq), lengths))
    context = low(low_back(context.reshape(TOKENS, D)))
    attn_out = low_back(highest_dot(context, w_attn_out)) + b_attn_out
    hidden = layer_norm(inputs + attn_out, gain_one, bias_one)
    inner_pre = low_back(highest_dot(low(hidden), w_in) + b_in)
    activated = low(jax.nn.gelu(inner_pre, approximate=False))
    ffn_out = low_back(highest_dot(activated, w_out)) + b_out
    return layer_norm(hidden + ffn_out, gain_two, bias_two)

def pool_depths(layer_values, lengths):
    sentence_rows = layer_values.reshape(SEQS, SEQ_LEN, D)
    allowed = jnp.arange(SEQ_LEN, dtype=jnp.int32)[None, :] < lengths[:, None]
    totals = lax.optimization_barrier(jnp.sum(jnp.where(allowed[:, :, None], sentence_rows, 0.0), axis=1))
    average = totals / lengths[:, None].astype(jnp.float32)
    pieces = []
    for cut_width in (D, D * 2 // 3, D // 3, D // 6, D // 12):
        prefix = average[:, :cut_width]
        centred = prefix - lax.optimization_barrier(jnp.mean(prefix, axis=-1, keepdims=True))
        pieces.append(centred * lax.rsqrt(lax.optimization_barrier(jnp.mean(centred * centred, axis=-1, keepdims=True)) + EPSILON))
    return jnp.concatenate(pieces, axis=1)

def reference(tokens, w_query, b_query, w_key, w_value, b_value, w_attn_out, b_attn_out, gain_one, bias_one, w_in, b_in, w_out, b_out, gain_two, bias_two, lengths, grad_out):

    def run_layer(inputs, wq_arg, bq_arg, wk_arg, wv_arg, bv_arg, wo_arg, bo_arg, gone_arg, bone_arg, win_arg, bin_arg, wout_arg, bout_arg, gtwo_arg, btwo_arg):
        return forward(inputs, wq_arg, bq_arg, wk_arg, wv_arg, bv_arg, wo_arg, bo_arg, gone_arg, bone_arg, win_arg, bin_arg, wout_arg, bout_arg, gtwo_arg, btwo_arg, lengths)
    result, pullback = jax.vjp(run_layer, tokens.astype(jnp.float32), w_query.astype(jnp.float32), b_query.astype(jnp.float32), w_key.astype(jnp.float32), w_value.astype(jnp.float32), b_value.astype(jnp.float32), w_attn_out.astype(jnp.float32), b_attn_out.astype(jnp.float32), gain_one.astype(jnp.float32), bias_one.astype(jnp.float32), w_in.astype(jnp.float32), b_in.astype(jnp.float32), w_out.astype(jnp.float32), b_out.astype(jnp.float32), gain_two.astype(jnp.float32), bias_two.astype(jnp.float32))
    gradients = pullback(grad_out.astype(jnp.float32))
    layer_out = result.astype(jnp.bfloat16)
    pooled = pool_depths(layer_out.astype(jnp.float32), lengths)
    return (layer_out, pooled, gradients[0].astype(jnp.bfloat16), gradients[1], gradients[2], gradients[3], gradients[4], gradients[5], gradients[6], gradients[7], gradients[8], gradients[9], gradients[10], gradients[11], gradients[12], gradients[13], gradients[14], gradients[15])
```

```python
import math

import jax
import jax.numpy as jnp
from jax import lax
from jax.experimental import pallas as pl
from jax.experimental.pallas import tpu as pltpu
from jax.sharding import PartitionSpec as P

HEAD = 64
SEQ_LEN = 512
HALF = SEQ_LEN // 2
EPSILON = 1e-06
BLOCK = 32
F32 = jnp.float32
BF16 = jnp.bfloat16
MESH = pl.DeviceIdType.MESH

NN = (((1,), (0,)), ((), ()))
NT = (((1,), (1,)), ((), ()))
TN = (((0,), (0,)), ((), ()))

ATTN, FFN, HID = 0, 1, 2
G_HID, G_FFN, G_RES, G_ATTN = 0, 1, 2, 3


def mm(left, right, dims):
    return lax.dot_general(left, right, dims, preferred_element_type=F32)


def fold8(block):
    rows, width = block.shape
    return jnp.sum(block.reshape(rows // 8, 8, width), axis=0)


def row_mean(block):
    return jnp.mean(block, axis=-1, keepdims=True)


def layer_kernel(
    batch_size,
    len_ref,
    tok_hbm,
    wq_hbm,
    wk_hbm,
    wv_hbm,
    wo_hbm,
    win_hbm,
    wout_hbm,
    gout_hbm,
    bq_ref,
    bv_ref,
    bin_ref,
    battn_ref,
    gain1_ref,
    bias1_ref,
    bout_ref,
    gain2_ref,
    bias2_ref,
    lay_hbm,
    pool_ref,
    gtok_ref,
    gw_hbm,
    vec_ref,
    tok_v,
    wqkv_v,
    wo_v,
    win_v,
    wout_v,
    gout_v,
    qkv_v,
    ctx_v,
    lse_v,
    hid_v,
    act_v,
    slope_v,
    norm1_v,
    inv1_v,
    res2_v,
    gffn_v,
    din_v,
    lay_v,
    gt_v,
    do_v,
    mask_v,
    big_v,
    part_v,
    cs_v,
    cr_v,
    ys_v,
    yr_v,
    tcs_v,
    tcr_v,
    tow_v,
    tys_v,
    tyr_v,
    gw_v,
    sum_v,
    xr_v,
    zr_v,
    acc_v,
    vec_v,
    vc_v,
    vx_v,
    vz_v,
    in_sem,
    cs_sem,
    cr_sem,
    ys_sem,
    yr_sem,
    as_sem,
    ar_sem,
    tcs_sem,
    tcr_sem,
    tys_sem,
    tyr_sem,
    xs_sem,
    xr_sem,
    zs_sem,
    zr_sem,
    vs_sem,
    vr_sem,
    vzs_sem,
    vzr_sem,
    out_sem,
):
    rows_all, width = tok_v.shape
    sentences = rows_all // SEQ_LEN
    qw = wo_v.shape[0]
    heads = qw // HEAD
    groups = batch_size // 2
    piece = zr_v.shape[2]
    x_half = groups * piece

    gattn_v = gffn_v

    tp = lax.axis_index("tp")
    ba = lax.axis_index("batch")
    core = lax.rem(tp, 2)
    other = 1 - core
    chip = tp // 2
    xbit = lax.rem(ba, 2)
    grp = ba // 2
    core_id = {"tp": chip * 2 + other}
    y_id = {"tp": (1 - chip) * 2 + core}
    x_id = {"batch": grp * 2 + 1 - xbit}
    z_grps = [lax.rem(grp + k, groups) for k in range(1, groups)]
    z_ids = [{"batch": g * 2 + xbit} for g in z_grps]

    def remote(src, dst, send, recv, dev):
        return pltpu.make_async_remote_copy(
            src_ref=src,
            dst_ref=dst,
            send_sem=send,
            recv_sem=recv,
            device_id=dev,
            device_id_type=MESH,
        )

    def order(i):
        return lax.rem(2 * i, sentences)

    def tok_copy(i):
        rows = pl.ds(pl.multiple_of(order(i) * SEQ_LEN, SEQ_LEN), SEQ_LEN)
        return pltpu.make_async_copy(tok_hbm.at[rows], tok_v.at[rows], in_sem.at[i])

    w_copies = [
        pltpu.make_async_copy(src, dst, in_sem.at[sentences + k])
        for k, (src, dst) in enumerate(
            [
                (wq_hbm, wqkv_v.at[pl.ds(0, qw)]),
                (wk_hbm, wqkv_v.at[pl.ds(qw, qw)]),
                (wv_hbm, wqkv_v.at[pl.ds(2 * qw, qw)]),
                (wo_hbm, wo_v),
                (win_hbm, win_v),
                (wout_hbm, wout_v),
            ]
        )
    ]

    def gout_copy(i):
        src = pl.ds(pl.multiple_of(order(i) * SEQ_LEN + core * HALF, HALF), HALF)
        dst = pl.ds(pl.multiple_of(i * HALF, HALF), HALF)
        return pltpu.make_async_copy(
            gout_hbm.at[src], gout_v.at[dst], in_sem.at[sentences + 6 + i]
        )

    for k in range(3):
        w_copies[k].start()
    for i in range(sentences):
        tok_copy(i).start()
    for k in range(3, 6):
        w_copies[k].start()
    for i in range(sentences):
        gout_copy(i).start()

    barrier = pltpu.get_barrier_semaphore()
    peers = [core_id, y_id, x_id] + z_ids
    for dev in peers:
        pl.semaphore_signal(barrier, inc=1, device_id=dev, device_id_type=MESH)
    pl.semaphore_wait(barrier, len(peers))

    acc_v[...] = jnp.zeros_like(acc_v)

    def core_copy(ph, i):
        k = ph * sentences + i
        slot = (ph % 2) * sentences + i
        return remote(cs_v.at[slot], cr_v.at[slot], cs_sem.at[k], cr_sem.at[k], core_id)

    def y_copy(ph, i):
        k = ph * sentences + i
        slot = (ph % 2) * sentences + i
        return remote(ys_v.at[slot], yr_v.at[slot], ys_sem.at[k], yr_sem.at[k], y_id)

    def gather_copy(which, ref, i):
        k = which * sentences + i
        rows = pl.ds(pl.multiple_of(order(i) * SEQ_LEN + core * HALF, HALF), HALF)
        return remote(ref.at[rows], ref.at[rows], as_sem.at[k], ar_sem.at[k], core_id)

    def chip_sum(ph, i):
        slot = (ph % 2) * sentences + i
        core_copy(ph, i).wait_recv()

        @pl.loop(0, HALF // BLOCK)
        def _(j):
            rows = pl.ds(pl.multiple_of(j * BLOCK, BLOCK), BLOCK)
            ys_v[slot, rows, :] = (part_v[rows, :] + cr_v[slot, rows, :].astype(F32)).astype(BF16)

        y_copy(ph, i).start()

    def total_rows(ph, i, rows):
        slot = (ph % 2) * sentences + i
        return ys_v[slot, rows, :].astype(F32) + yr_v[slot, rows, :].astype(F32)

    def add_acc(k, value):
        rows = pl.ds(8 * k, 8)
        acc_v[rows, :] = acc_v[rows, :] + fold8(value)

    def fill_mask(s):
        limit = len_ref[s]
        key = lax.broadcasted_iota(jnp.int32, mask_v.shape, 0)
        mask_v[...] = jnp.where(key < limit, 0.0, -1e30)

    def masked_scores(k_t, q_t):
        mask = mask_v[...]
        return mm(k_t, q_t, TN) + jnp.concatenate([mask, mask], axis=1)

    def column(row_ref):
        return jnp.transpose(jnp.broadcast_to(row_ref[...], (8, row_ref.shape[1])))[:, :1]

    for k in range(3):
        w_copies[k].wait()

    @pl.loop(0, sentences)
    def _(i):
        s = order(i)
        r0 = pl.multiple_of(s * SEQ_LEN, SEQ_LEN)
        cols = pl.ds(r0, SEQ_LEN)
        tok_copy(i).wait()
        x = tok_v[cols, :]
        qkv_v[pl.ds(0, qw), cols] = (
            mm(wqkv_v[pl.ds(0, qw), :], x, NT) + column(bq_ref)
        ).astype(BF16) * jnp.asarray(HEAD ** (-0.5), BF16)
        qkv_v[pl.ds(qw, qw), cols] = mm(wqkv_v[pl.ds(qw, qw), :], x, NT).astype(BF16)
        qkv_v[pl.ds(2 * qw, qw), cols] = (
            mm(wqkv_v[pl.ds(2 * qw, qw), :], x, NT) + column(bv_ref)
        ).astype(BF16)
        fill_mask(s)
        for h in range(heads):
            k_t = qkv_v[pl.ds(qw + h * HEAD, HEAD), cols]
            v_t = qkv_v[pl.ds(2 * qw + h * HEAD, HEAD), cols]
            for qb in range(2):
                qcols = pl.ds(pl.multiple_of(r0 + qb * HALF, HALF), HALF)
                scores = masked_scores(k_t, qkv_v[pl.ds(h * HEAD, HEAD), qcols])
                top = jnp.max(scores, axis=0, keepdims=True)
                expo = jnp.exp(scores - top)
                total = jnp.sum(expo, axis=0, keepdims=True)
                shares = (expo * (1.0 / total)).astype(BF16)
                ctx_v[pl.ds(h * HEAD, HEAD), qcols] = mm(v_t, shares, NN).astype(BF16)
                lse_v[pl.ds(h, 1), qcols] = top + jnp.log(total)

        @pl.when(i == 0)
        def _():
            w_copies[3].wait()

        oc = pl.ds(pl.multiple_of(r0 + other * HALF, HALF), HALF)
        wc = pl.ds(pl.multiple_of(r0 + core * HALF, HALF), HALF)
        cs_v[i] = mm(ctx_v[:, oc], wo_v[...], TN).astype(BF16)
        core_copy(ATTN, i).start()
        part_v[...] = mm(ctx_v[:, wc], wo_v[...], TN)
        chip_sum(ATTN, i)

    w_copies[4].wait()
    w_copies[5].wait()

    @pl.loop(0, sentences)
    def _(i):
        r0 = pl.multiple_of(order(i) * SEQ_LEN, SEQ_LEN)
        own0 = pl.multiple_of(r0 + core * HALF, HALF)
        oth0 = pl.multiple_of(r0 + other * HALF, HALF)
        y_copy(ATTN, i).wait_recv()

        @pl.loop(0, HALF // BLOCK)
        def _(j):
            rows = pl.ds(pl.multiple_of(j * BLOCK, BLOCK), BLOCK)
            full = pl.ds(pl.multiple_of(own0 + j * BLOCK, BLOCK), BLOCK)
            kept = pl.ds(pl.multiple_of(i * HALF + j * BLOCK, BLOCK), BLOCK)
            resid = tok_v[full, :].astype(F32) + (total_rows(ATTN, i, rows) + battn_ref[...])
            centred = resid - row_mean(resid)
            inv = lax.rsqrt(row_mean(centred * centred) + EPSILON)
            normed = centred * inv
            norm1_v[kept, :] = normed
            inv1_v[kept, :] = jnp.broadcast_to(inv, (BLOCK, 128))
            hid_v[full, :] = (normed * gain1_ref[...] + bias1_ref[...]).astype(BF16)

        gather_copy(G_HID, hid_v, i).start()

        def feed(base):
            big_v[...] = mm(hid_v[pl.ds(base, HALF), :], win_v[...], NN)

            @pl.loop(0, HALF // BLOCK)
            def _(j):
                rows = pl.ds(pl.multiple_of(j * BLOCK, BLOCK), BLOCK)
                full = pl.ds(pl.multiple_of(base + j * BLOCK, BLOCK), BLOCK)
                pre = big_v[rows, :] + bin_ref[...]
                cdf = 0.5 * (1.0 + lax.erf(pre * 0.5**0.5))
                act_v[full, :] = (pre * cdf).astype(BF16)
                slope_v[full, :] = (
                    cdf + pre * (jnp.exp(-0.5 * pre * pre) * (2.0 * math.pi) ** (-0.5))
                ).astype(slope_v.dtype)

            return mm(act_v[pl.ds(base, HALF), :], wout_v[...], NN)

        part_v[...] = feed(own0)
        gather_copy(G_HID, hid_v, i).wait_recv()
        slot = sentences + i
        cs_v[slot] = feed(oth0).astype(BF16)
        core_copy(FFN, i).start()
        chip_sum(FFN, i)

    def weight_grad(j, left_v, right_v):
        for t in range(width // 256):
            block = mm(left_v[:, pl.ds(t * 256, 256)], right_v[...], TN)
            gw_v[j, pl.ds(t * 256, 256), :] = block.astype(BF16)

    def xrs_copy(j):
        return remote(
            gw_v.at[j, pl.ds(pl.multiple_of((1 - xbit) * x_half, 16), x_half)],
            xr_v.at[j],
            xs_sem.at[j],
            xr_sem.at[j],
            x_id,
        )

    @pl.loop(0, sentences)
    def _(i):
        r0 = pl.multiple_of(order(i) * SEQ_LEN, SEQ_LEN)
        own0 = pl.multiple_of(r0 + core * HALF, HALF)
        oth0 = pl.multiple_of(r0 + other * HALF, HALF)
        gout_copy(i).wait()
        y_copy(FFN, i).wait_recv()

        @pl.loop(0, HALF // BLOCK)
        def _(j):
            rows = pl.ds(pl.multiple_of(j * BLOCK, BLOCK), BLOCK)
            full = pl.ds(pl.multiple_of(own0 + j * BLOCK, BLOCK), BLOCK)
            kept = pl.ds(pl.multiple_of(i * HALF + j * BLOCK, BLOCK), BLOCK)
            hidden = norm1_v[kept, :] * gain1_ref[...] + bias1_ref[...]
            resid = hidden + (total_rows(FFN, i, rows) + bout_ref[...])
            centred = resid - row_mean(resid)
            inv = lax.rsqrt(row_mean(centred * centred) + EPSILON)
            normed = centred * inv
            lay_v[full, :] = (normed * gain2_ref[...] + bias2_ref[...]).astype(BF16)
            up = gout_v[kept, :].astype(F32)
            scaled = up * gain2_ref[...]
            grad = inv * (scaled - row_mean(scaled) - normed * row_mean(scaled * normed))
            res2_v[kept, :] = grad
            gffn_v[full, :] = grad.astype(BF16)
            add_acc(4, grad)
            add_acc(5, up * normed)
            add_acc(6, up)

        gather_copy(G_FFN, gffn_v, i).start()
        gather_copy(G_RES, lay_v, i).start()

        def back(base):
            big_v[...] = mm(gffn_v[pl.ds(base, HALF), :], wout_v[...], NT)

            @pl.loop(0, HALF // BLOCK)
            def _(j):
                rows = pl.ds(pl.multiple_of(j * BLOCK, BLOCK), BLOCK)
                full = pl.ds(pl.multiple_of(base + j * BLOCK, BLOCK), BLOCK)
                inner = (big_v[rows, :] * slope_v[full, :].astype(F32)).astype(BF16)
                din_v[full, :] = inner
                add_acc(0, inner.astype(F32))

            return mm(din_v[pl.ds(base, HALF), :], win_v[...], NT)

        part_v[...] = back(own0)
        gather_copy(G_FFN, gffn_v, i).wait_recv()

        @pl.when(i == sentences - 1)
        def _():
            weight_grad(0, act_v, gffn_v)
            xrs_copy(0).start()

        core_copy(ATTN, i).wait_send()
        cs_v[i] = back(oth0).astype(BF16)
        core_copy(HID, i).start()
        y_copy(ATTN, i).wait_send()
        chip_sum(HID, i)

    weight_grad(1, hid_v, din_v)
    xrs_copy(1).start()

    own_x = pl.multiple_of(xbit * x_half, 16)

    def zrs_copy(j, k):
        src = pl.ds(pl.multiple_of(own_x + z_grps[k] * piece, 16), piece)
        return remote(
            gw_v.at[j, src], zr_v.at[j, grp], zs_sem.at[j, 0, k], zr_sem.at[j, 0, grp], z_ids[k]
        )

    def zrs_wait(j, k):
        src = pl.ds(pl.multiple_of(own_x + z_grps[k] * piece, 16), piece)
        g = z_grps[k]
        remote(
            gw_v.at[j, src], zr_v.at[j, g], zs_sem.at[j, 0, k], zr_sem.at[j, 0, g], z_ids[k]
        ).wait_recv()

    def zag_copy(j, k):
        at = pl.ds(pl.multiple_of(own_x + grp * piece, 16), piece)
        return remote(
            sum_v.at[j, at],
            sum_v.at[j, at],
            zs_sem.at[j, 1, k],
            zr_sem.at[j, 1, grp],
            z_ids[k],
        )

    def zag_wait(j, k):
        g = z_grps[k]
        at = pl.ds(pl.multiple_of(own_x + g * piece, 16), piece)
        remote(
            sum_v.at[j, at], sum_v.at[j, at], zs_sem.at[j, 1, k], zr_sem.at[j, 1, g], z_ids[k]
        ).wait_recv()

    def xag_copy(j):
        at = pl.ds(own_x, x_half)
        return remote(sum_v.at[j, at], sum_v.at[j, at], xs_sem.at[3 + j], xr_sem.at[3 + j], x_id)

    def xag_wait(j):
        at = pl.ds(pl.multiple_of((1 - xbit) * x_half, 16), x_half)
        remote(
            sum_v.at[j, at], sum_v.at[j, at], xs_sem.at[3 + j], xr_sem.at[3 + j], x_id
        ).wait_recv()

    def sum_step1(j):
        xrs_copy(j).wait_recv()
        for t in range(groups):
            at = pl.ds(pl.multiple_of(own_x + t * piece, 16), piece)
            got = xr_v[j, pl.ds(t * piece, piece), :]
            gw_v[j, at, :] = (gw_v[j, at, :].astype(F32) + got.astype(F32)).astype(BF16)
        for k in range(groups - 1):
            zrs_copy(j, k).start()

    def sum_step2(j):
        at = pl.ds(pl.multiple_of(own_x + grp * piece, 16), piece)
        total = gw_v[j, at, :].astype(F32)
        for k in range(groups - 1):
            zrs_wait(j, k)
            total = total + zr_v[j, z_grps[k]].astype(F32)
        sum_v[j, at, :] = total.astype(BF16)
        for k in range(groups - 1):
            zag_copy(j, k).start()

    def sum_step3(j):
        for k in range(groups - 1):
            zag_wait(j, k)
        xag_copy(j).start()

    @pl.loop(0, sentences)
    def _(i):
        s = order(i)
        r0 = pl.multiple_of(s * SEQ_LEN, SEQ_LEN)
        cols = pl.ds(r0, SEQ_LEN)
        own0 = pl.multiple_of(r0 + core * HALF, HALF)
        y_copy(HID, i).wait_recv()
        gather_copy(G_FFN, gffn_v, i).wait_send()

        @pl.loop(0, HALF // BLOCK)
        def _(j):
            rows = pl.ds(pl.multiple_of(j * BLOCK, BLOCK), BLOCK)
            full = pl.ds(pl.multiple_of(own0 + j * BLOCK, BLOCK), BLOCK)
            kept = pl.ds(pl.multiple_of(i * HALF + j * BLOCK, BLOCK), BLOCK)
            grad_hidden = res2_v[kept, :] + total_rows(HID, i, rows)
            normed = norm1_v[kept, :]
            inv = inv1_v[kept, :][:, :1]
            scaled = grad_hidden * gain1_ref[...]
            grad = inv * (scaled - row_mean(scaled) - normed * row_mean(scaled * normed))
            gattn_v[full, :] = grad.astype(BF16)
            add_acc(1, grad)
            add_acc(2, grad_hidden * normed)
            add_acc(3, grad_hidden)

        gather_copy(G_ATTN, gattn_v, i).start()
        fill_mask(s)
        gather_copy(G_ATTN, gattn_v, i).wait_recv()
        do_v[...] = mm(wo_v[...], gattn_v[cols, :], NT).astype(BF16)
        for h in range(heads):
            k_t = qkv_v[pl.ds(qw + h * HEAD, HEAD), cols]
            v_t = qkv_v[pl.ds(2 * qw + h * HEAD, HEAD), cols]
            grad_k = None
            grad_v = None
            for qb in range(2):
                qcols = pl.ds(pl.multiple_of(r0 + qb * HALF, HALF), HALF)
                q_t = qkv_v[pl.ds(h * HEAD, HEAD), qcols]
                d_t = do_v[pl.ds(h * HEAD, HEAD), pl.ds(qb * HALF, HALF)]
                c_t = ctx_v[pl.ds(h * HEAD, HEAD), qcols]
                delta = jnp.sum(d_t.astype(F32) * c_t.astype(F32), axis=0, keepdims=True)
                shares = jnp.exp(masked_scores(k_t, q_t) - lse_v[pl.ds(h, 1), qcols])
                grad_shares = mm(v_t, d_t, TN)
                grad_scores = (shares * (grad_shares - delta)).astype(BF16)
                gt_v[pl.ds(h * HEAD, HEAD), qcols] = (
                    mm(k_t, grad_scores, NN) * HEAD ** (-0.5)
                ).astype(BF16)
                new_k = mm(q_t, grad_scores, NT)
                new_v = mm(d_t, shares.astype(BF16), NT)
                grad_k = new_k if grad_k is None else grad_k + new_k
                grad_v = new_v if grad_v is None else grad_v + new_v
            gt_v[pl.ds(qw + h * HEAD, HEAD), cols] = grad_k.astype(BF16)
            gt_v[pl.ds(2 * qw + h * HEAD, HEAD), cols] = grad_v.astype(BF16)

        @pl.loop(0, SEQ_LEN // 128)
        def _(j):
            blk = s * (SEQ_LEN // 128) + j
            quarter = blk // 3
            place = lax.rem(blk, 3)
            slot = (quarter // 2) * 3 + place
            bcols = pl.ds(pl.multiple_of(r0 + j * 128, 128), 128)
            part = mm(gt_v[:, bcols], wqkv_v[...], TN).astype(BF16)

            @pl.when(lax.rem(quarter, 2) == core)
            def _():
                tow_v[slot] = part

            @pl.when(lax.rem(quarter, 2) == other)
            def _():
                tcs_v[slot] = part
                remote(
                    tcs_v.at[slot],
                    tcr_v.at[slot],
                    tcs_sem.at[slot],
                    tcr_sem.at[slot],
                    core_id,
                ).start()

        @pl.when(i == 0)
        def _():
            sum_step1(0)

        @pl.when(i == 1)
        def _():
            sum_step1(1)
            sum_step2(0)

    gw_v[2, pl.ds(0, 3 * qw), :] = mm(gt_v[...], tok_v[...], NN).astype(BF16)
    gw_v[2, pl.ds(3 * qw, qw), :] = mm(ctx_v[...], gattn_v[...], NN).astype(BF16)
    xrs_copy(2).start()

    ones = jnp.ones((8, rows_all), BF16)
    vec_v[...] = jnp.zeros_like(vec_v)
    vec_v[pl.ds(0, 1), pl.ds(0, qw)] = mm(ones, gt_v[pl.ds(0, qw), :], NT)[:1]
    vec_v[pl.ds(0, 1), pl.ds(256, qw)] = mm(ones, gt_v[pl.ds(2 * qw, qw), :], NT)[:1]
    for k in range(7):
        vec_v[pl.ds(1 + k, 1), :] = jnp.sum(acc_v[pl.ds(8 * k, 8), :], axis=0, keepdims=True)
    v_core = remote(vec_v, vc_v, vs_sem.at[0], vr_sem.at[0], core_id)
    v_core.start()

    def t_core(slot):
        return remote(
            tcs_v.at[slot], tcr_v.at[slot], tcs_sem.at[slot], tcr_sem.at[slot], core_id
        )

    def t_y(k):
        return remote(tys_v.at[k], tyr_v.at[k], tys_sem.at[k], tyr_sem.at[k], y_id)

    for k in range(3):
        slot = (1 - chip) * 3 + k
        t_core(slot).wait_recv()
        tys_v[k] = (tow_v[slot].astype(F32) + tcr_v[slot].astype(F32)).astype(BF16)
        t_y(k).start()

    v_core.wait()
    row_id = lax.broadcasted_iota(jnp.int32, vec_v.shape, 0)
    vx_v[0] = vec_v[...] + jnp.where(row_id >= 2, vc_v[...], 0.0)
    v_x = remote(vx_v.at[0], vx_v.at[1], vs_sem.at[1], vr_sem.at[1], x_id)
    v_x.start()

    sum_step3(0)
    v_x.wait()
    vz_v[grp] = vx_v[0] + vx_v[1]

    def vz_copy(k):
        return remote(vz_v.at[grp], vz_v.at[grp], vzs_sem.at[k], vzr_sem.at[grp], z_ids[k])

    def vz_wait(k):
        g = z_grps[k]
        remote(vz_v.at[g], vz_v.at[g], vzs_sem.at[k], vzr_sem.at[g], z_ids[k]).wait_recv()

    for k in range(groups - 1):
        vz_copy(k).start()

    for i in range(sentences):
        gather_copy(G_RES, lay_v, i).wait_recv()
    quarter_rows = rows_all // 4
    lay_out = pltpu.make_async_copy(
        lay_v.at[pl.ds(pl.multiple_of(tp * quarter_rows, quarter_rows), quarter_rows)],
        lay_hbm,
        out_sem.at[0],
    )
    lay_out.start()
    for s in range(sentences):
        key = lax.broadcasted_iota(jnp.int32, (8, SEQ_LEN), 1)
        member = jnp.where(key < len_ref[s], 1.0, 0.0).astype(BF16)
        total = mm(member, lay_v[pl.ds(s * SEQ_LEN, SEQ_LEN), :], NN)[:1]
        average = total / len_ref[s].astype(F32)
        at = 0
        for cut in (width, width * 2 // 3, width // 3, width // 6, width // 12):
            prefix = average[:, :cut]
            centred = prefix - row_mean(prefix)
            pool_ref[pl.ds(s, 1), pl.ds(at, cut)] = centred * lax.rsqrt(
                row_mean(centred * centred) + EPSILON
            )
            at += cut

    for k in range(3):
        slot = chip * 3 + k
        t_core(slot).wait_recv()
        mine = (tow_v[slot].astype(F32) + tcr_v[slot].astype(F32)).astype(BF16)
        t_y(k).wait_recv()
        at = pl.ds(pl.multiple_of(tp * quarter_rows + k * 128, 128), 128)
        gtok_ref[pl.ds(k * 128, 128), :] = (
            gattn_v[at, :].astype(F32) + (mine.astype(F32) + tyr_v[k].astype(F32))
        ).astype(BF16)

    sum_step2(1)
    sum_step1(2)
    sum_step3(1)
    sum_step2(2)

    for k in range(groups - 1):
        vz_wait(k)
    total = vz_v[0]
    for g in range(1, groups):
        total = total + vz_v[g]
    vec_ref[...] = total

    def out_copy(j):
        return pltpu.make_async_copy(sum_v.at[j], gw_hbm.at[j], out_sem.at[1 + j])

    xag_wait(0)
    out_copy(0).start()
    sum_step3(2)
    for j in (1, 2):
        xag_wait(j)
        out_copy(j).start()

    for j in range(3):
        out_copy(j).wait()
    lay_out.wait()
    for i in range(sentences):
        core_copy(FFN, i).wait_send()
        y_copy(FFN, i).wait_send()
        core_copy(HID, i).wait_send()
        y_copy(HID, i).wait_send()
        gather_copy(G_HID, hid_v, i).wait_send()
        gather_copy(G_RES, lay_v, i).wait_send()
        gather_copy(G_ATTN, gattn_v, i).wait_send()
    for slot in range(6):
        t_core(slot).wait_send()
    for k in range(3):
        t_y(k).wait_send()
    for j in range(3):
        xrs_copy(j).wait_send()
        xag_copy(j).wait_send()
        for k in range(groups - 1):
            zrs_copy(j, k).wait_send()
            zag_copy(j, k).wait_send()
    for k in range(groups - 1):
        vz_copy(k).wait_send()


def layer_call(batch_size, tp_size, args):
    (
        tokens,
        w_query,
        b_query,
        w_key,
        w_value,
        b_value,
        w_attn_out,
        b_attn_out,
        gain_one,
        bias_one,
        w_in,
        b_in,
        w_out,
        b_out,
        gain_two,
        bias_two,
        lengths,
        grad_out,
    ) = args
    rows, width = tokens.shape
    sentences = lengths.shape[0]
    qw = w_attn_out.shape[0]
    units = w_in.shape[1]
    groups = batch_size // 2
    piece = -(-width // batch_size)
    piece = -(-piece // 16) * 16
    padded = piece * batch_size
    quarter = rows // tp_size
    row = lambda v: v.reshape(1, v.shape[0])
    anyspec = pl.BlockSpec(memory_space=pl.ANY)
    vmem = pl.BlockSpec(memory_space=pltpu.VMEM)
    smem = pl.BlockSpec(memory_space=pltpu.SMEM)
    dma = pltpu.SemaphoreType.DMA
    V = pltpu.VMEM
    kept = rows // 2
    return pl.pallas_call(
        lambda *refs: layer_kernel(batch_size, *refs),
        out_shape=(
            jax.ShapeDtypeStruct((quarter, width), BF16),
            jax.ShapeDtypeStruct((sentences, width * 9 // 4), F32),
            jax.ShapeDtypeStruct((quarter, width), BF16),
            jax.ShapeDtypeStruct((3, padded, width), BF16),
            jax.ShapeDtypeStruct((8, width), F32),
        ),
        in_specs=[smem] + [anyspec] * 8 + [vmem] * 9,
        out_specs=(anyspec, vmem, vmem, anyspec, vmem),
        scratch_shapes=[
            V((rows, width), BF16),
            V((3 * qw, width), BF16),
            V((qw, width), BF16),
            V((width, units), BF16),
            V((units, width), BF16),
            V((kept, width), BF16),
            V((3 * qw, rows), BF16),
            V((qw, rows), BF16),
            V((8, rows), F32),
            V((rows, width), BF16),
            V((rows, units), BF16),
            V((rows, units), BF16),
            V((kept, width), F32),
            V((kept, 128), F32),
            V((kept, width), F32),
            V((rows, width), BF16),
            V((rows, units), BF16),
            V((rows, width), BF16),
            V((3 * qw, rows), BF16),
            V((qw, SEQ_LEN), BF16),
            V((SEQ_LEN, 128), F32),
            V((HALF, units), F32),
            V((HALF, width), F32),
            V((2 * sentences, HALF, width), BF16),
            V((2 * sentences, HALF, width), BF16),
            V((2 * sentences, HALF, width), BF16),
            V((2 * sentences, HALF, width), BF16),
            V((6, 128, width), BF16),
            V((6, 128, width), BF16),
            V((6, 128, width), BF16),
            V((3, 128, width), BF16),
            V((3, 128, width), BF16),
            V((3, padded, width), BF16),
            V((3, padded, width), BF16),
            V((3, padded // 2, width), BF16),
            V((3, groups, piece, width), BF16),
            V((64, width), F32),
            V((8, width), F32),
            V((8, width), F32),
            V((2, 8, width), F32),
            V((groups, 8, width), F32),
            dma((2 * sentences + 6,)),
            dma((3 * sentences,)),
            dma((3 * sentences,)),
            dma((3 * sentences,)),
            dma((3 * sentences,)),
            dma((4 * sentences,)),
            dma((4 * sentences,)),
            dma((6,)),
            dma((6,)),
            dma((3,)),
            dma((3,)),
            dma((6,)),
            dma((6,)),
            dma((3, 2, groups)),
            dma((3, 2, groups)),
            dma((2,)),
            dma((2,)),
            dma((groups,)),
            dma((groups,)),
            dma((4,)),
        ],
        compiler_params=pltpu.CompilerParams(
            collective_id=0, has_side_effects=True, vmem_limit_bytes=63 << 20
        ),
    )(
        lengths,
        tokens,
        w_query.T,
        w_key.T,
        w_value.T,
        w_attn_out,
        w_in,
        w_out,
        grad_out,
        row(b_query),
        row(b_value),
        row(b_in),
        row(b_attn_out),
        row(gain_one),
        row(bias_one),
        row(b_out),
        row(gain_two),
        row(bias_two),
    )


def shards(*args):
    batch_size = lax.axis_size("batch")
    tp_size = lax.axis_size("tp")
    lay, pooled, gtok, gw, vec = layer_call(batch_size, tp_size, args)
    qw = args[6].shape[0]
    width = args[0].shape[1]
    attn = gw[2].astype(F32)
    return (
        lay,
        pooled,
        gtok,
        attn[:qw].T,
        vec[0, :qw],
        attn[qw : 2 * qw].T,
        attn[2 * qw : 3 * qw].T,
        vec[0, 256 : 256 + qw],
        attn[3 * qw : 4 * qw],
        vec[2],
        vec[3],
        vec[4],
        gw[1, :width].astype(F32),
        vec[1],
        gw[0, :width].astype(F32),
        vec[5],
        vec[6],
        vec[7],
    )


def solution(mesh):
    placed = (
        P("batch", None),
        P(None, "tp"),
        P("tp"),
        P(None, "tp"),
        P(None, "tp"),
        P("tp"),
        P("tp", None),
        P(),
        P(),
        P(),
        P(None, "tp"),
        P("tp"),
        P("tp", None),
        P(),
        P(),
        P(),
        P("batch"),
        P("batch", None),
    )
    return jax.shard_map(
        shards,
        mesh=mesh,
        in_specs=placed,
        out_specs=(
            P(("batch", "tp"), None),
            P("batch", None),
            P(("batch", "tp"), None),
            P(None, "tp"),
            P("tp"),
            P(None, "tp"),
            P(None, "tp"),
            P("tp"),
            P("tp", None),
            P(),
            P(),
            P(),
            P(None, "tp"),
            P("tp"),
            P("tp", None),
            P(),
            P(),
            P(),
        ),
        check_vma=False,
    )
```

```python
import math

import jax
import jax.numpy as jnp
from jax import lax
from jax.experimental import pallas as pl
from jax.experimental.pallas import tpu as pltpu
from jax.sharding import PartitionSpec as P

HEAD = 64
SEQ_LEN = 512
HALF = SEQ_LEN // 2
EPSILON = 1e-06
BLOCK = 32
F32 = jnp.float32
BF16 = jnp.bfloat16
MESH = pl.DeviceIdType.MESH

NN = (((1,), (0,)), ((), ()))
NT = (((1,), (1,)), ((), ()))
TN = (((0,), (0,)), ((), ()))

ATTN, FFN, HID = 0, 1, 2
G_HID, G_FFN, G_RES, G_ATTN = 0, 1, 2, 3


def mm(left, right, dims):
    return lax.dot_general(left, right, dims, preferred_element_type=F32)


def fold8(block):
    rows, width = block.shape
    return jnp.sum(block.reshape(rows // 8, 8, width), axis=0)


def row_mean(block):
    return jnp.mean(block, axis=-1, keepdims=True)


def layer_kernel(
    batch_size,
    units,
    len_ref,
    tok_hbm,
    wq_hbm,
    wk_hbm,
    wv_hbm,
    wo_hbm,
    win_hbm,
    wout_hbm,
    gout_hbm,
    bq_ref,
    bv_ref,
    bin_ref,
    battn_ref,
    gain1_ref,
    bias1_ref,
    bout_ref,
    gain2_ref,
    bias2_ref,
    lay_hbm,
    pool_ref,
    gtok_ref,
    gw_hbm,
    vec_ref,
    tok_v,
    wqkv_v,
    wo_v,
    win_v,
    wout_v,
    gout_v,
    qkv_v,
    ctx_v,
    lse_v,
    hid_v,
    act_v,
    slope_v,
    norm1_v,
    inv1_v,
    res2_v,
    gffn_v,
    lay_v,
    gt_v,
    do_v,
    mask_v,
    big_v,
    part_v,
    cs_v,
    cr_v,
    ys_v,
    yr_v,
    tcs_v,
    tcr_v,
    tow_v,
    tys_v,
    tyr_v,
    gw_v,
    sum_v,
    xr_v,
    pr_v,
    qr_v,
    wacc_v,
    par_v,
    acc_v,
    vec_v,
    vc_v,
    vx_v,
    vq_v,
    in_sem,
    cs_sem,
    cr_sem,
    ys_sem,
    yr_sem,
    as_sem,
    ar_sem,
    tcs_sem,
    tcr_sem,
    tys_sem,
    tyr_sem,
    xs_sem,
    xr_sem,
    ps_sem,
    pr_sem,
    qs_sem,
    qr_sem,
    vs_sem,
    vr_sem,
    vqs_sem,
    vqr_sem,
    out_sem,
):
    rows_all, width = tok_v.shape
    sentences = rows_all // SEQ_LEN
    qw = wo_v.shape[0]
    heads = qw // HEAD
    quads = batch_size // 4
    padded = gw_v.shape[1]
    piece = padded // batch_size
    half_rows, quad_rows = padded // 2, padded // 4
    subs = units // 3
    unit_rows = width // subs

    gattn_v = gffn_v
    din_v = slope_v

    tp = lax.axis_index("tp")
    ba = lax.axis_index("batch")
    core = lax.rem(tp, 2)
    other = 1 - core
    chip = tp // 2
    xbit = lax.rem(ba, 2)
    pbit = lax.rem(ba // 2, 2)
    quad = ba // 4
    core_id = {"tp": chip * 2 + other}
    y_id = {"tp": (1 - chip) * 2 + core}
    x_id = {"batch": ba + 1 - 2 * xbit}
    p_id = {"batch": ba + 2 - 4 * pbit}
    q_at = [lax.rem(quad + k, quads) for k in range(1, quads)]
    q_ids = [{"batch": q * 4 + lax.rem(ba, 4)} for q in q_at]

    def remote(src, dst, send, recv, dev):
        return pltpu.make_async_remote_copy(
            src_ref=src,
            dst_ref=dst,
            send_sem=send,
            recv_sem=recv,
            device_id=dev,
            device_id_type=MESH,
        )

    def order(i):
        return lax.rem(2 * i, sentences)

    def tok_copy(i):
        rows = pl.ds(pl.multiple_of(order(i) * SEQ_LEN, SEQ_LEN), SEQ_LEN)
        return pltpu.make_async_copy(tok_hbm.at[rows], tok_v.at[rows], in_sem.at[i])

    w_copies = [
        pltpu.make_async_copy(src, dst, in_sem.at[sentences + k])
        for k, (src, dst) in enumerate(
            [
                (wq_hbm, wqkv_v.at[pl.ds(0, qw)]),
                (wk_hbm, wqkv_v.at[pl.ds(qw, qw)]),
                (wv_hbm, wqkv_v.at[pl.ds(2 * qw, qw)]),
                (wo_hbm, wo_v),
                (win_hbm, win_v),
                (wout_hbm, wout_v),
            ]
        )
    ]

    def gout_copy(i):
        src = pl.ds(pl.multiple_of(order(i) * SEQ_LEN + core * HALF, HALF), HALF)
        dst = pl.ds(pl.multiple_of(i * HALF, HALF), HALF)
        return pltpu.make_async_copy(
            gout_hbm.at[src], gout_v.at[dst], in_sem.at[sentences + 6 + i]
        )

    for k in range(3):
        w_copies[k].start()
    for i in range(sentences):
        tok_copy(i).start()
    for k in range(3, 6):
        w_copies[k].start()
    for i in range(sentences):
        gout_copy(i).start()

    barrier = pltpu.get_barrier_semaphore()
    peers = [core_id, y_id, x_id, p_id] + q_ids
    for dev in peers:
        pl.semaphore_signal(barrier, inc=1, device_id=dev, device_id_type=MESH)

    acc_v[...] = jnp.zeros_like(acc_v)
    for k, ref in enumerate(
        (bin_ref, battn_ref, gain1_ref, bias1_ref, bout_ref, gain2_ref, bias2_ref)
    ):
        par_v[pl.ds(k, 1), :] = ref[...].reshape(1, width)
    bin_row, battn_row, gain1_row, bias1_row, bout_row, gain2_row, bias2_row = [
        par_v.at[pl.ds(k, 1)] for k in range(7)
    ]

    def core_copy(ph, i):
        k = ph * sentences + i
        slot = (ph % 2) * sentences + i
        return remote(cs_v.at[slot], cr_v.at[slot], cs_sem.at[k], cr_sem.at[k], core_id)

    def y_copy(ph, i):
        k = ph * sentences + i
        slot = (ph % 2) * sentences + i
        return remote(ys_v.at[slot], yr_v.at[slot], ys_sem.at[k], yr_sem.at[k], y_id)

    def gather_copy(which, ref, i):
        k = which * sentences + i
        rows = pl.ds(pl.multiple_of(order(i) * SEQ_LEN + core * HALF, HALF), HALF)
        return remote(ref.at[rows], ref.at[rows], as_sem.at[k], ar_sem.at[k], core_id)

    def chip_sum(ph, i):
        slot = (ph % 2) * sentences + i
        core_copy(ph, i).wait_recv()

        @pl.loop(0, HALF // BLOCK)
        def _(j):
            rows = pl.ds(pl.multiple_of(j * BLOCK, BLOCK), BLOCK)
            ys_v[slot, rows, :] = (part_v[rows, :] + cr_v[slot, rows, :].astype(F32)).astype(BF16)

        y_copy(ph, i).start()

    def total_rows(ph, i, rows):
        slot = (ph % 2) * sentences + i
        return ys_v[slot, rows, :].astype(F32) + yr_v[slot, rows, :].astype(F32)

    def add_acc(k, value):
        rows = pl.ds(8 * k, 8)
        acc_v[rows, :] = acc_v[rows, :] + fold8(value)

    def fill_mask(s):
        limit = len_ref[s]
        key = lax.broadcasted_iota(jnp.int32, mask_v.shape, 0)
        mask_v[...] = jnp.where(key < limit, 0.0, -1e30)

    def masked_scores(k_t, q_t):
        mask = mask_v[...]
        return mm(k_t, q_t, TN) + jnp.concatenate([mask, mask], axis=1)

    def column(row_ref):
        row = row_ref[...].reshape(1, qw)
        return jnp.transpose(jnp.broadcast_to(row, (8, qw)))[:, :1]

    for k in range(3):
        w_copies[k].wait()

    def attend(i):
        s = order(i)
        r0 = pl.multiple_of(s * SEQ_LEN, SEQ_LEN)
        cols = pl.ds(r0, SEQ_LEN)
        tok_copy(i).wait()
        x = tok_v[cols, :]
        qkv_v[pl.ds(0, qw), cols] = (
            mm(wqkv_v[pl.ds(0, qw), :], x, NT) + column(bq_ref)
        ).astype(BF16) * jnp.asarray(HEAD ** (-0.5), BF16)
        qkv_v[pl.ds(qw, qw), cols] = mm(wqkv_v[pl.ds(qw, qw), :], x, NT).astype(BF16)
        qkv_v[pl.ds(2 * qw, qw), cols] = (
            mm(wqkv_v[pl.ds(2 * qw, qw), :], x, NT) + column(bv_ref)
        ).astype(BF16)
        fill_mask(s)
        for h in range(heads):
            k_t = qkv_v[pl.ds(qw + h * HEAD, HEAD), cols]
            v_t = qkv_v[pl.ds(2 * qw + h * HEAD, HEAD), cols]
            for qb in range(2):
                qcols = pl.ds(pl.multiple_of(r0 + qb * HALF, HALF), HALF)
                scores = masked_scores(k_t, qkv_v[pl.ds(h * HEAD, HEAD), qcols])
                top = jnp.max(scores, axis=0, keepdims=True)
                expo = jnp.exp(scores - top)
                total = jnp.sum(expo, axis=0, keepdims=True)
                shares = (expo * (1.0 / total)).astype(BF16)
                ctx_v[pl.ds(h * HEAD, HEAD), qcols] = mm(v_t, shares, NN).astype(BF16)
                lse_v[pl.ds(h, 1), qcols] = top + jnp.log(total)

    attend(0)
    w_copies[3].wait()
    pl.semaphore_wait(barrier, len(peers))

    @pl.loop(0, sentences)
    def _(i):
        r0 = pl.multiple_of(order(i) * SEQ_LEN, SEQ_LEN)
        oc = pl.ds(pl.multiple_of(r0 + other * HALF, HALF), HALF)
        wc = pl.ds(pl.multiple_of(r0 + core * HALF, HALF), HALF)
        cs_v[i] = mm(ctx_v[:, oc], wo_v[...], TN).astype(BF16)
        core_copy(ATTN, i).start()
        part_v[...] = mm(ctx_v[:, wc], wo_v[...], TN)
        chip_sum(ATTN, i)

        @pl.when(i + 1 < sentences)
        def _():
            attend(i + 1)

    w_copies[4].wait()
    w_copies[5].wait()

    @pl.loop(0, sentences)
    def _(i):
        r0 = pl.multiple_of(order(i) * SEQ_LEN, SEQ_LEN)
        own0 = pl.multiple_of(r0 + core * HALF, HALF)
        oth0 = pl.multiple_of(r0 + other * HALF, HALF)
        y_copy(ATTN, i).wait_recv()

        @pl.loop(0, HALF // BLOCK)
        def _(j):
            rows = pl.ds(pl.multiple_of(j * BLOCK, BLOCK), BLOCK)
            full = pl.ds(pl.multiple_of(own0 + j * BLOCK, BLOCK), BLOCK)
            kept = pl.ds(pl.multiple_of(i * HALF + j * BLOCK, BLOCK), BLOCK)
            resid = tok_v[full, :].astype(F32) + (total_rows(ATTN, i, rows) + battn_row[...])
            centred = resid - row_mean(resid)
            inv = lax.rsqrt(row_mean(centred * centred) + EPSILON)
            normed = centred * inv
            norm1_v[kept, :] = normed
            inv1_v[kept, :] = jnp.broadcast_to(inv, (BLOCK, 128))
            hid_v[full, :] = (normed * gain1_row[...] + bias1_row[...]).astype(BF16)

        gather_copy(G_HID, hid_v, i).start()

        def feed(base):
            big_v[...] = mm(hid_v[pl.ds(base, HALF), :], win_v[...], NN)

            @pl.loop(0, HALF // BLOCK)
            def _(j):
                rows = pl.ds(pl.multiple_of(j * BLOCK, BLOCK), BLOCK)
                full = pl.ds(pl.multiple_of(base + j * BLOCK, BLOCK), BLOCK)
                pre = big_v[rows, :] + bin_row[...]
                cdf = 0.5 * (1.0 + lax.erf(pre * 0.5**0.5))
                act_v[full, :] = (pre * cdf).astype(BF16)
                slope_v[full, :] = (
                    cdf + pre * (jnp.exp(-0.5 * pre * pre) * (2.0 * math.pi) ** (-0.5))
                ).astype(slope_v.dtype)

            return mm(act_v[pl.ds(base, HALF), :], wout_v[...], NN)

        part_v[...] = feed(own0)
        gather_copy(G_HID, hid_v, i).wait_recv()
        slot = sentences + i
        cs_v[slot] = feed(oth0).astype(BF16)
        core_copy(FFN, i).start()
        chip_sum(FFN, i)

    def store_unit(j, t, block):
        for r in range(0, 384, min(384, unit_rows)):
            at = t * 384 + r
            gw_v[
                j * subs + at // unit_rows, pl.ds(at % unit_rows, min(384, unit_rows)), :
            ] = block[r : r + min(384, unit_rows)].astype(BF16)

    def xrs_copy(u):
        return remote(
            gw_v.at[u, pl.ds(pl.multiple_of((1 - xbit) * half_rows, 16), half_rows)],
            xr_v.at[u],
            xs_sem.at[0, u],
            xr_sem.at[0, u],
            x_id,
        )

    wacc_v[...] = jnp.zeros_like(wacc_v)

    @pl.loop(0, sentences)
    def _(i):
        r0 = pl.multiple_of(order(i) * SEQ_LEN, SEQ_LEN)
        own0 = pl.multiple_of(r0 + core * HALF, HALF)
        oth0 = pl.multiple_of(r0 + other * HALF, HALF)
        gout_copy(i).wait()
        y_copy(FFN, i).wait_recv()

        @pl.loop(0, HALF // BLOCK)
        def _(j):
            rows = pl.ds(pl.multiple_of(j * BLOCK, BLOCK), BLOCK)
            full = pl.ds(pl.multiple_of(own0 + j * BLOCK, BLOCK), BLOCK)
            kept = pl.ds(pl.multiple_of(i * HALF + j * BLOCK, BLOCK), BLOCK)
            hidden = norm1_v[kept, :] * gain1_row[...] + bias1_row[...]
            resid = hidden + (total_rows(FFN, i, rows) + bout_row[...])
            centred = resid - row_mean(resid)
            inv = lax.rsqrt(row_mean(centred * centred) + EPSILON)
            normed = centred * inv
            lay_v[full, :] = (normed * gain2_row[...] + bias2_row[...]).astype(BF16)
            up = gout_v[kept, :].astype(F32)
            scaled = up * gain2_row[...]
            grad = inv * (scaled - row_mean(scaled) - normed * row_mean(scaled * normed))
            res2_v[kept, :] = grad
            gffn_v[full, :] = grad.astype(BF16)
            add_acc(4, grad)
            add_acc(5, up * normed)
            add_acc(6, up)

        gather_copy(G_FFN, gffn_v, i).start()
        gather_copy(G_RES, lay_v, i).start()

        def back(base):
            big_v[...] = mm(gffn_v[pl.ds(base, HALF), :], wout_v[...], NT)

            @pl.loop(0, HALF // BLOCK)
            def _(j):
                rows = pl.ds(pl.multiple_of(j * BLOCK, BLOCK), BLOCK)
                full = pl.ds(pl.multiple_of(base + j * BLOCK, BLOCK), BLOCK)
                inner = (big_v[rows, :] * slope_v[full, :].astype(F32)).astype(BF16)
                din_v[full, :] = inner
                add_acc(0, inner.astype(F32))

            return mm(din_v[pl.ds(base, HALF), :], win_v[...], NT)

        part_v[...] = back(own0)
        gather_copy(G_FFN, gffn_v, i).wait_recv()

        both = pl.ds(r0, SEQ_LEN)
        for t in range(width // 384):
            at = pl.ds(t * 384, 384)
            wacc_v[at, :] = wacc_v[at, :] + mm(act_v[both, at], gffn_v[both, :], TN)

        @pl.when(i == sentences - 1)
        def _():
            for t in range(width // 384):
                store_unit(0, t, wacc_v[pl.ds(t * 384, 384), :])
            for u in range(subs):
                xrs_copy(u).start()

        core_copy(ATTN, i).wait_send()
        cs_v[i] = back(oth0).astype(BF16)
        core_copy(HID, i).start()
        y_copy(ATTN, i).wait_send()
        chip_sum(HID, i)

    for t in range(width // 384):
        store_unit(1, t, mm(hid_v[:, pl.ds(t * 384, 384)], din_v[...], TN))
    for u in range(subs, 2 * subs):
        xrs_copy(u).start()

    own1 = pl.multiple_of(xbit * half_rows, 16)
    own2 = pl.multiple_of(own1 + pbit * quad_rows, 16)
    give2 = pl.multiple_of(own1 + (1 - pbit) * quad_rows, 16)
    own3 = pl.multiple_of(own2 + quad * piece, 16)

    def at_quad(q):
        return pl.ds(pl.multiple_of(own2 + q * piece, 16), piece)

    def prs_copy(u):
        return remote(
            gw_v.at[u, pl.ds(give2, quad_rows)],
            pr_v.at[u],
            ps_sem.at[0, u],
            pr_sem.at[0, u],
            p_id,
        )

    def qrs_copy(u, k):
        return remote(
            gw_v.at[u, at_quad(q_at[k])],
            qr_v.at[u, quad],
            qs_sem.at[0, u, k],
            qr_sem.at[0, u, quad],
            q_ids[k],
        )

    def qrs_from(u, k):
        return remote(
            gw_v.at[u, at_quad(q_at[k])],
            qr_v.at[u, q_at[k]],
            qs_sem.at[0, u, k],
            qr_sem.at[0, u, q_at[k]],
            q_ids[k],
        )

    def qag_copy(u, k):
        at = at_quad(quad)
        return remote(
            sum_v.at[u, at], sum_v.at[u, at], qs_sem.at[1, u, k], qr_sem.at[1, u, quad], q_ids[k]
        )

    def qag_from(u, k):
        at = at_quad(q_at[k])
        return remote(
            sum_v.at[u, at],
            sum_v.at[u, at],
            qs_sem.at[1, u, k],
            qr_sem.at[1, u, q_at[k]],
            q_ids[k],
        )

    def pag_copy(u):
        at = pl.ds(own2, quad_rows)
        return remote(sum_v.at[u, at], sum_v.at[u, at], ps_sem.at[1, u], pr_sem.at[1, u], p_id)

    def pag_from(u):
        at = pl.ds(give2, quad_rows)
        return remote(sum_v.at[u, at], sum_v.at[u, at], ps_sem.at[1, u], pr_sem.at[1, u], p_id)

    def xag_copy(u):
        at = pl.ds(own1, half_rows)
        return remote(sum_v.at[u, at], sum_v.at[u, at], xs_sem.at[1, u], xr_sem.at[1, u], x_id)

    def xag_from(u):
        at = pl.ds(pl.multiple_of((1 - xbit) * half_rows, 16), half_rows)
        return remote(sum_v.at[u, at], sum_v.at[u, at], xs_sem.at[1, u], xr_sem.at[1, u], x_id)

    def add_rows(u, start, got):
        at = pl.ds(start, got.shape[0])
        gw_v[u, at, :] = (gw_v[u, at, :].astype(F32) + got.astype(F32)).astype(BF16)

    def step1(u):
        xrs_copy(u).wait_recv()
        add_rows(u, give2, xr_v[u, pl.ds(pl.multiple_of(give2 - own1, 16), quad_rows), :])
        prs_copy(u).start()
        add_rows(u, own2, xr_v[u, pl.ds(pl.multiple_of(own2 - own1, 16), quad_rows), :])

    def step2(u):
        prs_copy(u).wait_recv()
        add_rows(u, own2, pr_v[u])
        for k in range(quads - 1):
            qrs_copy(u, k).start()

    def step3(u):
        total = gw_v[u, at_quad(quad), :].astype(F32)
        for k in range(quads - 1):
            qrs_from(u, k).wait_recv()
            total = total + qr_v[u, q_at[k]].astype(F32)
        sum_v[u, at_quad(quad), :] = total.astype(BF16)
        for k in range(quads - 1):
            qag_copy(u, k).start()

    def step4(u):
        for k in range(quads - 1):
            qag_from(u, k).wait_recv()
        pag_copy(u).start()

    def step5(u):
        pag_from(u).wait_recv()
        xag_copy(u).start()

    def out_copy(u):
        return pltpu.make_async_copy(sum_v.at[u], gw_hbm.at[u], out_sem.at[1 + u])

    def step6(u):
        xag_from(u).wait_recv()
        out_copy(u).start()

    steps = {1: step1, 2: step2, 3: step3, 4: step4, 5: step5, 6: step6}
    if units == 6:
        early = {
            (0, 2): [(1, 0)],
            (1, 2): [(1, 1), (2, 0)],
            (2, 1): [(1, 2)],
            (2, 2): [(2, 1), (3, 0)],
            (2, 5): [(1, 3), (2, 2)],
        }
        late = [(3, 1), (4, 0), (2, 3), (7, 0), (3, 2), (5, 0), (4, 1), (8, 0), (1, 4), (3, 3)]
        late += [(4, 2), (5, 1), (1, 5), (9, 0), (2, 4), (4, 3), (5, 2), (10, 0), (6, 0), (3, 4)]
        late += [(2, 5), (5, 3), (6, 1), (4, 4), (11, 0), (3, 5), (6, 2), (5, 4), (4, 5), (6, 3)]
        late += [(5, 5), (6, 4), (6, 5)]
    else:
        early = {}
        late = [(n, u) for n in range(1, 7) for u in range(units)]
        late = late[:units] + [(n, 0) for n in range(7, 12)] + late[units:]

    def serve(i, point):
        for (turn, place), todo in early.items():
            if place == point:

                @pl.when(i == turn)
                def _():
                    for n, u in todo:
                        steps[n](u)

    @pl.loop(0, sentences)
    def _(i):
        s = order(i)
        r0 = pl.multiple_of(s * SEQ_LEN, SEQ_LEN)
        cols = pl.ds(r0, SEQ_LEN)
        own0 = pl.multiple_of(r0 + core * HALF, HALF)
        y_copy(HID, i).wait_recv()
        gather_copy(G_FFN, gffn_v, i).wait_send()

        @pl.loop(0, HALF // BLOCK)
        def _(j):
            rows = pl.ds(pl.multiple_of(j * BLOCK, BLOCK), BLOCK)
            full = pl.ds(pl.multiple_of(own0 + j * BLOCK, BLOCK), BLOCK)
            kept = pl.ds(pl.multiple_of(i * HALF + j * BLOCK, BLOCK), BLOCK)
            grad_hidden = res2_v[kept, :] + total_rows(HID, i, rows)
            normed = norm1_v[kept, :]
            inv = inv1_v[kept, :][:, :1]
            scaled = grad_hidden * gain1_row[...]
            grad = inv * (scaled - row_mean(scaled) - normed * row_mean(scaled * normed))
            gattn_v[full, :] = grad.astype(BF16)
            add_acc(1, grad)
            add_acc(2, grad_hidden * normed)
            add_acc(3, grad_hidden)

        gather_copy(G_ATTN, gattn_v, i).start()
        fill_mask(s)
        serve(i, 1)
        gather_copy(G_ATTN, gattn_v, i).wait_recv()
        do_v[...] = mm(wo_v[...], gattn_v[cols, :], NT).astype(BF16)
        for h in range(heads):
            k_t = qkv_v[pl.ds(qw + h * HEAD, HEAD), cols]
            v_t = qkv_v[pl.ds(2 * qw + h * HEAD, HEAD), cols]
            grad_k = None
            grad_v = None
            for qb in range(2):
                qcols = pl.ds(pl.multiple_of(r0 + qb * HALF, HALF), HALF)
                q_t = qkv_v[pl.ds(h * HEAD, HEAD), qcols]
                d_t = do_v[pl.ds(h * HEAD, HEAD), pl.ds(qb * HALF, HALF)]
                c_t = ctx_v[pl.ds(h * HEAD, HEAD), qcols]
                delta = jnp.sum(d_t.astype(F32) * c_t.astype(F32), axis=0, keepdims=True)
                shares = jnp.exp(masked_scores(k_t, q_t) - lse_v[pl.ds(h, 1), qcols])
                grad_shares = mm(v_t, d_t, TN)
                grad_scores = (shares * (grad_shares - delta)).astype(BF16)
                gt_v[pl.ds(h * HEAD, HEAD), qcols] = (
                    mm(k_t, grad_scores, NN) * HEAD ** (-0.5)
                ).astype(BF16)
                new_k = mm(q_t, grad_scores, NT)
                new_v = mm(d_t, shares.astype(BF16), NT)
                grad_k = new_k if grad_k is None else grad_k + new_k
                grad_v = new_v if grad_v is None else grad_v + new_v
            gt_v[pl.ds(qw + h * HEAD, HEAD), cols] = grad_k.astype(BF16)
            gt_v[pl.ds(2 * qw + h * HEAD, HEAD), cols] = grad_v.astype(BF16)
            serve(i, 2 + h)

        @pl.loop(0, SEQ_LEN // 128)
        def _(j):
            blk = s * (SEQ_LEN // 128) + j
            quarter = blk // 3
            place = lax.rem(blk, 3)
            slot = (quarter // 2) * 3 + place
            bcols = pl.ds(pl.multiple_of(r0 + j * 128, 128), 128)
            part = mm(gt_v[:, bcols], wqkv_v[...], TN).astype(BF16)

            @pl.when(lax.rem(quarter, 2) == core)
            def _():
                tow_v[slot] = part

            @pl.when(lax.rem(quarter, 2) == other)
            def _():
                tcs_v[slot] = part
                remote(
                    tcs_v.at[slot],
                    tcr_v.at[slot],
                    tcs_sem.at[slot],
                    tcr_sem.at[slot],
                    core_id,
                ).start()

        serve(i, 5)

    ones = jnp.ones((8, rows_all), BF16)
    vec_v[...] = jnp.zeros_like(vec_v)
    vec_v[pl.ds(0, 1), pl.ds(0, qw)] = mm(ones, gt_v[pl.ds(0, qw), :], NT)[:1]
    vec_v[pl.ds(0, 1), pl.ds(256, qw)] = mm(ones, gt_v[pl.ds(2 * qw, qw), :], NT)[:1]
    for k in range(7):
        vec_v[pl.ds(1 + k, 1), :] = jnp.sum(acc_v[pl.ds(8 * k, 8), :], axis=0, keepdims=True)
    v_core = remote(vec_v, vc_v, vs_sem.at[0], vr_sem.at[0], core_id)
    v_core.start()

    store_unit(2, 0, mm(gt_v[pl.ds(0, 384), :], tok_v[...], NN))
    last = [
        mm(gt_v[pl.ds(384, 192), :], tok_v[...], NN),
        mm(ctx_v[...], gattn_v[...], NN),
    ]
    store_unit(2, 1, jnp.concatenate(last, axis=0))
    v_core.wait()
    row_id = lax.broadcasted_iota(jnp.int32, vec_v.shape, 0)
    vx_v[0] = vec_v[...] + jnp.where(row_id >= 2, vc_v[...], 0.0)
    v_x = remote(vx_v.at[0], vx_v.at[1], vs_sem.at[1], vr_sem.at[1], x_id)
    v_x.start()
    for u in range(2 * subs, 3 * subs):
        xrs_copy(u).start()

    def t_core(slot):
        return remote(
            tcs_v.at[slot], tcr_v.at[slot], tcs_sem.at[slot], tcr_sem.at[slot], core_id
        )

    def t_y(k):
        return remote(tys_v.at[k], tyr_v.at[k], tys_sem.at[k], tyr_sem.at[k], y_id)

    for k in range(3):
        slot = (1 - chip) * 3 + k
        t_core(slot).wait_recv()
        tys_v[k] = (tow_v[slot].astype(F32) + tcr_v[slot].astype(F32)).astype(BF16)
        t_y(k).start()

    v_p = remote(vx_v.at[2], vx_v.at[3], vs_sem.at[2], vr_sem.at[2], p_id)

    def vector_step1(_):
        v_x.wait()
        vx_v[2] = vx_v[0] + vx_v[1]
        v_p.start()

    def vq_copy(k):
        return remote(vq_v.at[quad], vq_v.at[quad], vqs_sem.at[k], vqr_sem.at[quad], q_ids[k])

    def vq_from(k):
        q = q_at[k]
        return remote(vq_v.at[q], vq_v.at[q], vqs_sem.at[k], vqr_sem.at[q], q_ids[k])

    def vector_step2(_):
        v_p.wait()
        vq_v[quad] = vx_v[2] + vx_v[3]
        for k in range(quads - 1):
            vq_copy(k).start()

    def vector_step3(_):
        for k in range(quads - 1):
            vq_from(k).wait_recv()
        total = vq_v[0]
        for q in range(1, quads):
            total = total + vq_v[q]
        vec_ref[...] = total

    quarter_rows = rows_all // 4
    lay_out = pltpu.make_async_copy(
        lay_v.at[pl.ds(pl.multiple_of(tp * quarter_rows, quarter_rows), quarter_rows)],
        lay_hbm,
        out_sem.at[0],
    )

    def layer_step(_):
        for i in range(sentences):
            gather_copy(G_RES, lay_v, i).wait_recv()
        lay_out.start()
        for s in range(sentences):
            key = lax.broadcasted_iota(jnp.int32, (8, SEQ_LEN), 1)
            member = jnp.where(key < len_ref[s], 1.0, 0.0).astype(BF16)
            total = mm(member, lay_v[pl.ds(s * SEQ_LEN, SEQ_LEN), :], NN)[:1]
            average = total / len_ref[s].astype(F32)
            at = 0
            for cut in (width, width * 2 // 3, width // 3, width // 6, width // 12):
                prefix = average[:, :cut]
                centred = prefix - row_mean(prefix)
                pool_ref[pl.ds(s, 1), pl.ds(at, cut)] = centred * lax.rsqrt(
                    row_mean(centred * centred) + EPSILON
                )
                at += cut

    def input_step(_):
        for k in range(3):
            slot = chip * 3 + k
            t_core(slot).wait_recv()
            mine = (tow_v[slot].astype(F32) + tcr_v[slot].astype(F32)).astype(BF16)
            t_y(k).wait_recv()
            at = pl.ds(pl.multiple_of(tp * quarter_rows + k * 128, 128), 128)
            gtok_ref[pl.ds(k * 128, 128), :] = (
                gattn_v[at, :].astype(F32) + (mine.astype(F32) + tyr_v[k].astype(F32))
            ).astype(BF16)

    steps[7] = vector_step1
    steps[8] = vector_step2
    steps[9] = input_step
    steps[10] = vector_step3
    steps[11] = layer_step
    for n, u in late:
        steps[n](u)

    for u in range(units):
        out_copy(u).wait()
    lay_out.wait()
    for i in range(sentences):
        core_copy(FFN, i).wait_send()
        y_copy(FFN, i).wait_send()
        core_copy(HID, i).wait_send()
        y_copy(HID, i).wait_send()
        gather_copy(G_HID, hid_v, i).wait_send()
        gather_copy(G_RES, lay_v, i).wait_send()
        gather_copy(G_ATTN, gattn_v, i).wait_send()
    for slot in range(6):
        t_core(slot).wait_send()
    for k in range(3):
        t_y(k).wait_send()
    for u in range(units):
        xrs_copy(u).wait_send()
        prs_copy(u).wait_send()
        pag_copy(u).wait_send()
        xag_copy(u).wait_send()
        for k in range(quads - 1):
            qrs_copy(u, k).wait_send()
            qag_copy(u, k).wait_send()
    for k in range(quads - 1):
        vq_copy(k).wait_send()


def layer_call(batch_size, tp_size, args):
    (
        tokens,
        w_query,
        b_query,
        w_key,
        w_value,
        b_value,
        w_attn_out,
        b_attn_out,
        gain_one,
        bias_one,
        w_in,
        b_in,
        w_out,
        b_out,
        gain_two,
        bias_two,
        lengths,
        grad_out,
    ) = args
    rows, width = tokens.shape
    sentences = lengths.shape[0]
    qw = w_attn_out.shape[0]
    ff = w_in.shape[1]
    quads = batch_size // 4
    units = 6 if (width // 2) % (16 * batch_size) == 0 else 3
    piece = -(-(width * 3 // units) // batch_size)
    piece = -(-piece // 16) * 16
    padded = piece * batch_size
    quarter = rows // tp_size
    anyspec = pl.BlockSpec(memory_space=pl.ANY)
    vmem = pl.BlockSpec(memory_space=pltpu.VMEM)
    smem = pl.BlockSpec(memory_space=pltpu.SMEM)
    dma = pltpu.SemaphoreType.DMA
    V = pltpu.VMEM
    kept = rows // 2
    return pl.pallas_call(
        lambda *refs: layer_kernel(batch_size, units, *refs),
        out_shape=(
            jax.ShapeDtypeStruct((quarter, width), BF16),
            jax.ShapeDtypeStruct((sentences, width * 9 // 4), F32),
            jax.ShapeDtypeStruct((quarter, width), BF16),
            jax.ShapeDtypeStruct((units, padded, width), BF16),
            jax.ShapeDtypeStruct((8, width), F32),
        ),
        in_specs=[smem] + [anyspec] * 8 + [vmem] * 9,
        out_specs=(anyspec, vmem, vmem, anyspec, vmem),
        scratch_shapes=[
            V((rows, width), BF16),
            V((3 * qw, width), BF16),
            V((qw, width), BF16),
            V((width, ff), BF16),
            V((ff, width), BF16),
            V((kept, width), BF16),
            V((3 * qw, rows), BF16),
            V((qw, rows), BF16),
            V((8, rows), F32),
            V((rows, width), BF16),
            V((rows, ff), BF16),
            V((rows, ff), BF16),
            V((kept, width), F32),
            V((kept, 128), F32),
            V((kept, width), F32),
            V((rows, width), BF16),
            V((rows, width), BF16),
            V((3 * qw, rows), BF16),
            V((qw, SEQ_LEN), BF16),
            V((SEQ_LEN, 128), F32),
            V((HALF, ff), F32),
            V((HALF, width), F32),
            V((2 * sentences, HALF, width), BF16),
            V((2 * sentences, HALF, width), BF16),
            V((2 * sentences, HALF, width), BF16),
            V((2 * sentences, HALF, width), BF16),
            V((6, 128, width), BF16),
            V((6, 128, width), BF16),
            V((6, 128, width), BF16),
            V((3, 128, width), BF16),
            V((3, 128, width), BF16),
            V((units, padded, width), BF16),
            V((units, padded, width), BF16),
            V((units, padded // 2, width), BF16),
            V((units, padded // 4, width), BF16),
            V((units, quads, piece, width), BF16),
            V((ff, width), F32),
            V((8, width), F32),
            V((64, width), F32),
            V((8, width), F32),
            V((8, width), F32),
            V((4, 8, width), F32),
            V((quads, 8, width), F32),
            dma((2 * sentences + 6,)),
            dma((3 * sentences,)),
            dma((3 * sentences,)),
            dma((3 * sentences,)),
            dma((3 * sentences,)),
            dma((4 * sentences,)),
            dma((4 * sentences,)),
            dma((6,)),
            dma((6,)),
            dma((3,)),
            dma((3,)),
            dma((2, units)),
            dma((2, units)),
            dma((2, units)),
            dma((2, units)),
            dma((2, units, quads)),
            dma((2, units, quads)),
            dma((3,)),
            dma((3,)),
            dma((quads,)),
            dma((quads,)),
            dma((1 + units,)),
        ],
        compiler_params=pltpu.CompilerParams(
            collective_id=0, has_side_effects=True, vmem_limit_bytes=63 << 20
        ),
    )(
        lengths,
        tokens,
        w_query.T,
        w_key.T,
        w_value.T,
        w_attn_out,
        w_in,
        w_out,
        grad_out,
        b_query,
        b_value,
        b_in,
        b_attn_out,
        gain_one,
        bias_one,
        b_out,
        gain_two,
        bias_two,
    )


def unpack_kernel(
    qw,
    gw_hbm,
    lay_in,
    gtok_in,
    pool_in,
    vec_in,
    lay_ref,
    pool_ref,
    gtok_ref,
    wq_hbm,
    bq_ref,
    wk_hbm,
    wv_hbm,
    bv_ref,
    wo_hbm,
    battn_ref,
    gain1_ref,
    bias1_ref,
    win_hbm,
    bin_ref,
    wout_hbm,
    bout_ref,
    gain2_ref,
    bias2_ref,
    low_v,
    full_v,
    in_sem,
    out_sem,
    side_sem,
):
    units, padded, width = low_v.shape
    subs = units // 3
    unit_rows = width // subs
    ins = [pltpu.make_async_copy(gw_hbm.at[u], low_v.at[u], in_sem.at[u]) for u in range(units)]
    for copy in ins:
        copy.start()
    side = [
        pltpu.make_async_copy(src, dst, side_sem.at[k])
        for k, (src, dst) in enumerate(((lay_in, lay_ref), (gtok_in, gtok_ref), (pool_in, pool_ref)))
    ]
    for copy in side:
        copy.start()
    outs = []

    def send(at, count, dst):
        copy = pltpu.make_async_copy(full_v.at[pl.ds(at, count)], dst, out_sem.at[len(outs)])
        copy.start()
        outs.append(copy)

    for u in range(units):
        ins[u].wait()
        full_v[pl.ds(u * unit_rows, unit_rows), :] = low_v[u, pl.ds(0, unit_rows), :].astype(F32)
        if u < 2 * subs:
            dst = (wout_hbm, win_hbm)[u // subs]
            send(u * unit_rows, unit_rows, dst.at[pl.ds((u % subs) * unit_rows, unit_rows)])
    for k, dst in enumerate((wq_hbm, wk_hbm, wv_hbm, wo_hbm)):
        send(2 * width + k * qw, qw, dst)
    bq_ref[...] = vec_in[0, pl.ds(0, qw)]
    bv_ref[...] = vec_in[0, pl.ds(256, qw)]
    for k, ref in enumerate(
        (bin_ref, battn_ref, gain1_ref, bias1_ref, bout_ref, gain2_ref, bias2_ref)
    ):
        ref[...] = vec_in[1 + k, :]
    for copy in outs + side:
        copy.wait()


def unpack_call(qw, lay, pooled, gtok, gw, vec):
    units, padded, width = gw.shape
    anyspec = pl.BlockSpec(memory_space=pl.ANY)
    vmem = pl.BlockSpec(memory_space=pltpu.VMEM)
    like = lambda v: jax.ShapeDtypeStruct(v.shape, v.dtype)
    mat = lambda n: jax.ShapeDtypeStruct((n, width), F32)
    one = lambda n: jax.ShapeDtypeStruct((n,), F32)
    outs = pl.pallas_call(
        lambda *refs: unpack_kernel(qw, *refs),
        out_shape=(
            like(lay),
            like(pooled),
            like(gtok),
            mat(qw),
            one(qw),
            mat(qw),
            mat(qw),
            one(qw),
            mat(qw),
            one(width),
            one(width),
            one(width),
            mat(width),
            one(width),
            mat(width),
            one(width),
            one(width),
            one(width),
        ),
        in_specs=[anyspec] * 4 + [vmem],
        out_specs=tuple(
            anyspec if k in (3, 5, 6, 8, 12, 14) else vmem for k in range(18)
        ),
        scratch_shapes=[
            pltpu.VMEM((units, padded, width), BF16),
            pltpu.VMEM((3 * width, width), F32),
            pltpu.SemaphoreType.DMA((units,)),
            pltpu.SemaphoreType.DMA((2 * units + 4,)),
            pltpu.SemaphoreType.DMA((3,)),
        ],
        compiler_params=pltpu.CompilerParams(vmem_limit_bytes=63 << 20),
    )(gw, lay, gtok, pooled, vec)
    return tuple(v.T if k in (3, 5, 6) else v for k, v in enumerate(outs))


def shards(*args):
    batch_size = lax.axis_size("batch")
    tp_size = lax.axis_size("tp")
    return unpack_call(args[6].shape[0], *layer_call(batch_size, tp_size, args))


def solution(mesh):
    placed = (
        P("batch", None),
        P(None, "tp"),
        P("tp"),
        P(None, "tp"),
        P(None, "tp"),
        P("tp"),
        P("tp", None),
        P(),
        P(),
        P(),
        P(None, "tp"),
        P("tp"),
        P("tp", None),
        P(),
        P(),
        P(),
        P("batch"),
        P("batch", None),
    )
    return jax.shard_map(
        shards,
        mesh=mesh,
        in_specs=placed,
        out_specs=(
            P(("batch", "tp"), None),
            P("batch", None),
            P(("batch", "tp"), None),
            P(None, "tp"),
            P("tp"),
            P(None, "tp"),
            P(None, "tp"),
            P("tp"),
            P("tp", None),
            P(),
            P(),
            P(),
            P(None, "tp"),
            P("tp"),
            P("tp", None),
            P(),
            P(),
            P(),
        ),
        check_vma=False,
    )
```

```python
import math

import jax
import jax.numpy as jnp
from jax import lax
from jax.experimental import pallas as pl
from jax.experimental.pallas import tpu as pltpu
from jax.sharding import PartitionSpec as P

HEAD = 64
SEQ_LEN = 512
HALF = SEQ_LEN // 2
EPSILON = 1e-06
BLOCK = 256
F32 = jnp.float32
BF16 = jnp.bfloat16
MESH = pl.DeviceIdType.MESH

NN = (((1,), (0,)), ((), ()))
NT = (((1,), (1,)), ((), ()))
TN = (((0,), (0,)), ((), ()))

ATTN, FFN, HID = 0, 1, 2
G_HID, G_FFN, G_RES, G_ATTN = 0, 1, 2, 3


UNITS = [
    (0, 128, [[0], [1, 2]], [[1, 2], [0]]),
    (128, 256, [[0], [1, 2]], [[2], [1], [0]]),
    (384, 384, [[1], [0], [2]], [[2], [0], [1]]),
    (768, 128, [[1], [0], [2]], [[2], [0], [1]]),
    (896, 256, [[0], [1], [2]], [[2], [1], [0]]),
    (1152, 128, [[0], [1], [2]], [[2], [1], [0]]),
    (1280, 128, [[0], [1], [2]], [[2], [1], [0]]),
    (1408, 128, [[0], [1, 2]], [[1, 2], [0]]),
    (1536, 128, [[0], [1], [2]], [[1, 2], [0]]),
    (1664, 256, [[0], [1], [2]], [[1, 2], [0]]),
    (1920, 256, [[0], [1], [2]], [[1, 2], [0]]),
    (2176, 128, [[1, 2], [0]], [[0], [1, 2]]),
]
EARLY = {
    (0, 1): [(1, 0)],
    (0, 3): [(1, 1), (1, 2)],
    (0, 4): [(1, 3)],
    (0, 5): [(1, 4)],
    (1, 1): [(2, 0)],
    (1, 2): [(1, 5)],
    (1, 3): [(1, 6), (2, 1), (2, 4)],
    (1, 4): [(1, 7)],
    (1, 5): [(2, 5), (3, 0), (2, 6), (2, 2)],
    (2, 1): [(2, 3), (3, 1)],
    (2, 2): [(3, 4)],
    (2, 3): [(4, 0)],
    (2, 5): [(2, 7), (3, 5), (3, 6), (4, 1)],
}
LATE = [
    (3, 2),
    (3, 3),
    (1, 8),
    (4, 4),
    (111, 0),
    (1, 9),
    (1, 11),
    (2, 8),
    (1, 10),
    (3, 7),
    (5, 4),
    (4, 5),
    (4, 6),
    (2, 9),
    (5, 1),
    (107, 0),
    (4, 2),
    (2, 10),
    (2, 11),
    (4, 3),
    (5, 5),
    (109, 0),
    (3, 8),
    (5, 6),
    (4, 7),
    (108, 0),
    (3, 9),
    (3, 10),
    (6, 4),
    (4, 8),
    (110, 0),
    (5, 2),
    (3, 11),
    (5, 3),
    (6, 5),
    (4, 9),
    (6, 6),
    (5, 8),
    (4, 10),
    (6, 2),
    (5, 9),
    (4, 11),
    (6, 3),
    (5, 10),
]


def mm(left, right, dims):
    return lax.dot_general(left, right, dims, preferred_element_type=F32)


def fold8(block):
    rows, width = block.shape
    return jnp.sum(block.reshape(rows // 8, 8, width), axis=0)


def row_mean(block):
    return jnp.mean(block, axis=-1, keepdims=True)


def layer_kernel(
    batch_size,
    plan,
    early,
    late,
    len_ref,
    tok_hbm,
    wq_hbm,
    wk_hbm,
    wv_hbm,
    wo_hbm,
    win_hbm,
    wout_hbm,
    gout_hbm,
    bq_ref,
    bv_ref,
    bin_ref,
    battn_ref,
    gain1_ref,
    bias1_ref,
    bout_ref,
    gain2_ref,
    bias2_ref,
    lay_hbm,
    pool_ref,
    gtok_ref,
    gw_hbm,
    vec_ref,
    tok_v,
    wqkv_v,
    wo_v,
    win_v,
    wout_v,
    gout_v,
    qkv_v,
    ctx_v,
    lse_v,
    hid_v,
    act_v,
    slope_v,
    norm1_v,
    inv1_v,
    res2_v,
    gffn_v,
    lay_v,
    gt_v,
    do_v,
    mask_v,
    big_v,
    part_v,
    cs_v,
    cr_v,
    ys_v,
    yr_v,
    tcs_v,
    tcr_v,
    tow_v,
    tys_v,
    tyr_v,
    gw_v,
    sum_v,
    rv_v,
    wacc_v,
    par_v,
    acc_v,
    vec_v,
    vc_v,
    vx_v,
    vq_v,
    in_sem,
    cs_sem,
    cr_sem,
    ys_sem,
    yr_sem,
    as_sem,
    ar_sem,
    tcs_sem,
    tcr_sem,
    tys_sem,
    tyr_sem,
    ws_sem,
    wr_sem,
    vs_sem,
    vr_sem,
    vqs_sem,
    vqr_sem,
    out_sem,
):
    rows_all, width = tok_v.shape
    sentences = rows_all // SEQ_LEN
    qw = wo_v.shape[0]
    heads = qw // HEAD
    quads = batch_size // 4
    bits = batch_size.bit_length() - 1

    gattn_v = gffn_v
    din_v = slope_v

    tp = lax.axis_index("tp")
    ba = lax.axis_index("batch")
    core = lax.rem(tp, 2)
    other = 1 - core
    chip = tp // 2
    quad = ba // 4
    bit = [lax.rem(ba // 2**k, 2) for k in range(bits)]
    core_id = {"tp": chip * 2 + other}
    y_id = {"tp": (1 - chip) * 2 + core}

    def flip_id(flips):
        at = ba
        for k in flips:
            at = at + (1 - 2 * bit[k]) * 2**k
        return {"batch": at}

    def flip_quad(flips):
        at = quad
        for k in flips:
            at = at + (1 - 2 * bit[k]) * 2 ** (k - 2)
        return at

    def subsets(group):
        return [
            [k for j, k in enumerate(group) if n >> j & 1] for n in range(1, 2 ** len(group))
        ]

    quad_flips = subsets(range(2, bits))
    batch_peers = []
    for _, _, down, up in plan:
        for group in down + up:
            batch_peers += [f for f in subsets(group) if f not in batch_peers]
    for f in [[0], [1]] + quad_flips:
        if f not in batch_peers:
            batch_peers.append(f)

    def remote(src, dst, send, recv, dev):
        return pltpu.make_async_remote_copy(
            src_ref=src,
            dst_ref=dst,
            send_sem=send,
            recv_sem=recv,
            device_id=dev,
            device_id_type=MESH,
        )

    def order(i):
        return lax.rem(2 * i, sentences)

    def tok_copy(i):
        rows = pl.ds(pl.multiple_of(order(i) * SEQ_LEN, SEQ_LEN), SEQ_LEN)
        return pltpu.make_async_copy(tok_hbm.at[rows], tok_v.at[rows], in_sem.at[i])

    w_copies = [
        pltpu.make_async_copy(src, dst, in_sem.at[sentences + k])
        for k, (src, dst) in enumerate(
            [
                (wq_hbm, wqkv_v.at[pl.ds(0, qw)]),
                (wk_hbm, wqkv_v.at[pl.ds(qw, qw)]),
                (wv_hbm, wqkv_v.at[pl.ds(2 * qw, qw)]),
                (wo_hbm, wo_v),
                (win_hbm, win_v),
                (wout_hbm, wout_v),
            ]
        )
    ]

    def gout_copy(i):
        src = pl.ds(pl.multiple_of(order(i) * SEQ_LEN + core * HALF, HALF), HALF)
        dst = pl.ds(pl.multiple_of(i * HALF, HALF), HALF)
        return pltpu.make_async_copy(
            gout_hbm.at[src], gout_v.at[dst], in_sem.at[sentences + 6 + i]
        )

    for k in range(3):
        w_copies[k].start()
    for i in range(sentences):
        tok_copy(i).start()
    for k in range(3, 6):
        w_copies[k].start()
    for i in range(sentences):
        gout_copy(i).start()

    barrier = pltpu.get_barrier_semaphore()
    peers = [core_id, y_id] + [flip_id(f) for f in batch_peers]
    for dev in peers:
        pl.semaphore_signal(barrier, inc=1, device_id=dev, device_id_type=MESH)

    acc_v[...] = jnp.zeros_like(acc_v)
    for k, ref in enumerate(
        (bin_ref, battn_ref, gain1_ref, bias1_ref, bout_ref, gain2_ref, bias2_ref)
    ):
        par_v[pl.ds(k, 1), :] = ref[...].reshape(1, width)
    bin_row, battn_row, gain1_row, bias1_row, bout_row, gain2_row, bias2_row = [
        par_v.at[pl.ds(k, 1)] for k in range(7)
    ]

    def core_copy(ph, i):
        k = ph * sentences + i
        slot = (ph % 2) * sentences + i
        return remote(cs_v.at[slot], cr_v.at[slot], cs_sem.at[k], cr_sem.at[k], core_id)

    def y_copy(ph, i):
        k = ph * sentences + i
        slot = (ph % 2) * sentences + i
        return remote(ys_v.at[slot], yr_v.at[slot], ys_sem.at[k], yr_sem.at[k], y_id)

    def gather_copy(which, ref, i):
        k = which * sentences + i
        rows = pl.ds(pl.multiple_of(order(i) * SEQ_LEN + core * HALF, HALF), HALF)
        return remote(ref.at[rows], ref.at[rows], as_sem.at[k], ar_sem.at[k], core_id)

    def chip_sum(ph, i):
        slot = (ph % 2) * sentences + i
        core_copy(ph, i).wait_recv()

        @pl.loop(0, HALF // BLOCK)
        def _(j):
            rows = pl.ds(pl.multiple_of(j * BLOCK, BLOCK), BLOCK)
            ys_v[slot, rows, :] = (part_v[rows, :] + cr_v[slot, rows, :].astype(F32)).astype(BF16)

        y_copy(ph, i).start()

    def total_rows(ph, i, rows):
        slot = (ph % 2) * sentences + i
        return ys_v[slot, rows, :].astype(F32) + yr_v[slot, rows, :].astype(F32)

    def add_acc(k, value):
        rows = pl.ds(8 * k, 8)
        acc_v[rows, :] = acc_v[rows, :] + fold8(value)

    def fill_mask(s):
        limit = len_ref[s]
        key = lax.broadcasted_iota(jnp.int32, mask_v.shape, 0)
        mask_v[...] = jnp.where(key < limit, 0.0, -1e30)

    def masked_scores(k_t, q_t):
        mask = mask_v[...]
        return mm(k_t, q_t, TN) + jnp.concatenate([mask] * (q_t.shape[1] // 128), axis=1)

    def column(row_ref):
        row = row_ref[...].reshape(1, qw)
        return jnp.transpose(jnp.broadcast_to(row, (8, qw)))[:, :1]

    for k in range(3):
        w_copies[k].wait()

    def project(i):
        s = order(i)
        cols = pl.ds(pl.multiple_of(s * SEQ_LEN, SEQ_LEN), SEQ_LEN)
        tok_copy(i).wait()
        x = tok_v[cols, :]
        qkv_v[pl.ds(0, qw), cols] = (
            mm(wqkv_v[pl.ds(0, qw), :], x, NT) + column(bq_ref)
        ).astype(BF16) * jnp.asarray(HEAD ** (-0.5), BF16)
        qkv_v[pl.ds(qw, qw), cols] = mm(wqkv_v[pl.ds(qw, qw), :], x, NT).astype(BF16)
        qkv_v[pl.ds(2 * qw, qw), cols] = (
            mm(wqkv_v[pl.ds(2 * qw, qw), :], x, NT) + column(bv_ref)
        ).astype(BF16)
        fill_mask(s)

    def attend(i, half):
        r0 = pl.multiple_of(order(i) * SEQ_LEN, SEQ_LEN)
        cols = pl.ds(r0, SEQ_LEN)
        qcols = pl.ds(pl.multiple_of(r0 + half * HALF, HALF), HALF)
        for h in range(heads):
            k_t = qkv_v[pl.ds(qw + h * HEAD, HEAD), cols]
            v_t = qkv_v[pl.ds(2 * qw + h * HEAD, HEAD), cols]
            scores = masked_scores(k_t, qkv_v[pl.ds(h * HEAD, HEAD), qcols])
            top = jnp.max(scores, axis=0, keepdims=True)
            expo = jnp.exp(scores - top)
            total = jnp.sum(expo, axis=0, keepdims=True)
            shares = (expo * (1.0 / total)).astype(BF16)
            ctx_v[pl.ds(h * HEAD, HEAD), qcols] = mm(v_t, shares, NN).astype(BF16)
            lse_v[pl.ds(h, 1), qcols] = top + jnp.log(total)
        return mm(ctx_v[:, qcols], wo_v[...], TN)

    project(0)
    w_copies[3].wait()
    cs_v[0] = attend(0, other).astype(BF16)
    pl.semaphore_wait(barrier, len(peers))

    @pl.loop(0, sentences)
    def _(i):
        core_copy(ATTN, i).start()
        part_v[...] = attend(i, core)
        chip_sum(ATTN, i)

        @pl.when(i + 1 < sentences)
        def _():
            project(i + 1)
            cs_v[i + 1] = attend(i + 1, other).astype(BF16)

    w_copies[4].wait()
    w_copies[5].wait()

    @pl.loop(0, sentences)
    def _(i):
        r0 = pl.multiple_of(order(i) * SEQ_LEN, SEQ_LEN)
        own0 = pl.multiple_of(r0 + core * HALF, HALF)
        oth0 = pl.multiple_of(r0 + other * HALF, HALF)
        y_copy(ATTN, i).wait_recv()

        @pl.loop(0, HALF // BLOCK)
        def _(j):
            rows = pl.ds(pl.multiple_of(j * BLOCK, BLOCK), BLOCK)
            full = pl.ds(pl.multiple_of(own0 + j * BLOCK, BLOCK), BLOCK)
            kept = pl.ds(pl.multiple_of(i * HALF + j * BLOCK, BLOCK), BLOCK)
            resid = tok_v[full, :].astype(F32) + (total_rows(ATTN, i, rows) + battn_row[...])
            centred = resid - row_mean(resid)
            inv = lax.rsqrt(row_mean(centred * centred) + EPSILON)
            normed = centred * inv
            norm1_v[kept, :] = normed
            inv1_v[kept, :] = jnp.broadcast_to(inv, (BLOCK, 128))
            hid_v[full, :] = (normed * gain1_row[...] + bias1_row[...]).astype(BF16)

        gather_copy(G_HID, hid_v, i).start()

        def feed(base):
            big_v[...] = mm(hid_v[pl.ds(base, HALF), :], win_v[...], NN)

            @pl.loop(0, HALF // BLOCK)
            def _(j):
                rows = pl.ds(pl.multiple_of(j * BLOCK, BLOCK), BLOCK)
                full = pl.ds(pl.multiple_of(base + j * BLOCK, BLOCK), BLOCK)
                pre = big_v[rows, :] + bin_row[...]
                cdf = 0.5 * (1.0 + lax.erf(pre * 0.5**0.5))
                act_v[full, :] = (pre * cdf).astype(BF16)
                slope_v[full, :] = (
                    cdf + pre * (jnp.exp(-0.5 * pre * pre) * (2.0 * math.pi) ** (-0.5))
                ).astype(slope_v.dtype)

            return mm(act_v[pl.ds(base, HALF), :], wout_v[...], NN)

        part_v[...] = feed(own0)
        gather_copy(G_HID, hid_v, i).wait_recv()
        slot = sentences + i
        cs_v[slot] = feed(oth0).astype(BF16)
        core_copy(FFN, i).start()
        chip_sum(FFN, i)

    chunk_rows = gw_v.shape[0] // 3

    def store_rows(j, t, block):
        gw_v[pl.ds(j * chunk_rows + t * 384, 384), :] = block.astype(BF16)

    stages = []
    used = 0
    for base, rows, down, up in plan:
        where, size, unit, spare = base, rows, [], base
        for group in down:
            unit_stage = {"sends": [], "waits": [], "adds": []}
            size = size // 2 ** len(group)

            def place(flips, group=group, where=where, size=size):
                at = where
                for j, k in enumerate(group):
                    side = 1 - bit[k] if k in flips else bit[k]
                    at = at + side * (size * 2 ** (len(group) - 1 - j))
                return at

            own = place([])
            for flips in subsets(group):
                src = gw_v.at[pl.ds(pl.multiple_of(place(flips), 16), size)]
                dst = rv_v.at[pl.ds(spare, size)]
                args = (src, dst, ws_sem.at[used], wr_sem.at[used], flip_id(flips))
                unit_stage["sends"].append(lambda args=args: remote(*args))
                unit_stage["waits"].append(lambda args=args: remote(*args))
                unit_stage["adds"].append((own, spare, size))
                spare += size
                used += 1
            unit.append(unit_stage)
            where = own
        final = (where, size)
        for group in up:
            unit_stage = {"sends": [], "waits": [], "adds": []}
            order_bits = [k for g in down for k in g]
            weight = {}
            width_of = rows
            for k in order_bits:
                width_of = width_of // 2
                weight[k] = width_of
            held = [k for g in up[: up.index(group)] for k in g]
            mine = base
            span = rows
            for k in order_bits:
                if k not in held:
                    mine = mine + bit[k] * weight[k]
                    span = span // 2
            for flips in subsets(group):
                theirs = mine
                for k in flips:
                    theirs = theirs + (1 - 2 * bit[k]) * weight[k]
                here = sum_v.at[pl.ds(pl.multiple_of(mine, 16), span)]
                there = sum_v.at[pl.ds(pl.multiple_of(theirs, 16), span)]
                sems = (ws_sem.at[used], wr_sem.at[used], flip_id(flips))
                unit_stage["sends"].append(lambda r=here, t=sems: remote(r, r, *t))
                unit_stage["waits"].append(lambda r=there, t=sems: remote(r, r, *t))
                used += 1
            unit.append(unit_stage)
        for unit_stage in unit:
            unit_stage["final"] = final
            unit_stage["last_down"] = len(down) - 1
        stages.append(unit)

    def start_stage(u, n):
        for copy in stages[u][n]["sends"]:
            copy().start()

    def out_copy(u):
        base, rows = plan[u][:2]
        at = pl.ds(base, rows)
        return pltpu.make_async_copy(sum_v.at[at], gw_hbm.at[at], out_sem.at[1 + u])

    def step(n, u):
        done = stages[u][n - 1]
        for copy in done["waits"]:
            copy().wait_recv()
        if done["adds"]:
            own, _, size = done["adds"][0]
            for r in range(0, size, 96):
                part = min(96, size - r)
                at = pl.ds(pl.multiple_of(own + r, 16), part)
                total = gw_v[at, :].astype(F32)
                for _, spare, _ in done["adds"]:
                    total = total + rv_v[pl.ds(spare + r, part), :].astype(F32)
                if n - 1 == done["last_down"]:
                    sum_v[at, :] = total.astype(BF16)
                else:
                    gw_v[at, :] = total.astype(BF16)
        if n < len(stages[u]):
            start_stage(u, n)
        else:
            out_copy(u).start()

    def start_chunk(c):
        for u, unit in enumerate(plan):
            if unit[0] // chunk_rows == c:
                start_stage(u, 0)

    wacc_v[...] = jnp.zeros_like(wacc_v)

    @pl.loop(0, sentences)
    def _(i):
        r0 = pl.multiple_of(order(i) * SEQ_LEN, SEQ_LEN)
        own0 = pl.multiple_of(r0 + core * HALF, HALF)
        oth0 = pl.multiple_of(r0 + other * HALF, HALF)
        gout_copy(i).wait()
        y_copy(FFN, i).wait_recv()

        @pl.loop(0, HALF // BLOCK)
        def _(j):
            rows = pl.ds(pl.multiple_of(j * BLOCK, BLOCK), BLOCK)
            full = pl.ds(pl.multiple_of(own0 + j * BLOCK, BLOCK), BLOCK)
            kept = pl.ds(pl.multiple_of(i * HALF + j * BLOCK, BLOCK), BLOCK)
            hidden = norm1_v[kept, :] * gain1_row[...] + bias1_row[...]
            resid = hidden + (total_rows(FFN, i, rows) + bout_row[...])
            centred = resid - row_mean(resid)
            inv = lax.rsqrt(row_mean(centred * centred) + EPSILON)
            normed = centred * inv
            lay_v[full, :] = (normed * gain2_row[...] + bias2_row[...]).astype(BF16)
            up = gout_v[kept, :].astype(F32)
            scaled = up * gain2_row[...]
            grad = inv * (scaled - row_mean(scaled) - normed * row_mean(scaled * normed))
            res2_v[kept, :] = grad
            gffn_v[full, :] = grad.astype(BF16)
            add_acc(4, grad)
            add_acc(5, up * normed)
            add_acc(6, up)

        gather_copy(G_FFN, gffn_v, i).start()
        gather_copy(G_RES, lay_v, i).start()

        def back(base):
            big_v[...] = mm(gffn_v[pl.ds(base, HALF), :], wout_v[...], NT)

            @pl.loop(0, HALF // BLOCK)
            def _(j):
                rows = pl.ds(pl.multiple_of(j * BLOCK, BLOCK), BLOCK)
                full = pl.ds(pl.multiple_of(base + j * BLOCK, BLOCK), BLOCK)
                inner = (big_v[rows, :] * slope_v[full, :].astype(F32)).astype(BF16)
                din_v[full, :] = inner
                add_acc(0, inner.astype(F32))

            return mm(din_v[pl.ds(base, HALF), :], win_v[...], NT)

        def grow(base):
            for t in range(width // 384):
                at = pl.ds(t * 384, 384)
                half = pl.ds(base, HALF)
                wacc_v[at, :] = wacc_v[at, :] + mm(act_v[half, at], gffn_v[half, :], TN)

        grow(own0)
        gather_copy(G_FFN, gffn_v, i).wait_recv()
        grow(oth0)

        @pl.when(i == sentences - 1)
        def _():
            for t in range(width // 384):
                store_rows(0, t, wacc_v[pl.ds(t * 384, 384), :])
            start_chunk(0)

        part_v[...] = back(own0)
        core_copy(ATTN, i).wait_send()
        cs_v[i] = back(oth0).astype(BF16)
        core_copy(HID, i).start()
        y_copy(ATTN, i).wait_send()
        chip_sum(HID, i)

    for t in range(width // 384):
        store_rows(1, t, mm(hid_v[:, pl.ds(t * 384, 384)], din_v[...], TN))
    start_chunk(1)

    steps = {}

    def run_step(n, u):
        if n in steps:
            steps[n]()
        else:
            step(n, u)

    def serve(i, point):
        for (turn, place), todo in early.items():
            if place == point:

                @pl.when(i == turn)
                def _():
                    for n, u in todo:
                        run_step(n, u)

    wacc_v[...] = jnp.zeros_like(wacc_v)

    @pl.loop(0, sentences)
    def _(i):
        s = order(i)
        r0 = pl.multiple_of(s * SEQ_LEN, SEQ_LEN)
        cols = pl.ds(r0, SEQ_LEN)
        own0 = pl.multiple_of(r0 + core * HALF, HALF)
        y_copy(HID, i).wait_recv()
        gather_copy(G_FFN, gffn_v, i).wait_send()

        @pl.loop(0, HALF // BLOCK)
        def _(j):
            rows = pl.ds(pl.multiple_of(j * BLOCK, BLOCK), BLOCK)
            full = pl.ds(pl.multiple_of(own0 + j * BLOCK, BLOCK), BLOCK)
            kept = pl.ds(pl.multiple_of(i * HALF + j * BLOCK, BLOCK), BLOCK)
            grad_hidden = res2_v[kept, :] + total_rows(HID, i, rows)
            normed = norm1_v[kept, :]
            inv = inv1_v[kept, :][:, :1]
            scaled = grad_hidden * gain1_row[...]
            grad = inv * (scaled - row_mean(scaled) - normed * row_mean(scaled * normed))
            gattn_v[full, :] = grad.astype(BF16)
            add_acc(1, grad)
            add_acc(2, grad_hidden * normed)
            add_acc(3, grad_hidden)

        gather_copy(G_ATTN, gattn_v, i).start()
        fill_mask(s)
        serve(i, 1)
        gather_copy(G_ATTN, gattn_v, i).wait_recv()
        do_v[...] = mm(wo_v[...], gattn_v[cols, :], NT).astype(BF16)
        for h in range(heads):
            k_t = qkv_v[pl.ds(qw + h * HEAD, HEAD), cols]
            v_t = qkv_v[pl.ds(2 * qw + h * HEAD, HEAD), cols]
            q_t = qkv_v[pl.ds(h * HEAD, HEAD), cols]
            d_t = do_v[pl.ds(h * HEAD, HEAD), :]
            c_t = ctx_v[pl.ds(h * HEAD, HEAD), cols]
            delta = jnp.sum(d_t.astype(F32) * c_t.astype(F32), axis=0, keepdims=True)
            shares = jnp.exp(masked_scores(k_t, q_t) - lse_v[pl.ds(h, 1), cols])
            grad_shares = mm(v_t, d_t, TN)
            grad_scores = (shares * (grad_shares - delta)).astype(BF16)
            gt_v[pl.ds(h * HEAD, HEAD), cols] = (
                mm(k_t, grad_scores, NN) * HEAD ** (-0.5)
            ).astype(BF16)
            gt_v[pl.ds(qw + h * HEAD, HEAD), cols] = mm(q_t, grad_scores, NT).astype(BF16)
            gt_v[pl.ds(2 * qw + h * HEAD, HEAD), cols] = mm(
                d_t, shares.astype(BF16), NT
            ).astype(BF16)
            serve(i, 2 + h)

        flat = pl.ds(0, 3 * qw)
        wacc_v[flat, :] = wacc_v[flat, :] + mm(gt_v[:, cols], tok_v[cols, :], NN)
        flat = pl.ds(3 * qw, qw)
        wacc_v[flat, :] = wacc_v[flat, :] + mm(ctx_v[:, cols], gattn_v[cols, :], NN)

        @pl.when(i == sentences - 1)
        def _():
            for t in range(width // 384):
                store_rows(2, t, wacc_v[pl.ds(t * 384, 384), :])
            start_chunk(2)

        @pl.loop(0, 2)
        def _(j2):
            hcols = pl.ds(pl.multiple_of(r0 + j2 * 256, 256), 256)
            half_part = mm(gt_v[:, hcols], wqkv_v[...], TN).astype(BF16)
            for j1 in range(2):
                blk = s * (SEQ_LEN // 128) + j2 * 2 + j1
                quarter = blk // 3
                place = lax.rem(blk, 3)
                slot = (quarter // 2) * 3 + place
                part = half_part[j1 * 128 : j1 * 128 + 128]

                @pl.when(lax.rem(quarter, 2) == core)
                def _():
                    tow_v[slot] = part

                @pl.when(lax.rem(quarter, 2) == other)
                def _():
                    tcs_v[slot] = part
                    remote(
                        tcs_v.at[slot],
                        tcr_v.at[slot],
                        tcs_sem.at[slot],
                        tcr_sem.at[slot],
                        core_id,
                    ).start()

        serve(i, 5)

    ones = jnp.ones((8, rows_all), BF16)
    vec_v[...] = jnp.zeros_like(vec_v)
    vec_v[pl.ds(0, 1), pl.ds(0, qw)] = mm(ones, gt_v[pl.ds(0, qw), :], NT)[:1]
    vec_v[pl.ds(0, 1), pl.ds(256, qw)] = mm(ones, gt_v[pl.ds(2 * qw, qw), :], NT)[:1]
    for k in range(7):
        vec_v[pl.ds(1 + k, 1), :] = jnp.sum(acc_v[pl.ds(8 * k, 8), :], axis=0, keepdims=True)
    v_core = remote(vec_v, vc_v, vs_sem.at[0], vr_sem.at[0], core_id)
    v_core.start()

    v_core.wait()
    row_id = lax.broadcasted_iota(jnp.int32, vec_v.shape, 0)
    vx_v[0] = vec_v[...] + jnp.where(row_id >= 2, vc_v[...], 0.0)
    v_x = remote(vx_v.at[0], vx_v.at[1], vs_sem.at[1], vr_sem.at[1], flip_id([0]))
    v_x.start()

    def t_core(slot):
        return remote(
            tcs_v.at[slot], tcr_v.at[slot], tcs_sem.at[slot], tcr_sem.at[slot], core_id
        )

    def t_y(k):
        return remote(tys_v.at[k], tyr_v.at[k], tys_sem.at[k], tyr_sem.at[k], y_id)

    for k in range(3):
        slot = (1 - chip) * 3 + k
        t_core(slot).wait_recv()
        tys_v[k] = (tow_v[slot].astype(F32) + tcr_v[slot].astype(F32)).astype(BF16)
        t_y(k).start()

    v_p = remote(vx_v.at[2], vx_v.at[3], vs_sem.at[2], vr_sem.at[2], flip_id([1]))

    def vector_step1():
        v_x.wait()
        vx_v[2] = vx_v[0] + vx_v[1]
        v_p.start()

    def vq_copy(k):
        return remote(
            vq_v.at[quad], vq_v.at[quad], vqs_sem.at[k], vqr_sem.at[quad], flip_id(quad_flips[k])
        )

    def vq_from(k):
        q = flip_quad(quad_flips[k])
        return remote(vq_v.at[q], vq_v.at[q], vqs_sem.at[k], vqr_sem.at[q], flip_id(quad_flips[k]))

    def vector_step2():
        v_p.wait()
        vq_v[quad] = vx_v[2] + vx_v[3]
        for k in range(quads - 1):
            vq_copy(k).start()

    def vector_step3():
        for k in range(quads - 1):
            vq_from(k).wait_recv()
        total = vq_v[0]
        for q in range(1, quads):
            total = total + vq_v[q]
        vec_ref[...] = total

    quarter_rows = rows_all // 4
    lay_out = pltpu.make_async_copy(
        lay_v.at[pl.ds(pl.multiple_of(tp * quarter_rows, quarter_rows), quarter_rows)],
        lay_hbm,
        out_sem.at[0],
    )

    def layer_step():
        for i in range(sentences):
            gather_copy(G_RES, lay_v, i).wait_recv()
        lay_out.start()
        for s in range(sentences):
            key = lax.broadcasted_iota(jnp.int32, (8, SEQ_LEN), 1)
            member = jnp.where(key < len_ref[s], 1.0, 0.0).astype(BF16)
            total = mm(member, lay_v[pl.ds(s * SEQ_LEN, SEQ_LEN), :], NN)[:1]
            average = total / len_ref[s].astype(F32)
            at = 0
            for cut in (width, width * 2 // 3, width // 3, width // 6, width // 12):
                prefix = average[:, :cut]
                centred = prefix - row_mean(prefix)
                pool_ref[pl.ds(s, 1), pl.ds(at, cut)] = centred * lax.rsqrt(
                    row_mean(centred * centred) + EPSILON
                )
                at += cut

    def input_step():
        for k in range(3):
            slot = chip * 3 + k
            t_core(slot).wait_recv()
            mine = (tow_v[slot].astype(F32) + tcr_v[slot].astype(F32)).astype(BF16)
            t_y(k).wait_recv()
            at = pl.ds(pl.multiple_of(tp * quarter_rows + k * 128, 128), 128)
            gtok_ref[pl.ds(k * 128, 128), :] = (
                gattn_v[at, :].astype(F32) + (mine.astype(F32) + tyr_v[k].astype(F32))
            ).astype(BF16)

    steps.update(
        {107: vector_step1, 108: vector_step2, 109: input_step, 110: vector_step3, 111: layer_step}
    )
    for n, u in late:
        run_step(n, u)

    for u in range(len(plan)):
        out_copy(u).wait()
    lay_out.wait()
    for i in range(sentences):
        core_copy(FFN, i).wait_send()
        y_copy(FFN, i).wait_send()
        core_copy(HID, i).wait_send()
        y_copy(HID, i).wait_send()
        gather_copy(G_HID, hid_v, i).wait_send()
        gather_copy(G_RES, lay_v, i).wait_send()
        gather_copy(G_ATTN, gattn_v, i).wait_send()
    for slot in range(6):
        t_core(slot).wait_send()
    for k in range(3):
        t_y(k).wait_send()
    for u in range(len(plan)):
        for n in range(len(stages[u])):
            for copy in stages[u][n]["sends"]:
                copy().wait_send()
    for k in range(quads - 1):
        vq_copy(k).wait_send()


def layer_call(batch_size, tp_size, args):
    (
        tokens,
        w_query,
        b_query,
        w_key,
        w_value,
        b_value,
        w_attn_out,
        b_attn_out,
        gain_one,
        bias_one,
        w_in,
        b_in,
        w_out,
        b_out,
        gain_two,
        bias_two,
        lengths,
        grad_out,
    ) = args
    rows, width = tokens.shape
    sentences = lengths.shape[0]
    qw = w_attn_out.shape[0]
    ff = w_in.shape[1]
    quads = batch_size // 4
    piece = -(-width // batch_size)
    piece = -(-piece // 16) * 16
    chunk = piece * batch_size
    if batch_size == 8:
        plan, early, late = UNITS, EARLY, LATE
    else:
        high = list(range(2, batch_size.bit_length() - 1))
        plan = [(c * chunk, chunk, [[0], [1], high], [high, [1], [0]]) for c in range(3)]
        early = {}
        late = [(n, u) for n in range(1, 7) for u in range(3)]
        late = late[:3] + [(n, 0) for n in range(107, 112)] + late[3:]
    copies = sum(2 ** len(g) - 1 for unit in plan for g in unit[2] + unit[3])
    quarter = rows // tp_size
    anyspec = pl.BlockSpec(memory_space=pl.ANY)
    vmem = pl.BlockSpec(memory_space=pltpu.VMEM)
    smem = pl.BlockSpec(memory_space=pltpu.SMEM)
    dma = pltpu.SemaphoreType.DMA
    V = pltpu.VMEM
    kept = rows // 2
    return pl.pallas_call(
        lambda *refs: layer_kernel(batch_size, plan, early, late, *refs),
        out_shape=(
            jax.ShapeDtypeStruct((quarter, width), BF16),
            jax.ShapeDtypeStruct((sentences, width * 9 // 4), F32),
            jax.ShapeDtypeStruct((quarter, width), BF16),
            jax.ShapeDtypeStruct((3 * chunk, width), BF16),
            jax.ShapeDtypeStruct((8, width), F32),
        ),
        in_specs=[smem] + [anyspec] * 8 + [vmem] * 9,
        out_specs=(anyspec, vmem, vmem, anyspec, vmem),
        scratch_shapes=[
            V((rows, width), BF16),
            V((3 * qw, width), BF16),
            V((qw, width), BF16),
            V((width, ff), BF16),
            V((ff, width), BF16),
            V((kept, width), BF16),
            V((3 * qw, rows), BF16),
            V((qw, rows), BF16),
            V((8, rows), F32),
            V((rows, width), BF16),
            V((rows, ff), BF16),
            V((rows, ff), BF16),
            V((kept, width), F32),
            V((kept, 128), F32),
            V((kept, width), F32),
            V((rows, width), BF16),
            V((rows, width), BF16),
            V((3 * qw, rows), BF16),
            V((qw, SEQ_LEN), BF16),
            V((SEQ_LEN, 128), F32),
            V((HALF, ff), F32),
            V((HALF, width), F32),
            V((2 * sentences, HALF, width), BF16),
            V((2 * sentences, HALF, width), BF16),
            V((2 * sentences, HALF, width), BF16),
            V((2 * sentences, HALF, width), BF16),
            V((6, 128, width), BF16),
            V((6, 128, width), BF16),
            V((6, 128, width), BF16),
            V((3, 128, width), BF16),
            V((3, 128, width), BF16),
            V((3 * chunk, width), BF16),
            V((3 * chunk, width), BF16),
            V((3 * chunk, width), BF16),
            V((ff, width), F32),
            V((8, width), F32),
            V((64, width), F32),
            V((8, width), F32),
            V((8, width), F32),
            V((4, 8, width), F32),
            V((quads, 8, width), F32),
            dma((2 * sentences + 6,)),
            dma((3 * sentences,)),
            dma((3 * sentences,)),
            dma((3 * sentences,)),
            dma((3 * sentences,)),
            dma((4 * sentences,)),
            dma((4 * sentences,)),
            dma((6,)),
            dma((6,)),
            dma((3,)),
            dma((3,)),
            dma((copies,)),
            dma((copies,)),
            dma((3,)),
            dma((3,)),
            dma((quads,)),
            dma((quads,)),
            dma((1 + len(plan),)),
        ],
        compiler_params=pltpu.CompilerParams(
            collective_id=0, has_side_effects=True, vmem_limit_bytes=63 << 20
        ),
    )(
        lengths,
        tokens,
        w_query.T,
        w_key.T,
        w_value.T,
        w_attn_out,
        w_in,
        w_out,
        grad_out,
        b_query,
        b_value,
        b_in,
        b_attn_out,
        gain_one,
        bias_one,
        b_out,
        gain_two,
        bias_two,
    )


def unpack_kernel(
    qw,
    gw_hbm,
    lay_in,
    gtok_in,
    pool_in,
    vec_in,
    lay_hbm,
    pool_ref,
    gtok_hbm,
    wq_hbm,
    bq_ref,
    wk_hbm,
    wv_hbm,
    bv_ref,
    wo_hbm,
    battn_ref,
    gain1_ref,
    bias1_ref,
    win_hbm,
    bin_ref,
    wout_hbm,
    bout_ref,
    gain2_ref,
    bias2_ref,
    low_v,
    full_v,
    lay_v,
    gtok_v,
    in_sem,
    out_sem,
    side_sem,
):
    chunk = low_v.shape[0] // 3
    width = low_v.shape[1]
    pieces = [
        (c * chunk + r, c * width + r, dst.at[pl.ds(r, 192)])
        for c, dst in ((0, wout_hbm), (1, win_hbm))
        for r in range(0, width, 192)
    ]
    pieces += [
        (2 * chunk + k * qw, 2 * width + k * qw, dst)
        for k, dst in enumerate((wq_hbm, wk_hbm, wv_hbm, wo_hbm))
    ]
    ins = [
        pltpu.make_async_copy(
            gw_hbm.at[pl.ds(src, 192)], low_v.at[pl.ds(src, 192)], in_sem.at[k]
        )
        for k, (src, _, _) in enumerate(pieces)
    ]
    for copy in ins:
        copy.start()
    lay_copy = pltpu.make_async_copy(lay_in, lay_v, side_sem.at[0])
    gtok_copy = pltpu.make_async_copy(gtok_in, gtok_v, side_sem.at[1])
    pool_copy = pltpu.make_async_copy(pool_in, pool_ref, side_sem.at[2])
    lay_copy.start()
    gtok_copy.start()
    pool_copy.start()
    outs = []
    for k, (src, at, dst) in enumerate(pieces):
        ins[k].wait()
        full_v[pl.ds(at, 192), :] = low_v[pl.ds(src, 192), :].astype(F32)
        copy = pltpu.make_async_copy(full_v.at[pl.ds(at, 192)], dst, out_sem.at[k])
        copy.start()
        outs.append(copy)
    lay_copy.wait()
    outs.append(pltpu.make_async_copy(lay_v, lay_hbm, side_sem.at[3]))
    outs[-1].start()
    gtok_copy.wait()
    outs.append(pltpu.make_async_copy(gtok_v, gtok_hbm, side_sem.at[4]))
    outs[-1].start()
    bq_ref[...] = vec_in[0, pl.ds(0, qw)]
    bv_ref[...] = vec_in[0, pl.ds(256, qw)]
    for k, ref in enumerate(
        (bin_ref, battn_ref, gain1_ref, bias1_ref, bout_ref, gain2_ref, bias2_ref)
    ):
        ref[...] = vec_in[1 + k, :]
    pool_copy.wait()
    for copy in outs:
        copy.wait()


def unpack_call(qw, lay, pooled, gtok, gw, vec):
    width = gw.shape[1]
    anyspec = pl.BlockSpec(memory_space=pl.ANY)
    vmem = pl.BlockSpec(memory_space=pltpu.VMEM)
    like = lambda v: jax.ShapeDtypeStruct(v.shape, v.dtype)
    mat = lambda n: jax.ShapeDtypeStruct((n, width), F32)
    one = lambda n: jax.ShapeDtypeStruct((n,), F32)
    outs = pl.pallas_call(
        lambda *refs: unpack_kernel(qw, *refs),
        out_shape=(
            like(lay),
            like(pooled),
            like(gtok),
            mat(qw),
            one(qw),
            mat(qw),
            mat(qw),
            one(qw),
            mat(qw),
            one(width),
            one(width),
            one(width),
            mat(width),
            one(width),
            mat(width),
            one(width),
            one(width),
            one(width),
        ),
        in_specs=[anyspec] * 4 + [vmem],
        out_specs=tuple(anyspec if k in (0, 2, 3, 5, 6, 8, 12, 14) else vmem for k in range(18)),
        scratch_shapes=[
            pltpu.VMEM(gw.shape, BF16),
            pltpu.VMEM((3 * width, width), F32),
            pltpu.VMEM(lay.shape, BF16),
            pltpu.VMEM(gtok.shape, BF16),
            pltpu.SemaphoreType.DMA((12,)),
            pltpu.SemaphoreType.DMA((12,)),
            pltpu.SemaphoreType.DMA((5,)),
        ],
        compiler_params=pltpu.CompilerParams(vmem_limit_bytes=63 << 20),
    )(gw, lay, gtok, pooled, vec)
    return tuple(v.T if k in (3, 5, 6) else v for k, v in enumerate(outs))


def shards(*args):
    batch_size = lax.axis_size("batch")
    tp_size = lax.axis_size("tp")
    return unpack_call(args[6].shape[0], *layer_call(batch_size, tp_size, args))


def solution(mesh):
    placed = (
        P("batch", None),
        P(None, "tp"),
        P("tp"),
        P(None, "tp"),
        P(None, "tp"),
        P("tp"),
        P("tp", None),
        P(),
        P(),
        P(),
        P(None, "tp"),
        P("tp"),
        P("tp", None),
        P(),
        P(),
        P(),
        P("batch"),
        P("batch", None),
    )
    return jax.shard_map(
        shards,
        mesh=mesh,
        in_specs=placed,
        out_specs=(
            P(("batch", "tp"), None),
            P("batch", None),
            P(("batch", "tp"), None),
            P(None, "tp"),
            P("tp"),
            P(None, "tp"),
            P(None, "tp"),
            P("tp"),
            P("tp", None),
            P(),
            P(),
            P(),
            P(None, "tp"),
            P("tp"),
            P("tp", None),
            P(),
            P(),
            P(),
        ),
        check_vma=False,
    )
```

```python
import math

import jax
import jax.numpy as jnp
from jax import lax
from jax.experimental import pallas as pl
from jax.experimental.pallas import tpu as pltpu
from jax.sharding import PartitionSpec as P

HEAD = 64
SEQ_LEN = 512
HALF = SEQ_LEN // 2
EPSILON = 1e-06
BLOCK = 256
F32 = jnp.float32
BF16 = jnp.bfloat16
MESH = pl.DeviceIdType.MESH

NN = (((1,), (0,)), ((), ()))
NT = (((1,), (1,)), ((), ()))
TN = (((0,), (0,)), ((), ()))

FFN, HID = 0, 1
G_HID, G_FFN, G_RES, G_ATTN = 0, 1, 2, 3


UNITS = [
    (0, 256, [[0], [1, 2]], [[2], [1], [0]]),
    (256, 384, [[1], [0], [2]], [[2], [0], [1]]),
    (640, 128, [[0], [1], [2]], [[2], [1], [0]]),
    (768, 256, [[1], [0], [2]], [[2], [0], [1]]),
    (1024, 256, [[0], [1, 2]], [[2], [1], [0]]),
    (1280, 256, [[0], [1], [2]], [[2], [1], [0]]),
    (1536, 128, [[0], [1], [2]], [[2], [1], [0]]),
    (1664, 128, [[0], [1, 2]], [[2], [1], [0]]),
    (1792, 128, [[1], [0], [2]], [[2], [0], [1]]),
    (1920, 128, [[0], [1], [2]], [[2], [1], [0]]),
    (2048, 128, [[0], [1, 2]], [[1, 2], [0]]),
    (2176, 128, [[0], [1], [2]], [[1, 2], [0]]),
]
EARLY = {
    (0, 2): [(1, 0), (1, 1), (1, 2)],
    (0, 5): [(1, 3), (1, 4)],
    (1, 3): [(2, 2), (1, 5), (2, 0)],
    (1, 5): [(2, 1)],
    (2, 1): [(2, 4), (2, 3), (3, 2)],
    (2, 2): [(2, 5)],
    (2, 3): [(3, 0)],
    (2, 5): [(3, 1)],
}
LATE = [
    (3, 4),
    (4, 0),
    (3, 3),
    (1, 6),
    (4, 2),
    (1, 8),
    (1, 7),
    (3, 5),
    (1, 9),
    (4, 4),
    (4, 1),
    (1, 10),
    (2, 6),
    (5, 2),
    (4, 3),
    (1, 11),
    (107, 0),
    (2, 7),
    (2, 9),
    (4, 5),
    (5, 0),
    (109, 0),
    (2, 8),
    (2, 11),
    (2, 10),
    (108, 0),
    (3, 6),
    (3, 7),
    (3, 9),
    (5, 5),
    (5, 4),
    (3, 8),
    (3, 11),
    (5, 1),
    (4, 7),
    (3, 10),
    (110, 0),
    (6, 2),
    (4, 6),
    (4, 9),
    (5, 3),
    (4, 8),
    (111, 0),
    (4, 11),
    (6, 5),
    (6, 1),
    (5, 7),
    (5, 6),
    (5, 9),
    (4, 10),
    (5, 8),
    (5, 11),
    (6, 3),
    (6, 6),
    (6, 8),
    (6, 9),
]


def mm(left, right, dims):
    return lax.dot_general(left, right, dims, preferred_element_type=F32)


def fold8(block):
    rows, width = block.shape
    return jnp.sum(block.reshape(rows // 8, 8, width), axis=0)


def row_mean(block):
    return jnp.mean(block, axis=-1, keepdims=True)


def layer_kernel(
    batch_size,
    plan,
    early,
    late,
    len_ref,
    tok_hbm,
    wq_hbm,
    wk_hbm,
    wv_hbm,
    wo_hbm,
    win_hbm,
    wout_hbm,
    gout_hbm,
    bq_ref,
    bv_ref,
    bin_ref,
    battn_ref,
    gain1_ref,
    bias1_ref,
    bout_ref,
    gain2_ref,
    bias2_ref,
    lay_hbm,
    pool_ref,
    gtok_ref,
    gw_hbm,
    vec_ref,
    tok_v,
    wqkv_v,
    wo_v,
    wof_v,
    win_v,
    wout_v,
    gout_v,
    qkv_v,
    ctx_v,
    lse_v,
    hid_v,
    act_v,
    slope_v,
    norm1_v,
    inv1_v,
    res2_v,
    gffn_v,
    lay_v,
    gt_v,
    do_v,
    mask_v,
    part_v,
    cs_v,
    cr_v,
    ys_v,
    yr_v,
    all_v,
    tcr_v,
    tow_v,
    tys_v,
    tyr_v,
    gw_v,
    sum_v,
    rv_v,
    wacc_v,
    par_v,
    acc_v,
    vec_v,
    vc_v,
    vx_v,
    vq_v,
    in_sem,
    cs_sem,
    cr_sem,
    ys_sem,
    yr_sem,
    as_sem,
    ar_sem,
    hs_sem,
    hr_sem,
    tcs_sem,
    tcr_sem,
    tys_sem,
    tyr_sem,
    ws_sem,
    wr_sem,
    vs_sem,
    vr_sem,
    vqs_sem,
    vqr_sem,
    out_sem,
):
    rows_all, width = tok_v.shape
    sentences = rows_all // SEQ_LEN
    qw = wo_v.shape[0]
    heads = qw // HEAD
    quads = batch_size // 4
    bits = batch_size.bit_length() - 1

    gattn_v = gffn_v
    din_v = slope_v

    tp = lax.axis_index("tp")
    ba = lax.axis_index("batch")
    core = lax.rem(tp, 2)
    other = 1 - core
    chip = tp // 2
    quad = ba // 4
    bit = [lax.rem(ba // 2**k, 2) for k in range(bits)]
    core_id = {"tp": chip * 2 + other}
    y_id = {"tp": (1 - chip) * 2 + core}

    def flip_id(flips):
        at = ba
        for k in flips:
            at = at + (1 - 2 * bit[k]) * 2**k
        return {"batch": at}

    def flip_quad(flips):
        at = quad
        for k in flips:
            at = at + (1 - 2 * bit[k]) * 2 ** (k - 2)
        return at

    def subsets(group):
        return [
            [k for j, k in enumerate(group) if n >> j & 1] for n in range(1, 2 ** len(group))
        ]

    quad_flips = subsets(range(2, bits))
    batch_peers = []
    for _, _, down, up in plan:
        for group in down + up:
            batch_peers += [f for f in subsets(group) if f not in batch_peers]
    for f in [[0], [1]] + quad_flips:
        if f not in batch_peers:
            batch_peers.append(f)

    def remote(src, dst, send, recv, dev):
        return pltpu.make_async_remote_copy(
            src_ref=src,
            dst_ref=dst,
            send_sem=send,
            recv_sem=recv,
            device_id=dev,
            device_id_type=MESH,
        )

    def order(i):
        return lax.rem(2 * i, sentences)

    def tok_copy(i):
        rows = pl.ds(pl.multiple_of(order(i) * SEQ_LEN, SEQ_LEN), SEQ_LEN)
        return pltpu.make_async_copy(tok_hbm.at[rows], tok_v.at[rows], in_sem.at[i])

    w_copies = [
        pltpu.make_async_copy(src, dst, in_sem.at[sentences + k])
        for k, (src, dst) in enumerate(
            [
                (wq_hbm, wqkv_v.at[pl.ds(0, qw)]),
                (wk_hbm, wqkv_v.at[pl.ds(qw, qw)]),
                (wv_hbm, wqkv_v.at[pl.ds(2 * qw, qw)]),
                (wo_hbm, wo_v),
                (win_hbm, win_v),
                (wout_hbm, wout_v),
            ]
        )
    ]

    def gout_copy(i):
        src = pl.ds(pl.multiple_of(order(i) * SEQ_LEN + core * HALF, HALF), HALF)
        dst = pl.ds(pl.multiple_of(i * HALF, HALF), HALF)
        return pltpu.make_async_copy(
            gout_hbm.at[src], gout_v.at[dst], in_sem.at[sentences + 6 + i]
        )

    for k in range(3):
        w_copies[k].start()
    tok_copy(0).start()
    w_copies[3].start()
    for i in range(1, sentences):
        tok_copy(i).start()
    for k in range(4, 6):
        w_copies[k].start()
    for i in range(sentences):
        gout_copy(i).start()

    barrier = pltpu.get_barrier_semaphore()
    cross_id = {"tp": (1 - chip) * 2 + other}
    peers = [core_id, y_id, cross_id] + [flip_id(f) for f in batch_peers]
    for dev in peers:
        pl.semaphore_signal(barrier, inc=1, device_id=dev, device_id_type=MESH)

    acc_v[...] = jnp.zeros_like(acc_v)
    for k, ref in enumerate(
        (bin_ref, battn_ref, gain1_ref, bias1_ref, bout_ref, gain2_ref, bias2_ref)
    ):
        par_v[pl.ds(k, 1), :] = ref[...].reshape(1, width)
    bin_row, battn_row, gain1_row, bias1_row, bout_row, gain2_row, bias2_row = [
        par_v.at[pl.ds(k, 1)] for k in range(7)
    ]

    def core_copy(ph, i):
        k = ph * sentences + i
        slot = k
        return remote(cs_v.at[slot], cr_v.at[slot], cs_sem.at[k], cr_sem.at[k], core_id)

    def y_copy(ph, i):
        k = ph * sentences + i
        slot = k
        return remote(ys_v.at[slot], yr_v.at[slot], ys_sem.at[k], yr_sem.at[k], y_id)

    ctx_all = all_v
    own_heads = pl.ds(pl.multiple_of(tp * qw, 16), qw)
    far_heads = pl.ds(pl.multiple_of(((1 - chip) * 2 + core) * qw, 16), qw)

    def heads_copy(kind, i):
        half = core if kind == 0 else other
        at = pl.multiple_of(order(i) * SEQ_LEN + half * HALF, HALF)
        dev = (y_id, core_id, cross_id)[kind]
        return remote(
            ctx_v.at[:, pl.ds(at, HALF)],
            ctx_all.at[own_heads, pl.ds(pl.multiple_of(i * HALF, HALF), HALF)],
            hs_sem.at[kind * sentences + i],
            hr_sem.at[kind * sentences + i],
            dev,
        )

    def proj_copy(kind):
        k = 3 * sentences + kind
        src = wof_v.at[far_heads] if kind == 2 else wo_v
        dst = wof_v.at[far_heads if kind == 2 else own_heads]
        return remote(src, dst, hs_sem.at[k], hr_sem.at[k], y_id if kind == 0 else core_id)

    def gather_copy(which, ref, i):
        k = which * sentences + i
        rows = pl.ds(pl.multiple_of(order(i) * SEQ_LEN + core * HALF, HALF), HALF)
        return remote(ref.at[rows], ref.at[rows], as_sem.at[k], ar_sem.at[k], core_id)

    def chip_sum(ph, i):
        slot = ph * sentences + i
        core_copy(ph, i).wait_recv()

        @pl.loop(0, HALF // BLOCK)
        def _(j):
            rows = pl.ds(pl.multiple_of(j * BLOCK, BLOCK), BLOCK)
            ys_v[slot, rows, :] = (part_v[rows, :] + cr_v[slot, rows, :].astype(F32)).astype(BF16)

        y_copy(ph, i).start()

    def total_rows(ph, i, rows):
        slot = ph * sentences + i
        return ys_v[slot, rows, :].astype(F32) + yr_v[slot, rows, :].astype(F32)

    def add_acc(k, value):
        rows = pl.ds(8 * k, 8)
        acc_v[rows, :] = acc_v[rows, :] + fold8(value)

    def fill_mask(s):
        limit = len_ref[s]
        key = lax.broadcasted_iota(jnp.int32, mask_v.shape, 0)
        mask_v[...] = jnp.where(key < limit, 0.0, -1e30)

    def masked_scores(k_t, q_t):
        mask = mask_v[...]
        return mm(k_t, q_t, TN) + jnp.concatenate([mask] * (q_t.shape[1] // 128), axis=1)

    def column(row_ref):
        row = row_ref[...].reshape(1, qw)
        return jnp.transpose(jnp.broadcast_to(row, (8, qw)))[:, :1]

    for k in range(3):
        w_copies[k].wait()

    def project(i):
        s = order(i)
        cols = pl.ds(pl.multiple_of(s * SEQ_LEN, SEQ_LEN), SEQ_LEN)
        tok_copy(i).wait()
        x = tok_v[cols, :]
        qkv_v[pl.ds(0, qw), cols] = (
            mm(wqkv_v[pl.ds(0, qw), :], x, NT) + column(bq_ref)
        ).astype(BF16) * jnp.asarray(HEAD ** (-0.5), BF16)
        qkv_v[pl.ds(qw, qw), cols] = mm(wqkv_v[pl.ds(qw, qw), :], x, NT).astype(BF16)
        qkv_v[pl.ds(2 * qw, qw), cols] = (
            mm(wqkv_v[pl.ds(2 * qw, qw), :], x, NT) + column(bv_ref)
        ).astype(BF16)
        fill_mask(s)

    def attend(i, half):
        r0 = pl.multiple_of(order(i) * SEQ_LEN, SEQ_LEN)
        cols = pl.ds(r0, SEQ_LEN)
        qcols = pl.ds(pl.multiple_of(r0 + half * HALF, HALF), HALF)
        for h in range(heads):
            k_t = qkv_v[pl.ds(qw + h * HEAD, HEAD), cols]
            v_t = qkv_v[pl.ds(2 * qw + h * HEAD, HEAD), cols]
            scores = masked_scores(k_t, qkv_v[pl.ds(h * HEAD, HEAD), qcols])
            top = jnp.max(scores, axis=0, keepdims=True)
            expo = jnp.exp(scores - top)
            total = jnp.sum(expo, axis=0, keepdims=True)
            shares = (expo * (1.0 / total)).astype(BF16)
            ctx_v[pl.ds(h * HEAD, HEAD), qcols] = mm(v_t, shares, NN).astype(BF16)
            lse_v[pl.ds(h, 1), qcols] = top + jnp.log(total)

    project(0)
    w_copies[3].wait()
    attend(0, other)
    pl.semaphore_wait(barrier, len(peers))
    proj_copy(0).start()
    proj_copy(1).start()

    @pl.loop(0, sentences)
    def _(i):
        heads_copy(2, i).start()
        heads_copy(1, i).start()
        attend(i, core)
        heads_copy(0, i).start()
        own = pl.ds(pl.multiple_of(order(i) * SEQ_LEN + core * HALF, HALF), HALF)
        ctx_all[own_heads, pl.ds(pl.multiple_of(i * HALF, HALF), HALF)] = ctx_v[:, own]

        @pl.when(i + 1 < sentences)
        def _():
            project(i + 1)
            attend(i + 1, other)

    wof_v[own_heads, :] = wo_v[...]
    proj_copy(0).wait_recv()
    proj_copy(2).start()

    w_copies[4].wait()
    w_copies[5].wait()
    proj_copy(1).wait_recv()
    proj_copy(2).wait_recv()

    @pl.loop(0, sentences)
    def _(i):
        r0 = pl.multiple_of(order(i) * SEQ_LEN, SEQ_LEN)
        own0 = pl.multiple_of(r0 + core * HALF, HALF)
        oth0 = pl.multiple_of(r0 + other * HALF, HALF)
        for kind in range(3):
            heads_copy(kind, i).wait_recv()
        heard = ctx_all[:, pl.ds(pl.multiple_of(i * HALF, HALF), HALF)]
        part_v[...] = mm(heard, wof_v[...], TN)

        @pl.loop(0, HALF // BLOCK)
        def _(j):
            rows = pl.ds(pl.multiple_of(j * BLOCK, BLOCK), BLOCK)
            full = pl.ds(pl.multiple_of(own0 + j * BLOCK, BLOCK), BLOCK)
            kept = pl.ds(pl.multiple_of(i * HALF + j * BLOCK, BLOCK), BLOCK)
            resid = tok_v[full, :].astype(F32) + (part_v[rows, :] + battn_row[...])
            centred = resid - row_mean(resid)
            inv = lax.rsqrt(row_mean(centred * centred) + EPSILON)
            normed = centred * inv
            norm1_v[kept, :] = normed
            inv1_v[kept, :] = jnp.broadcast_to(inv, (BLOCK, 128))
            hid_v[full, :] = (normed * gain1_row[...] + bias1_row[...]).astype(BF16)

        gather_copy(G_HID, hid_v, i).start()

        def feed(base):
            full = pl.ds(base, HALF)
            pre = mm(hid_v[full, :], win_v[...], NN) + bin_row[...]
            cdf = 0.5 * (1.0 + lax.erf(pre * 0.5**0.5))
            act_v[full, :] = (pre * cdf).astype(BF16)
            slope_v[full, :] = (
                cdf + pre * (jnp.exp(-0.5 * pre * pre) * (2.0 * math.pi) ** (-0.5))
            ).astype(slope_v.dtype)
            return mm(act_v[pl.ds(base, HALF), :], wout_v[...], NN)

        part_v[...] = feed(own0)
        gather_copy(G_HID, hid_v, i).wait_recv()
        cs_v[i] = feed(oth0).astype(BF16)
        core_copy(FFN, i).start()
        chip_sum(FFN, i)

    chunk_rows = gw_v.shape[0] // 3

    def store_rows(j, t, block):
        gw_v[pl.ds(j * chunk_rows + t * 384, 384), :] = block.astype(BF16)

    stages = []
    used = 0
    for base, rows, down, up in plan:
        where, size, unit, spare = base, rows, [], base
        for group in down:
            unit_stage = {"sends": [], "waits": [], "adds": []}
            size = size // 2 ** len(group)

            def place(flips, group=group, where=where, size=size):
                at = where
                for j, k in enumerate(group):
                    side = 1 - bit[k] if k in flips else bit[k]
                    at = at + side * (size * 2 ** (len(group) - 1 - j))
                return at

            own = place([])
            for flips in subsets(group):
                src = gw_v.at[pl.ds(pl.multiple_of(place(flips), 16), size)]
                dst = rv_v.at[pl.ds(spare, size)]
                args = (src, dst, ws_sem.at[used], wr_sem.at[used], flip_id(flips))
                unit_stage["sends"].append(lambda args=args: remote(*args))
                unit_stage["waits"].append(lambda args=args: remote(*args))
                unit_stage["adds"].append((own, spare, size))
                spare += size
                used += 1
            unit.append(unit_stage)
            where = own
        final = (where, size)
        for group in up:
            unit_stage = {"sends": [], "waits": [], "adds": []}
            order_bits = [k for g in down for k in g]
            weight = {}
            width_of = rows
            for k in order_bits:
                width_of = width_of // 2
                weight[k] = width_of
            held = [k for g in up[: up.index(group)] for k in g]
            mine = base
            span = rows
            for k in order_bits:
                if k not in held:
                    mine = mine + bit[k] * weight[k]
                    span = span // 2
            for flips in subsets(group):
                theirs = mine
                for k in flips:
                    theirs = theirs + (1 - 2 * bit[k]) * weight[k]
                here = sum_v.at[pl.ds(pl.multiple_of(mine, 16), span)]
                there = sum_v.at[pl.ds(pl.multiple_of(theirs, 16), span)]
                sems = (ws_sem.at[used], wr_sem.at[used], flip_id(flips))
                unit_stage["sends"].append(lambda r=here, t=sems: remote(r, r, *t))
                unit_stage["waits"].append(lambda r=there, t=sems: remote(r, r, *t))
                used += 1
            unit.append(unit_stage)
        for unit_stage in unit:
            unit_stage["final"] = final
            unit_stage["last_down"] = len(down) - 1
        stages.append(unit)

    def start_stage(u, n):
        for copy in stages[u][n]["sends"]:
            copy().start()

    def out_copy(u):
        base, rows = plan[u][:2]
        at = pl.ds(base, rows)
        return pltpu.make_async_copy(sum_v.at[at], gw_hbm.at[at], out_sem.at[1 + u])

    def step(n, u):
        done = stages[u][n - 1]
        for copy in done["waits"]:
            copy().wait_recv()
        if done["adds"]:
            own, _, size = done["adds"][0]
            for r in range(0, size, 96):
                part = min(96, size - r)
                at = pl.ds(pl.multiple_of(own + r, 16), part)
                total = gw_v[at, :].astype(F32)
                for _, spare, _ in done["adds"]:
                    total = total + rv_v[pl.ds(spare + r, part), :].astype(F32)
                if n - 1 == done["last_down"]:
                    sum_v[at, :] = total.astype(BF16)
                else:
                    gw_v[at, :] = total.astype(BF16)
        if n < len(stages[u]):
            start_stage(u, n)
        else:
            out_copy(u).start()

    def start_chunk(c):
        for u, unit in enumerate(plan):
            if unit[0] // chunk_rows == c:
                start_stage(u, 0)

    wacc_v[...] = jnp.zeros_like(wacc_v)

    @pl.loop(0, sentences)
    def _(i):
        r0 = pl.multiple_of(order(i) * SEQ_LEN, SEQ_LEN)
        own0 = pl.multiple_of(r0 + core * HALF, HALF)
        oth0 = pl.multiple_of(r0 + other * HALF, HALF)
        gout_copy(i).wait()
        y_copy(FFN, i).wait_recv()

        @pl.loop(0, HALF // BLOCK)
        def _(j):
            rows = pl.ds(pl.multiple_of(j * BLOCK, BLOCK), BLOCK)
            full = pl.ds(pl.multiple_of(own0 + j * BLOCK, BLOCK), BLOCK)
            kept = pl.ds(pl.multiple_of(i * HALF + j * BLOCK, BLOCK), BLOCK)
            hidden = norm1_v[kept, :] * gain1_row[...] + bias1_row[...]
            resid = hidden + (total_rows(FFN, i, rows) + bout_row[...])
            centred = resid - row_mean(resid)
            inv = lax.rsqrt(row_mean(centred * centred) + EPSILON)
            normed = centred * inv
            lay_v[full, :] = (normed * gain2_row[...] + bias2_row[...]).astype(BF16)
            up = gout_v[kept, :].astype(F32)
            scaled = up * gain2_row[...]
            grad = inv * (scaled - row_mean(scaled) - normed * row_mean(scaled * normed))
            res2_v[kept, :] = grad
            gffn_v[full, :] = grad.astype(BF16)
            add_acc(4, grad)
            add_acc(5, up * normed)
            add_acc(6, up)

        gather_copy(G_FFN, gffn_v, i).start()
        gather_copy(G_RES, lay_v, i).start()

        def back(base):
            full = pl.ds(base, HALF)
            inner = (
                mm(gffn_v[full, :], wout_v[...], NT) * slope_v[full, :].astype(F32)
            ).astype(BF16)
            din_v[full, :] = inner
            add_acc(0, inner.astype(F32))
            return mm(din_v[pl.ds(base, HALF), :], win_v[...], NT)

        def grow(base):
            for t in range(width // 384):
                at = pl.ds(t * 384, 384)
                half = pl.ds(base, HALF)
                wacc_v[at, :] = wacc_v[at, :] + mm(act_v[half, at], gffn_v[half, :], TN)

        grow(own0)
        gather_copy(G_FFN, gffn_v, i).wait_recv()
        grow(oth0)

        @pl.when(i == sentences - 1)
        def _():
            for t in range(width // 384):
                store_rows(0, t, wacc_v[pl.ds(t * 384, 384), :])
            start_chunk(0)

        part_v[...] = back(own0)
        cs_v[sentences + i] = back(oth0).astype(BF16)
        core_copy(HID, i).start()
        chip_sum(HID, i)

    for t in range(width // 384):
        store_rows(1, t, mm(hid_v[:, pl.ds(t * 384, 384)], din_v[...], TN))
    start_chunk(1)

    steps = {}

    def run_step(n, u):
        if n in steps:
            steps[n]()
        else:
            step(n, u)

    def serve(i, point):
        for (turn, place), todo in early.items():
            if place == point:

                @pl.when(i == turn)
                def _():
                    for n, u in todo:
                        run_step(n, u)

    wacc_v[...] = jnp.zeros_like(wacc_v)

    @pl.loop(0, sentences)
    def _(i):
        s = order(i)
        r0 = pl.multiple_of(s * SEQ_LEN, SEQ_LEN)
        cols = pl.ds(r0, SEQ_LEN)
        own0 = pl.multiple_of(r0 + core * HALF, HALF)
        y_copy(HID, i).wait_recv()
        gather_copy(G_FFN, gffn_v, i).wait_send()

        @pl.loop(0, HALF // BLOCK)
        def _(j):
            rows = pl.ds(pl.multiple_of(j * BLOCK, BLOCK), BLOCK)
            full = pl.ds(pl.multiple_of(own0 + j * BLOCK, BLOCK), BLOCK)
            kept = pl.ds(pl.multiple_of(i * HALF + j * BLOCK, BLOCK), BLOCK)
            grad_hidden = res2_v[kept, :] + total_rows(HID, i, rows)
            normed = norm1_v[kept, :]
            inv = inv1_v[kept, :][:, :1]
            scaled = grad_hidden * gain1_row[...]
            grad = inv * (scaled - row_mean(scaled) - normed * row_mean(scaled * normed))
            gattn_v[full, :] = grad.astype(BF16)
            add_acc(1, grad)
            add_acc(2, grad_hidden * normed)
            add_acc(3, grad_hidden)

        gather_copy(G_ATTN, gattn_v, i).start()
        fill_mask(s)
        serve(i, 1)
        gather_copy(G_ATTN, gattn_v, i).wait_recv()
        do_v[...] = mm(wo_v[...], gattn_v[cols, :], NT).astype(BF16)
        for h in range(heads):
            k_t = qkv_v[pl.ds(qw + h * HEAD, HEAD), cols]
            v_t = qkv_v[pl.ds(2 * qw + h * HEAD, HEAD), cols]
            q_t = qkv_v[pl.ds(h * HEAD, HEAD), cols]
            d_t = do_v[pl.ds(h * HEAD, HEAD), :]
            c_t = ctx_v[pl.ds(h * HEAD, HEAD), cols]
            delta = jnp.sum(d_t.astype(F32) * c_t.astype(F32), axis=0, keepdims=True)
            shares = jnp.exp(masked_scores(k_t, q_t) - lse_v[pl.ds(h, 1), cols])
            grad_shares = mm(v_t, d_t, TN)
            grad_scores = (shares * (grad_shares - delta)).astype(BF16)
            gt_v[pl.ds(h * HEAD, HEAD), cols] = (
                mm(k_t, grad_scores, NN) * HEAD ** (-0.5)
            ).astype(BF16)
            gt_v[pl.ds(qw + h * HEAD, HEAD), cols] = mm(q_t, grad_scores, NT).astype(BF16)
            gt_v[pl.ds(2 * qw + h * HEAD, HEAD), cols] = mm(
                d_t, shares.astype(BF16), NT
            ).astype(BF16)
            serve(i, 2 + h)

        flat = pl.ds(0, 3 * qw)
        wacc_v[flat, :] = wacc_v[flat, :] + mm(gt_v[:, cols], tok_v[cols, :], NN)
        flat = pl.ds(3 * qw, qw)
        wacc_v[flat, :] = wacc_v[flat, :] + mm(ctx_v[:, cols], gattn_v[cols, :], NN)

        @pl.when(i == sentences - 1)
        def _():
            for t in range(width // 384):
                store_rows(2, t, wacc_v[pl.ds(t * 384, 384), :])
            start_chunk(2)

        @pl.loop(0, 2)
        def _(j2):
            hcols = pl.ds(pl.multiple_of(r0 + j2 * 256, 256), 256)
            half_part = mm(gt_v[:, hcols], wqkv_v[...], TN).astype(BF16)
            for j1 in range(2):
                blk = s * (SEQ_LEN // 128) + j2 * 2 + j1
                quarter = blk // 3
                place = lax.rem(blk, 3)
                slot = (quarter // 2) * 3 + place
                part = half_part[j1 * 128 : j1 * 128 + 128]

                @pl.when(lax.rem(quarter, 2) == core)
                def _():
                    tow_v[slot] = part

                @pl.when(lax.rem(quarter, 2) == other)
                def _():
                    all_v[pl.ds(pl.multiple_of(slot * 128, 128), 128), :] = part
                    remote(
                        all_v.at[pl.ds(pl.multiple_of(slot * 128, 128), 128)],
                        tcr_v.at[slot],
                        tcs_sem.at[slot],
                        tcr_sem.at[slot],
                        core_id,
                    ).start()

        serve(i, 5)

    ones = jnp.ones((8, rows_all), BF16)
    vec_v[...] = jnp.zeros_like(vec_v)
    vec_v[pl.ds(0, 1), pl.ds(0, qw)] = mm(ones, gt_v[pl.ds(0, qw), :], NT)[:1]
    vec_v[pl.ds(0, 1), pl.ds(256, qw)] = mm(ones, gt_v[pl.ds(2 * qw, qw), :], NT)[:1]
    for k in range(7):
        vec_v[pl.ds(1 + k, 1), :] = jnp.sum(acc_v[pl.ds(8 * k, 8), :], axis=0, keepdims=True)
    v_core = remote(vec_v, vc_v, vs_sem.at[0], vr_sem.at[0], core_id)
    v_core.start()

    v_core.wait()
    row_id = lax.broadcasted_iota(jnp.int32, vec_v.shape, 0)
    vx_v[0] = vec_v[...] + jnp.where(row_id >= 2, vc_v[...], 0.0)
    v_x = remote(vx_v.at[0], vx_v.at[1], vs_sem.at[1], vr_sem.at[1], flip_id([0]))
    v_x.start()

    def t_core(slot):
        return remote(
            all_v.at[pl.ds(slot * 128, 128)],
            tcr_v.at[slot],
            tcs_sem.at[slot],
            tcr_sem.at[slot],
            core_id,
        )

    def t_y(k):
        return remote(tys_v.at[k], tyr_v.at[k], tys_sem.at[k], tyr_sem.at[k], y_id)

    for k in range(3):
        slot = (1 - chip) * 3 + k
        t_core(slot).wait_recv()
        tys_v[k] = (tow_v[slot].astype(F32) + tcr_v[slot].astype(F32)).astype(BF16)
        t_y(k).start()

    v_p = remote(vx_v.at[2], vx_v.at[3], vs_sem.at[2], vr_sem.at[2], flip_id([1]))

    def vector_step1():
        v_x.wait()
        vx_v[2] = vx_v[0] + vx_v[1]
        v_p.start()

    def vq_copy(k):
        return remote(
            vq_v.at[quad], vq_v.at[quad], vqs_sem.at[k], vqr_sem.at[quad], flip_id(quad_flips[k])
        )

    def vq_from(k):
        q = flip_quad(quad_flips[k])
        return remote(vq_v.at[q], vq_v.at[q], vqs_sem.at[k], vqr_sem.at[q], flip_id(quad_flips[k]))

    def vector_step2():
        v_p.wait()
        vq_v[quad] = vx_v[2] + vx_v[3]
        for k in range(quads - 1):
            vq_copy(k).start()

    def vector_step3():
        for k in range(quads - 1):
            vq_from(k).wait_recv()
        total = vq_v[0]
        for q in range(1, quads):
            total = total + vq_v[q]
        vec_ref[...] = total

    quarter_rows = rows_all // 4
    lay_out = pltpu.make_async_copy(
        lay_v.at[pl.ds(pl.multiple_of(tp * quarter_rows, quarter_rows), quarter_rows)],
        lay_hbm,
        out_sem.at[0],
    )

    def layer_step():
        for i in range(sentences):
            gather_copy(G_RES, lay_v, i).wait_recv()
        lay_out.start()
        for s in range(sentences):
            key = lax.broadcasted_iota(jnp.int32, (8, SEQ_LEN), 1)
            member = jnp.where(key < len_ref[s], 1.0, 0.0).astype(BF16)
            total = mm(member, lay_v[pl.ds(s * SEQ_LEN, SEQ_LEN), :], NN)[:1]
            average = total / len_ref[s].astype(F32)
            at = 0
            for cut in (width, width * 2 // 3, width // 3, width // 6, width // 12):
                prefix = average[:, :cut]
                centred = prefix - row_mean(prefix)
                pool_ref[pl.ds(s, 1), pl.ds(at, cut)] = centred * lax.rsqrt(
                    row_mean(centred * centred) + EPSILON
                )
                at += cut

    def input_step():
        for k in range(3):
            slot = chip * 3 + k
            t_core(slot).wait_recv()
            mine = (tow_v[slot].astype(F32) + tcr_v[slot].astype(F32)).astype(BF16)
            t_y(k).wait_recv()
            at = pl.ds(pl.multiple_of(tp * quarter_rows + k * 128, 128), 128)
            gtok_ref[pl.ds(k * 128, 128), :] = (
                gattn_v[at, :].astype(F32) + (mine.astype(F32) + tyr_v[k].astype(F32))
            ).astype(BF16)

    steps.update(
        {107: vector_step1, 108: vector_step2, 109: input_step, 110: vector_step3, 111: layer_step}
    )
    for n, u in late:
        run_step(n, u)

    for u in range(len(plan)):
        out_copy(u).wait()
    lay_out.wait()
    for kind in range(3):
        proj_copy(kind).wait_send()
        for i in range(sentences):
            heads_copy(kind, i).wait_send()
    for i in range(sentences):
        core_copy(FFN, i).wait_send()
        y_copy(FFN, i).wait_send()
        core_copy(HID, i).wait_send()
        y_copy(HID, i).wait_send()
        gather_copy(G_HID, hid_v, i).wait_send()
        gather_copy(G_RES, lay_v, i).wait_send()
        gather_copy(G_ATTN, gattn_v, i).wait_send()
    for slot in range(6):
        t_core(slot).wait_send()
    for k in range(3):
        t_y(k).wait_send()
    for u in range(len(plan)):
        for n in range(len(stages[u])):
            for copy in stages[u][n]["sends"]:
                copy().wait_send()
    for k in range(quads - 1):
        vq_copy(k).wait_send()


def layer_call(batch_size, tp_size, args):
    (
        tokens,
        w_query,
        b_query,
        w_key,
        w_value,
        b_value,
        w_attn_out,
        b_attn_out,
        gain_one,
        bias_one,
        w_in,
        b_in,
        w_out,
        b_out,
        gain_two,
        bias_two,
        lengths,
        grad_out,
    ) = args
    rows, width = tokens.shape
    sentences = lengths.shape[0]
    qw = w_attn_out.shape[0]
    ff = w_in.shape[1]
    quads = batch_size // 4
    piece = -(-width // batch_size)
    piece = -(-piece // 16) * 16
    chunk = piece * batch_size
    if batch_size == 8:
        plan, early, late = UNITS, EARLY, LATE
    else:
        high = list(range(2, batch_size.bit_length() - 1))
        plan = [(c * chunk, chunk, [[0], [1], high], [high, [1], [0]]) for c in range(3)]
        early = {}
        late = [(n, u) for n in range(1, 7) for u in range(3)]
        late = late[:3] + [(n, 0) for n in range(107, 112)] + late[3:]
    copies = sum(2 ** len(g) - 1 for unit in plan for g in unit[2] + unit[3])
    quarter = rows // tp_size
    anyspec = pl.BlockSpec(memory_space=pl.ANY)
    vmem = pl.BlockSpec(memory_space=pltpu.VMEM)
    smem = pl.BlockSpec(memory_space=pltpu.SMEM)
    dma = pltpu.SemaphoreType.DMA
    V = pltpu.VMEM
    kept = rows // 2
    return pl.pallas_call(
        lambda *refs: layer_kernel(batch_size, plan, early, late, *refs),
        out_shape=(
            jax.ShapeDtypeStruct((quarter, width), BF16),
            jax.ShapeDtypeStruct((sentences, width * 9 // 4), F32),
            jax.ShapeDtypeStruct((quarter, width), BF16),
            jax.ShapeDtypeStruct((3 * chunk, width), BF16),
            jax.ShapeDtypeStruct((8, width), F32),
        ),
        in_specs=[smem] + [anyspec] * 8 + [vmem] * 9,
        out_specs=(anyspec, vmem, vmem, anyspec, vmem),
        scratch_shapes=[
            V((rows, width), BF16),
            V((3 * qw, width), BF16),
            V((qw, width), BF16),
            V((width, width), BF16),
            V((width, ff), BF16),
            V((ff, width), BF16),
            V((kept, width), BF16),
            V((3 * qw, rows), BF16),
            V((qw, rows), BF16),
            V((8, rows), F32),
            V((rows, width), BF16),
            V((rows, ff), BF16),
            V((rows, ff), BF16),
            V((kept, width), F32),
            V((kept, 128), F32),
            V((kept, width), F32),
            V((rows, width), BF16),
            V((rows, width), BF16),
            V((3 * qw, rows), BF16),
            V((qw, SEQ_LEN), BF16),
            V((SEQ_LEN, 128), F32),
            V((HALF, width), F32),
            V((2 * sentences, HALF, width), BF16),
            V((2 * sentences, HALF, width), BF16),
            V((2 * sentences, HALF, width), BF16),
            V((2 * sentences, HALF, width), BF16),
            V((width, width), BF16),
            V((6, 128, width), BF16),
            V((6, 128, width), BF16),
            V((3, 128, width), BF16),
            V((3, 128, width), BF16),
            V((3 * chunk, width), BF16),
            V((3 * chunk, width), BF16),
            V((3 * chunk, width), BF16),
            V((ff, width), F32),
            V((8, width), F32),
            V((64, width), F32),
            V((8, width), F32),
            V((8, width), F32),
            V((4, 8, width), F32),
            V((quads, 8, width), F32),
            dma((2 * sentences + 6,)),
            dma((2 * sentences,)),
            dma((2 * sentences,)),
            dma((2 * sentences,)),
            dma((2 * sentences,)),
            dma((4 * sentences,)),
            dma((4 * sentences,)),
            dma((3 * sentences + 3,)),
            dma((3 * sentences + 3,)),
            dma((6,)),
            dma((6,)),
            dma((3,)),
            dma((3,)),
            dma((copies,)),
            dma((copies,)),
            dma((3,)),
            dma((3,)),
            dma((quads,)),
            dma((quads,)),
            dma((1 + len(plan),)),
        ],
        compiler_params=pltpu.CompilerParams(
            collective_id=0, has_side_effects=True, vmem_limit_bytes=63 << 20
        ),
    )(
        lengths,
        tokens,
        w_query.T,
        w_key.T,
        w_value.T,
        w_attn_out,
        w_in,
        w_out,
        grad_out,
        b_query,
        b_value,
        b_in,
        b_attn_out,
        gain_one,
        bias_one,
        b_out,
        gain_two,
        bias_two,
    )


def unpack_kernel(
    qw,
    gw_hbm,
    lay_in,
    gtok_in,
    pool_in,
    vec_in,
    lay_hbm,
    pool_ref,
    gtok_hbm,
    wq_hbm,
    bq_ref,
    wk_hbm,
    wv_hbm,
    bv_ref,
    wo_hbm,
    battn_ref,
    gain1_ref,
    bias1_ref,
    win_hbm,
    bin_ref,
    wout_hbm,
    bout_ref,
    gain2_ref,
    bias2_ref,
    low_v,
    full_v,
    lay_v,
    gtok_v,
    in_sem,
    out_sem,
    side_sem,
):
    chunk = low_v.shape[0] // 3
    width = low_v.shape[1]
    pieces = [
        (c * chunk + r, c * width + r, dst.at[pl.ds(r, 192)])
        for c, dst in ((0, wout_hbm), (1, win_hbm))
        for r in range(0, width, 192)
    ]
    pieces += [
        (2 * chunk + k * qw, 2 * width + k * qw, dst)
        for k, dst in enumerate((wq_hbm, wk_hbm, wv_hbm, wo_hbm))
    ]
    ins = [
        pltpu.make_async_copy(
            gw_hbm.at[pl.ds(src, 192)], low_v.at[pl.ds(src, 192)], in_sem.at[k]
        )
        for k, (src, _, _) in enumerate(pieces)
    ]
    for copy in ins:
        copy.start()
    lay_copy = pltpu.make_async_copy(lay_in, lay_v, side_sem.at[0])
    gtok_copy = pltpu.make_async_copy(gtok_in, gtok_v, side_sem.at[1])
    pool_copy = pltpu.make_async_copy(pool_in, pool_ref, side_sem.at[2])
    lay_copy.start()
    gtok_copy.start()
    pool_copy.start()
    outs = []
    for k, (src, at, dst) in enumerate(pieces):
        ins[k].wait()
        full_v[pl.ds(at, 192), :] = low_v[pl.ds(src, 192), :].astype(F32)
        copy = pltpu.make_async_copy(full_v.at[pl.ds(at, 192)], dst, out_sem.at[k])
        copy.start()
        outs.append(copy)
    lay_copy.wait()
    outs.append(pltpu.make_async_copy(lay_v, lay_hbm, side_sem.at[3]))
    outs[-1].start()
    gtok_copy.wait()
    outs.append(pltpu.make_async_copy(gtok_v, gtok_hbm, side_sem.at[4]))
    outs[-1].start()
    bq_ref[...] = vec_in[0, pl.ds(0, qw)]
    bv_ref[...] = vec_in[0, pl.ds(256, qw)]
    for k, ref in enumerate(
        (bin_ref, battn_ref, gain1_ref, bias1_ref, bout_ref, gain2_ref, bias2_ref)
    ):
        ref[...] = vec_in[1 + k, :]
    pool_copy.wait()
    for copy in outs:
        copy.wait()


def unpack_call(qw, lay, pooled, gtok, gw, vec):
    width = gw.shape[1]
    anyspec = pl.BlockSpec(memory_space=pl.ANY)
    vmem = pl.BlockSpec(memory_space=pltpu.VMEM)
    like = lambda v: jax.ShapeDtypeStruct(v.shape, v.dtype)
    mat = lambda n: jax.ShapeDtypeStruct((n, width), F32)
    one = lambda n: jax.ShapeDtypeStruct((n,), F32)
    outs = pl.pallas_call(
        lambda *refs: unpack_kernel(qw, *refs),
        out_shape=(
            like(lay),
            like(pooled),
            like(gtok),
            mat(qw),
            one(qw),
            mat(qw),
            mat(qw),
            one(qw),
            mat(qw),
            one(width),
            one(width),
            one(width),
            mat(width),
            one(width),
            mat(width),
            one(width),
            one(width),
            one(width),
        ),
        in_specs=[anyspec] * 4 + [vmem],
        out_specs=tuple(anyspec if k in (0, 2, 3, 5, 6, 8, 12, 14) else vmem for k in range(18)),
        scratch_shapes=[
            pltpu.VMEM(gw.shape, BF16),
            pltpu.VMEM((3 * width, width), F32),
            pltpu.VMEM(lay.shape, BF16),
            pltpu.VMEM(gtok.shape, BF16),
            pltpu.SemaphoreType.DMA((12,)),
            pltpu.SemaphoreType.DMA((12,)),
            pltpu.SemaphoreType.DMA((5,)),
        ],
        compiler_params=pltpu.CompilerParams(vmem_limit_bytes=63 << 20),
    )(gw, lay, gtok, pooled, vec)
    return tuple(v.T if k in (3, 5, 6) else v for k, v in enumerate(outs))


def shards(*args):
    batch_size = lax.axis_size("batch")
    tp_size = lax.axis_size("tp")
    return unpack_call(args[6].shape[0], *layer_call(batch_size, tp_size, args))


def solution(mesh):
    placed = (
        P("batch", None),
        P(None, "tp"),
        P("tp"),
        P(None, "tp"),
        P(None, "tp"),
        P("tp"),
        P("tp", None),
        P(),
        P(),
        P(),
        P(None, "tp"),
        P("tp"),
        P("tp", None),
        P(),
        P(),
        P(),
        P("batch"),
        P("batch", None),
    )
    return jax.shard_map(
        shards,
        mesh=mesh,
        in_specs=placed,
        out_specs=(
            P(("batch", "tp"), None),
            P("batch", None),
            P(("batch", "tp"), None),
            P(None, "tp"),
            P("tp"),
            P(None, "tp"),
            P(None, "tp"),
            P("tp"),
            P("tp", None),
            P(),
            P(),
            P(),
            P(None, "tp"),
            P("tp"),
            P("tp", None),
            P(),
            P(),
            P(),
        ),
        check_vma=False,
    )
```

```python
import math

import jax
import jax.numpy as jnp
from jax import lax
from jax.experimental import pallas as pl
from jax.experimental.pallas import tpu as pltpu
from jax.sharding import PartitionSpec as P

HEAD = 64
SEQ_LEN = 512
HALF = SEQ_LEN // 2
EPSILON = 1e-06
BLOCK = 256
F32 = jnp.float32
BF16 = jnp.bfloat16
MESH = pl.DeviceIdType.MESH

NN = (((1,), (0,)), ((), ()))
NT = (((1,), (1,)), ((), ()))
TN = (((0,), (0,)), ((), ()))

FFN, HID = 0, 1
G_HID, G_FFN, G_RES, G_ATTN = 0, 1, 2, 3


UNITS = [
    (0, 256, [[0], [1, 2]], [[2], [1], [0]]),
    (256, 384, [[1], [0], [2]], [[2], [0], [1]]),
    (640, 128, [[0], [1], [2]], [[2], [1], [0]]),
    (768, 256, [[1], [0], [2]], [[2], [0], [1]]),
    (1024, 256, [[0], [1, 2]], [[2], [1], [0]]),
    (1280, 256, [[0], [1], [2]], [[2], [1], [0]]),
    (1536, 128, [[0], [1], [2]], [[2], [1], [0]]),
    (1664, 128, [[0], [1, 2]], [[2], [1], [0]]),
    (1792, 128, [[1], [0], [2]], [[2], [0], [1]]),
    (1920, 128, [[0], [1], [2]], [[2], [1], [0]]),
    (2048, 128, [[0], [1, 2]], [[1, 2], [0]]),
    (2176, 128, [[0], [1], [2]], [[1, 2], [0]]),
]
EARLY = {
    (0, 2): [(1, 0), (1, 1), (1, 2)],
    (0, 5): [(1, 3), (1, 4)],
    (1, 3): [(2, 2), (1, 5), (2, 0)],
    (1, 5): [(2, 1)],
    (2, 1): [(2, 4), (2, 3), (3, 2)],
    (2, 2): [(2, 5)],
    (2, 3): [(3, 0)],
    (2, 5): [(3, 1)],
}
LATE = [
    (3, 4),
    (4, 0),
    (3, 3),
    (1, 6),
    (4, 2),
    (1, 8),
    (1, 7),
    (3, 5),
    (1, 9),
    (4, 4),
    (4, 1),
    (1, 10),
    (2, 6),
    (5, 2),
    (4, 3),
    (1, 11),
    (107, 0),
    (2, 7),
    (2, 9),
    (4, 5),
    (5, 0),
    (109, 0),
    (2, 8),
    (2, 11),
    (2, 10),
    (108, 0),
    (3, 6),
    (3, 7),
    (3, 9),
    (5, 5),
    (5, 4),
    (3, 8),
    (3, 11),
    (5, 1),
    (4, 7),
    (3, 10),
    (110, 0),
    (6, 2),
    (4, 6),
    (4, 9),
    (5, 3),
    (4, 8),
    (111, 0),
    (4, 11),
    (6, 5),
    (6, 1),
    (5, 7),
    (5, 6),
    (5, 9),
    (4, 10),
    (5, 8),
    (5, 11),
    (6, 3),
    (6, 6),
    (6, 8),
    (6, 9),
]


def mm(left, right, dims):
    return lax.dot_general(left, right, dims, preferred_element_type=F32)


def fold8(block):
    rows, width = block.shape
    return jnp.sum(block.reshape(rows // 8, 8, width), axis=0)


def row_mean(block):
    return jnp.mean(block, axis=-1, keepdims=True)


def layer_kernel(
    batch_size,
    plan,
    early,
    late,
    len_hbm,
    tok_hbm,
    wq_hbm,
    wk_hbm,
    wv_hbm,
    wo_hbm,
    win_hbm,
    wout_hbm,
    gout_hbm,
    bq_hbm,
    bv_hbm,
    bin_hbm,
    battn_hbm,
    gain1_hbm,
    bias1_hbm,
    bout_hbm,
    gain2_hbm,
    bias2_hbm,
    lay_hbm,
    pool_hbm,
    gtok_hbm,
    gw_hbm,
    vec_hbm,
    len_ref,
    bq_ref,
    bv_ref,
    bin_ref,
    battn_ref,
    gain1_ref,
    bias1_ref,
    bout_ref,
    gain2_ref,
    bias2_ref,
    pool_ref,
    gtok_ref,
    vec_ref,
    small_sem,
    tok_v,
    wqkv_v,
    wo_v,
    wof_v,
    win_v,
    wout_v,
    gout_v,
    qkv_v,
    ctx_v,
    lse_v,
    hid_v,
    act_v,
    slope_v,
    norm1_v,
    inv1_v,
    res2_v,
    gffn_v,
    lay_v,
    gt_v,
    do_v,
    mask_v,
    part_v,
    cs_v,
    cr_v,
    ys_v,
    yr_v,
    all_v,
    tcr_v,
    tow_v,
    tys_v,
    tyr_v,
    gw_v,
    sum_v,
    rv_v,
    wacc_v,
    par_v,
    acc_v,
    vec_v,
    vc_v,
    vx_v,
    vq_v,
    in_sem,
    cs_sem,
    cr_sem,
    ys_sem,
    yr_sem,
    as_sem,
    ar_sem,
    hs_sem,
    hr_sem,
    tcs_sem,
    tcr_sem,
    tys_sem,
    tyr_sem,
    ws_sem,
    wr_sem,
    vs_sem,
    vr_sem,
    vqs_sem,
    vqr_sem,
    out_sem,
):
    rows_all, width = tok_v.shape
    sentences = rows_all // SEQ_LEN
    qw = wo_v.shape[0]
    heads = qw // HEAD
    quads = batch_size // 4
    bits = batch_size.bit_length() - 1

    gattn_v = gffn_v
    din_v = slope_v

    tp = lax.axis_index("tp")
    ba = lax.axis_index("batch")
    core = lax.rem(tp, 2)
    other = 1 - core
    chip = tp // 2
    quad = ba // 4
    bit = [lax.rem(ba // 2**k, 2) for k in range(bits)]
    core_id = {"tp": chip * 2 + other}
    y_id = {"tp": (1 - chip) * 2 + core}

    def flip_id(flips):
        at = ba
        for k in flips:
            at = at + (1 - 2 * bit[k]) * 2**k
        return {"batch": at}

    def flip_quad(flips):
        at = quad
        for k in flips:
            at = at + (1 - 2 * bit[k]) * 2 ** (k - 2)
        return at

    def subsets(group):
        return [
            [k for j, k in enumerate(group) if n >> j & 1] for n in range(1, 2 ** len(group))
        ]

    quad_flips = subsets(range(2, bits))
    batch_peers = []
    for _, _, down, up in plan:
        for group in down + up:
            batch_peers += [f for f in subsets(group) if f not in batch_peers]
    for f in [[0], [1]] + quad_flips:
        if f not in batch_peers:
            batch_peers.append(f)

    def remote(src, dst, send, recv, dev):
        return pltpu.make_async_remote_copy(
            src_ref=src,
            dst_ref=dst,
            send_sem=send,
            recv_sem=recv,
            device_id=dev,
            device_id_type=MESH,
        )

    def order(i):
        return lax.rem(2 * i, sentences)

    def tok_copy(i):
        rows = pl.ds(pl.multiple_of(order(i) * SEQ_LEN, SEQ_LEN), SEQ_LEN)
        return pltpu.make_async_copy(tok_hbm.at[rows], tok_v.at[rows], in_sem.at[i])

    w_copies = [
        pltpu.make_async_copy(src, dst, in_sem.at[sentences + k])
        for k, (src, dst) in enumerate(
            [
                (wq_hbm, wqkv_v.at[pl.ds(0, qw)]),
                (wk_hbm, wqkv_v.at[pl.ds(qw, qw)]),
                (wv_hbm, wqkv_v.at[pl.ds(2 * qw, qw)]),
                (wo_hbm, wo_v),
                (win_hbm, win_v),
                (wout_hbm, wout_v),
            ]
        )
    ]

    small_copies = [
        pltpu.make_async_copy(src, dst, small_sem.at[k])
        for k, (src, dst) in enumerate(
            [
                (len_hbm, len_ref),
                (bq_hbm, bq_ref),
                (bv_hbm, bv_ref),
                (bin_hbm, bin_ref),
                (battn_hbm, battn_ref),
                (gain1_hbm, gain1_ref),
                (bias1_hbm, bias1_ref),
                (bout_hbm, bout_ref),
                (gain2_hbm, gain2_ref),
                (bias2_hbm, bias2_ref),
            ]
        )
    ]

    def gout_copy(i):
        src = pl.ds(pl.multiple_of(order(i) * SEQ_LEN + core * HALF, HALF), HALF)
        dst = pl.ds(pl.multiple_of(i * HALF, HALF), HALF)
        return pltpu.make_async_copy(
            gout_hbm.at[src], gout_v.at[dst], in_sem.at[sentences + 6 + i]
        )

    barrier = pltpu.get_barrier_semaphore()
    cross_id = {"tp": (1 - chip) * 2 + other}
    peers = [core_id, y_id, cross_id] + [flip_id(f) for f in batch_peers]
    for dev in peers:
        pl.semaphore_signal(barrier, inc=1, device_id=dev, device_id_type=MESH)

    w_copies[3].start()
    for k in range(3):
        w_copies[k].start()
    for k in range(3):
        small_copies[k].start()
    tok_copy(0).start()
    for i in range(1, sentences):
        tok_copy(i).start()
    for k in range(4, 6):
        w_copies[k].start()
    for k in range(3, 10):
        small_copies[k].start()
    for i in range(sentences):
        gout_copy(i).start()

    acc_v[...] = jnp.zeros_like(acc_v)
    bin_row, battn_row, gain1_row, bias1_row, bout_row, gain2_row, bias2_row = [
        par_v.at[pl.ds(k, 1)] for k in range(7)
    ]

    def core_copy(ph, i):
        k = ph * sentences + i
        slot = k
        return remote(cs_v.at[slot], cr_v.at[slot], cs_sem.at[k], cr_sem.at[k], core_id)

    def y_copy(ph, i):
        k = ph * sentences + i
        slot = k
        return remote(ys_v.at[slot], yr_v.at[slot], ys_sem.at[k], yr_sem.at[k], y_id)

    ctx_all = all_v
    own_heads = pl.ds(pl.multiple_of(tp * qw, 16), qw)
    far_heads = pl.ds(pl.multiple_of(((1 - chip) * 2 + core) * qw, 16), qw)

    def heads_copy(kind, i):
        half = core if kind == 0 else other
        at = pl.multiple_of(order(i) * SEQ_LEN + half * HALF, HALF)
        dev = (y_id, core_id, cross_id)[kind]
        return remote(
            ctx_v.at[:, pl.ds(at, HALF)],
            ctx_all.at[own_heads, pl.ds(pl.multiple_of(i * HALF, HALF), HALF)],
            hs_sem.at[kind * sentences + i],
            hr_sem.at[kind * sentences + i],
            dev,
        )

    def proj_copy(kind):
        k = 3 * sentences + kind
        src = wof_v.at[far_heads] if kind == 2 else wo_v
        dst = wof_v.at[far_heads if kind == 2 else own_heads]
        return remote(src, dst, hs_sem.at[k], hr_sem.at[k], y_id if kind == 0 else core_id)

    def gather_copy(which, ref, i):
        k = which * sentences + i
        rows = pl.ds(pl.multiple_of(order(i) * SEQ_LEN + core * HALF, HALF), HALF)
        return remote(ref.at[rows], ref.at[rows], as_sem.at[k], ar_sem.at[k], core_id)

    def chip_sum(ph, i):
        slot = ph * sentences + i
        core_copy(ph, i).wait_recv()

        @pl.loop(0, HALF // BLOCK)
        def _(j):
            rows = pl.ds(pl.multiple_of(j * BLOCK, BLOCK), BLOCK)
            ys_v[slot, rows, :] = (part_v[rows, :] + cr_v[slot, rows, :].astype(F32)).astype(BF16)

        y_copy(ph, i).start()

    def total_rows(ph, i, rows):
        slot = ph * sentences + i
        return ys_v[slot, rows, :].astype(F32) + yr_v[slot, rows, :].astype(F32)

    def add_acc(k, value):
        rows = pl.ds(8 * k, 8)
        acc_v[rows, :] = acc_v[rows, :] + fold8(value)

    def fill_mask(s):
        limit = len_ref[s]
        key = lax.broadcasted_iota(jnp.int32, mask_v.shape, 0)
        mask_v[...] = jnp.where(key < limit, 0.0, -1e30)

    def masked_scores(k_t, q_t):
        mask = mask_v[...]
        return mm(k_t, q_t, TN) + jnp.concatenate([mask] * (q_t.shape[1] // 128), axis=1)

    def column(row_ref):
        row = row_ref[...].reshape(1, qw)
        return jnp.transpose(jnp.broadcast_to(row, (8, qw)))[:, :1]

    w_copies[3].wait()
    pl.semaphore_wait(barrier, len(peers))
    proj_copy(0).start()
    proj_copy(1).start()
    for k in range(3):
        w_copies[k].wait()

    def project(i):
        s = order(i)
        cols = pl.ds(pl.multiple_of(s * SEQ_LEN, SEQ_LEN), SEQ_LEN)
        tok_copy(i).wait()
        x = tok_v[cols, :]
        qkv_v[pl.ds(0, qw), cols] = (
            mm(wqkv_v[pl.ds(0, qw), :], x, NT) + column(bq_ref)
        ).astype(BF16) * jnp.asarray(HEAD ** (-0.5), BF16)
        qkv_v[pl.ds(qw, qw), cols] = mm(wqkv_v[pl.ds(qw, qw), :], x, NT).astype(BF16)
        qkv_v[pl.ds(2 * qw, qw), cols] = (
            mm(wqkv_v[pl.ds(2 * qw, qw), :], x, NT) + column(bv_ref)
        ).astype(BF16)
        fill_mask(s)

    def attend(i, half):
        r0 = pl.multiple_of(order(i) * SEQ_LEN, SEQ_LEN)
        cols = pl.ds(r0, SEQ_LEN)
        qcols = pl.ds(pl.multiple_of(r0 + half * HALF, HALF), HALF)
        for h in range(heads):
            k_t = qkv_v[pl.ds(qw + h * HEAD, HEAD), cols]
            v_t = qkv_v[pl.ds(2 * qw + h * HEAD, HEAD), cols]
            scores = masked_scores(k_t, qkv_v[pl.ds(h * HEAD, HEAD), qcols])
            top = jnp.max(scores, axis=0, keepdims=True)
            expo = jnp.exp(scores - top)
            total = jnp.sum(expo, axis=0, keepdims=True)
            shares = (expo * (1.0 / total)).astype(BF16)
            ctx_v[pl.ds(h * HEAD, HEAD), qcols] = mm(v_t, shares, NN).astype(BF16)
            lse_v[pl.ds(h, 1), qcols] = top + jnp.log(total)

    for k in range(3):
        small_copies[k].wait()
    project(0)
    attend(0, other)

    @pl.loop(0, sentences)
    def _(i):
        heads_copy(2, i).start()
        heads_copy(1, i).start()
        attend(i, core)
        heads_copy(0, i).start()
        own = pl.ds(pl.multiple_of(order(i) * SEQ_LEN + core * HALF, HALF), HALF)
        ctx_all[own_heads, pl.ds(pl.multiple_of(i * HALF, HALF), HALF)] = ctx_v[:, own]

        @pl.when(i + 1 < sentences)
        def _():
            project(i + 1)
            attend(i + 1, other)

    wof_v[own_heads, :] = wo_v[...]
    proj_copy(0).wait_recv()
    proj_copy(2).start()

    w_copies[4].wait()
    w_copies[5].wait()
    for k in range(3, 10):
        small_copies[k].wait()
    for k, ref in enumerate(
        (bin_ref, battn_ref, gain1_ref, bias1_ref, bout_ref, gain2_ref, bias2_ref)
    ):
        par_v[pl.ds(k, 1), :] = ref[...].reshape(1, width)
    proj_copy(1).wait_recv()
    proj_copy(2).wait_recv()

    @pl.loop(0, sentences)
    def _(i):
        r0 = pl.multiple_of(order(i) * SEQ_LEN, SEQ_LEN)
        own0 = pl.multiple_of(r0 + core * HALF, HALF)
        oth0 = pl.multiple_of(r0 + other * HALF, HALF)
        for kind in range(3):
            heads_copy(kind, i).wait_recv()
        heard = ctx_all[:, pl.ds(pl.multiple_of(i * HALF, HALF), HALF)]
        part_v[...] = mm(heard, wof_v[...], TN)

        @pl.loop(0, HALF // BLOCK)
        def _(j):
            rows = pl.ds(pl.multiple_of(j * BLOCK, BLOCK), BLOCK)
            full = pl.ds(pl.multiple_of(own0 + j * BLOCK, BLOCK), BLOCK)
            kept = pl.ds(pl.multiple_of(i * HALF + j * BLOCK, BLOCK), BLOCK)
            resid = tok_v[full, :].astype(F32) + (part_v[rows, :] + battn_row[...])
            centred = resid - row_mean(resid)
            inv = lax.rsqrt(row_mean(centred * centred) + EPSILON)
            normed = centred * inv
            norm1_v[kept, :] = normed
            inv1_v[kept, :] = jnp.broadcast_to(inv, (BLOCK, 128))
            hid_v[full, :] = (normed * gain1_row[...] + bias1_row[...]).astype(BF16)

        gather_copy(G_HID, hid_v, i).start()

        def feed(base):
            full = pl.ds(base, HALF)
            pre = mm(hid_v[full, :], win_v[...], NN) + bin_row[...]
            cdf = 0.5 * (1.0 + lax.erf(pre * 0.5**0.5))
            act_v[full, :] = (pre * cdf).astype(BF16)
            slope_v[full, :] = (
                cdf + pre * (jnp.exp(-0.5 * pre * pre) * (2.0 * math.pi) ** (-0.5))
            ).astype(slope_v.dtype)
            return mm(act_v[pl.ds(base, HALF), :], wout_v[...], NN)

        part_v[...] = feed(own0)
        gather_copy(G_HID, hid_v, i).wait_recv()
        cs_v[i] = feed(oth0).astype(BF16)
        core_copy(FFN, i).start()
        chip_sum(FFN, i)

    chunk_rows = gw_v.shape[0] // 3

    def store_rows(j, t, block):
        gw_v[pl.ds(j * chunk_rows + t * 384, 384), :] = block.astype(BF16)

    stages = []
    used = 0
    for base, rows, down, up in plan:
        where, size, unit, spare = base, rows, [], base
        for group in down:
            unit_stage = {"sends": [], "waits": [], "adds": []}
            size = size // 2 ** len(group)

            def place(flips, group=group, where=where, size=size):
                at = where
                for j, k in enumerate(group):
                    side = 1 - bit[k] if k in flips else bit[k]
                    at = at + side * (size * 2 ** (len(group) - 1 - j))
                return at

            own = place([])
            for flips in subsets(group):
                src = gw_v.at[pl.ds(pl.multiple_of(place(flips), 16), size)]
                dst = rv_v.at[pl.ds(spare, size)]
                args = (src, dst, ws_sem.at[used], wr_sem.at[used], flip_id(flips))
                unit_stage["sends"].append(lambda args=args: remote(*args))
                unit_stage["waits"].append(lambda args=args: remote(*args))
                unit_stage["adds"].append((own, spare, size))
                spare += size
                used += 1
            unit.append(unit_stage)
            where = own
        final = (where, size)
        for group in up:
            unit_stage = {"sends": [], "waits": [], "adds": []}
            order_bits = [k for g in down for k in g]
            weight = {}
            width_of = rows
            for k in order_bits:
                width_of = width_of // 2
                weight[k] = width_of
            held = [k for g in up[: up.index(group)] for k in g]
            mine = base
            span = rows
            for k in order_bits:
                if k not in held:
                    mine = mine + bit[k] * weight[k]
                    span = span // 2
            for flips in subsets(group):
                theirs = mine
                for k in flips:
                    theirs = theirs + (1 - 2 * bit[k]) * weight[k]
                here = sum_v.at[pl.ds(pl.multiple_of(mine, 16), span)]
                there = sum_v.at[pl.ds(pl.multiple_of(theirs, 16), span)]
                sems = (ws_sem.at[used], wr_sem.at[used], flip_id(flips))
                unit_stage["sends"].append(lambda r=here, t=sems: remote(r, r, *t))
                unit_stage["waits"].append(lambda r=there, t=sems: remote(r, r, *t))
                used += 1
            unit.append(unit_stage)
        for unit_stage in unit:
            unit_stage["final"] = final
            unit_stage["last_down"] = len(down) - 1
        stages.append(unit)

    def start_stage(u, n):
        for copy in stages[u][n]["sends"]:
            copy().start()

    def out_copy(u):
        base, rows = plan[u][:2]
        at = pl.ds(base, rows)
        return pltpu.make_async_copy(sum_v.at[at], gw_hbm.at[at], out_sem.at[1 + u])

    def step(n, u):
        done = stages[u][n - 1]
        for copy in done["waits"]:
            copy().wait_recv()
        if done["adds"]:
            own, _, size = done["adds"][0]
            for r in range(0, size, 96):
                part = min(96, size - r)
                at = pl.ds(pl.multiple_of(own + r, 16), part)
                total = gw_v[at, :].astype(F32)
                for _, spare, _ in done["adds"]:
                    total = total + rv_v[pl.ds(spare + r, part), :].astype(F32)
                if n - 1 == done["last_down"]:
                    sum_v[at, :] = total.astype(BF16)
                else:
                    gw_v[at, :] = total.astype(BF16)
        if n < len(stages[u]):
            start_stage(u, n)
        else:
            out_copy(u).start()

    def start_rows(c, t):
        for u, (base, rows, _, _) in enumerate(plan):
            last_tile = min((base % chunk_rows + rows - 1) // 384, width // 384 - 1)
            if base // chunk_rows == c and last_tile == t:
                start_stage(u, 0)

    wacc_v[...] = jnp.zeros_like(wacc_v)

    @pl.loop(0, sentences)
    def _(i):
        r0 = pl.multiple_of(order(i) * SEQ_LEN, SEQ_LEN)
        own0 = pl.multiple_of(r0 + core * HALF, HALF)
        oth0 = pl.multiple_of(r0 + other * HALF, HALF)
        gout_copy(i).wait()
        y_copy(FFN, i).wait_recv()

        @pl.loop(0, HALF // BLOCK)
        def _(j):
            rows = pl.ds(pl.multiple_of(j * BLOCK, BLOCK), BLOCK)
            full = pl.ds(pl.multiple_of(own0 + j * BLOCK, BLOCK), BLOCK)
            kept = pl.ds(pl.multiple_of(i * HALF + j * BLOCK, BLOCK), BLOCK)
            hidden = norm1_v[kept, :] * gain1_row[...] + bias1_row[...]
            resid = hidden + (total_rows(FFN, i, rows) + bout_row[...])
            centred = resid - row_mean(resid)
            inv = lax.rsqrt(row_mean(centred * centred) + EPSILON)
            normed = centred * inv
            lay_v[full, :] = (normed * gain2_row[...] + bias2_row[...]).astype(BF16)
            up = gout_v[kept, :].astype(F32)
            scaled = up * gain2_row[...]
            grad = inv * (scaled - row_mean(scaled) - normed * row_mean(scaled * normed))
            res2_v[kept, :] = grad
            gffn_v[full, :] = grad.astype(BF16)
            add_acc(4, grad)
            add_acc(5, up * normed)
            add_acc(6, up)

        gather_copy(G_FFN, gffn_v, i).start()
        gather_copy(G_RES, lay_v, i).start()

        def back(base):
            full = pl.ds(base, HALF)
            inner = (
                mm(gffn_v[full, :], wout_v[...], NT) * slope_v[full, :].astype(F32)
            ).astype(BF16)
            din_v[full, :] = inner
            add_acc(0, inner.astype(F32))
            return mm(din_v[pl.ds(base, HALF), :], win_v[...], NT)

        def grow(base, t):
            at = pl.ds(t * 384, 384)
            half = pl.ds(base, HALF)
            wacc_v[at, :] = wacc_v[at, :] + mm(act_v[half, at], gffn_v[half, :], TN)

        for t in range(width // 384):
            grow(own0, t)
        gather_copy(G_FFN, gffn_v, i).wait_recv()
        for t in range(width // 384):
            grow(oth0, t)

            @pl.when(i == sentences - 1)
            def _():
                store_rows(0, t, wacc_v[pl.ds(t * 384, 384), :])
                start_rows(0, t)

        part_v[...] = back(own0)
        cs_v[sentences + i] = back(oth0).astype(BF16)
        core_copy(HID, i).start()
        chip_sum(HID, i)

    for t in range(width // 384):
        store_rows(1, t, mm(hid_v[:, pl.ds(t * 384, 384)], din_v[...], TN))
        start_rows(1, t)

    steps = {}

    def run_step(n, u):
        if n in steps:
            steps[n]()
        else:
            step(n, u)

    def serve(i, point):
        for (turn, place), todo in early.items():
            if place == point:

                @pl.when(i == turn)
                def _():
                    for n, u in todo:
                        run_step(n, u)

    wacc_v[...] = jnp.zeros_like(wacc_v)

    @pl.loop(0, sentences)
    def _(i):
        s = order(i)
        r0 = pl.multiple_of(s * SEQ_LEN, SEQ_LEN)
        cols = pl.ds(r0, SEQ_LEN)
        own0 = pl.multiple_of(r0 + core * HALF, HALF)
        y_copy(HID, i).wait_recv()
        gather_copy(G_FFN, gffn_v, i).wait_send()

        @pl.loop(0, HALF // BLOCK)
        def _(j):
            rows = pl.ds(pl.multiple_of(j * BLOCK, BLOCK), BLOCK)
            full = pl.ds(pl.multiple_of(own0 + j * BLOCK, BLOCK), BLOCK)
            kept = pl.ds(pl.multiple_of(i * HALF + j * BLOCK, BLOCK), BLOCK)
            grad_hidden = res2_v[kept, :] + total_rows(HID, i, rows)
            normed = norm1_v[kept, :]
            inv = inv1_v[kept, :][:, :1]
            scaled = grad_hidden * gain1_row[...]
            grad = inv * (scaled - row_mean(scaled) - normed * row_mean(scaled * normed))
            gattn_v[full, :] = grad.astype(BF16)
            add_acc(1, grad)
            add_acc(2, grad_hidden * normed)
            add_acc(3, grad_hidden)

        gather_copy(G_ATTN, gattn_v, i).start()
        fill_mask(s)
        serve(i, 1)
        gather_copy(G_ATTN, gattn_v, i).wait_recv()
        do_v[...] = mm(wo_v[...], gattn_v[cols, :], NT).astype(BF16)
        for h in range(heads):
            k_t = qkv_v[pl.ds(qw + h * HEAD, HEAD), cols]
            v_t = qkv_v[pl.ds(2 * qw + h * HEAD, HEAD), cols]
            q_t = qkv_v[pl.ds(h * HEAD, HEAD), cols]
            d_t = do_v[pl.ds(h * HEAD, HEAD), :]
            c_t = ctx_v[pl.ds(h * HEAD, HEAD), cols]
            delta = jnp.sum(d_t.astype(F32) * c_t.astype(F32), axis=0, keepdims=True)
            shares = jnp.exp(masked_scores(k_t, q_t) - lse_v[pl.ds(h, 1), cols])
            grad_shares = mm(v_t, d_t, TN)
            grad_scores = (shares * (grad_shares - delta)).astype(BF16)
            gt_v[pl.ds(h * HEAD, HEAD), cols] = (
                mm(k_t, grad_scores, NN) * HEAD ** (-0.5)
            ).astype(BF16)
            gt_v[pl.ds(qw + h * HEAD, HEAD), cols] = mm(q_t, grad_scores, NT).astype(BF16)
            gt_v[pl.ds(2 * qw + h * HEAD, HEAD), cols] = mm(
                d_t, shares.astype(BF16), NT
            ).astype(BF16)
            serve(i, 2 + h)

        flat = pl.ds(0, 3 * qw)
        wacc_v[flat, :] = wacc_v[flat, :] + mm(gt_v[:, cols], tok_v[cols, :], NN)
        flat = pl.ds(3 * qw, qw)
        wacc_v[flat, :] = wacc_v[flat, :] + mm(ctx_v[:, cols], gattn_v[cols, :], NN)

        @pl.when(i == sentences - 1)
        def _():
            for t in range(width // 384):
                store_rows(2, t, wacc_v[pl.ds(t * 384, 384), :])
                start_rows(2, t)

        @pl.loop(0, 2)
        def _(j2):
            hcols = pl.ds(pl.multiple_of(r0 + j2 * 256, 256), 256)
            half_part = mm(gt_v[:, hcols], wqkv_v[...], TN).astype(BF16)
            for j1 in range(2):
                blk = s * (SEQ_LEN // 128) + j2 * 2 + j1
                quarter = blk // 3
                place = lax.rem(blk, 3)
                slot = (quarter // 2) * 3 + place
                part = half_part[j1 * 128 : j1 * 128 + 128]

                @pl.when(lax.rem(quarter, 2) == core)
                def _():
                    tow_v[slot] = part

                @pl.when(lax.rem(quarter, 2) == other)
                def _():
                    all_v[pl.ds(pl.multiple_of(slot * 128, 128), 128), :] = part
                    remote(
                        all_v.at[pl.ds(pl.multiple_of(slot * 128, 128), 128)],
                        tcr_v.at[slot],
                        tcs_sem.at[slot],
                        tcr_sem.at[slot],
                        core_id,
                    ).start()

        serve(i, 5)

    ones = jnp.ones((8, rows_all), BF16)
    vec_v[...] = jnp.zeros_like(vec_v)
    vec_v[pl.ds(0, 1), pl.ds(0, qw)] = mm(ones, gt_v[pl.ds(0, qw), :], NT)[:1]
    vec_v[pl.ds(0, 1), pl.ds(256, qw)] = mm(ones, gt_v[pl.ds(2 * qw, qw), :], NT)[:1]
    for k in range(7):
        vec_v[pl.ds(1 + k, 1), :] = jnp.sum(acc_v[pl.ds(8 * k, 8), :], axis=0, keepdims=True)
    v_core = remote(vec_v, vc_v, vs_sem.at[0], vr_sem.at[0], core_id)
    v_core.start()

    v_core.wait()
    row_id = lax.broadcasted_iota(jnp.int32, vec_v.shape, 0)
    vx_v[0] = vec_v[...] + jnp.where(row_id >= 2, vc_v[...], 0.0)
    v_x = remote(vx_v.at[0], vx_v.at[1], vs_sem.at[1], vr_sem.at[1], flip_id([0]))
    v_x.start()

    def t_core(slot):
        return remote(
            all_v.at[pl.ds(slot * 128, 128)],
            tcr_v.at[slot],
            tcs_sem.at[slot],
            tcr_sem.at[slot],
            core_id,
        )

    def t_y(k):
        return remote(tys_v.at[k], tyr_v.at[k], tys_sem.at[k], tyr_sem.at[k], y_id)

    for k in range(3):
        slot = (1 - chip) * 3 + k
        t_core(slot).wait_recv()
        tys_v[k] = (tow_v[slot].astype(F32) + tcr_v[slot].astype(F32)).astype(BF16)
        t_y(k).start()

    v_p = remote(vx_v.at[2], vx_v.at[3], vs_sem.at[2], vr_sem.at[2], flip_id([1]))

    small_outs = [
        pltpu.make_async_copy(src, dst, small_sem.at[k])
        for k, (src, dst) in enumerate(
            [(vec_ref, vec_hbm), (pool_ref, pool_hbm), (gtok_ref, gtok_hbm)]
        )
    ]

    def vector_step1():
        v_x.wait()
        vx_v[2] = vx_v[0] + vx_v[1]
        v_p.start()

    def vq_copy(k):
        return remote(
            vq_v.at[quad], vq_v.at[quad], vqs_sem.at[k], vqr_sem.at[quad], flip_id(quad_flips[k])
        )

    def vq_from(k):
        q = flip_quad(quad_flips[k])
        return remote(vq_v.at[q], vq_v.at[q], vqs_sem.at[k], vqr_sem.at[q], flip_id(quad_flips[k]))

    def vector_step2():
        v_p.wait()
        vq_v[quad] = vx_v[2] + vx_v[3]
        for k in range(quads - 1):
            vq_copy(k).start()

    def vector_step3():
        for k in range(quads - 1):
            vq_from(k).wait_recv()
        total = vq_v[0]
        for q in range(1, quads):
            total = total + vq_v[q]
        vec_ref[...] = total
        small_outs[0].start()

    quarter_rows = rows_all // 4
    lay_out = pltpu.make_async_copy(
        lay_v.at[pl.ds(pl.multiple_of(tp * quarter_rows, quarter_rows), quarter_rows)],
        lay_hbm,
        out_sem.at[0],
    )

    def layer_step():
        for i in range(sentences):
            gather_copy(G_RES, lay_v, i).wait_recv()
        lay_out.start()
        for s in range(sentences):
            key = lax.broadcasted_iota(jnp.int32, (8, SEQ_LEN), 1)
            member = jnp.where(key < len_ref[s], 1.0, 0.0).astype(BF16)
            total = mm(member, lay_v[pl.ds(s * SEQ_LEN, SEQ_LEN), :], NN)[:1]
            average = total / len_ref[s].astype(F32)
            at = 0
            for cut in (width, width * 2 // 3, width // 3, width // 6, width // 12):
                prefix = average[:, :cut]
                centred = prefix - row_mean(prefix)
                pool_ref[pl.ds(s, 1), pl.ds(at, cut)] = centred * lax.rsqrt(
                    row_mean(centred * centred) + EPSILON
                )
                at += cut
        small_outs[1].start()

    def input_step():
        for k in range(3):
            slot = chip * 3 + k
            t_core(slot).wait_recv()
            mine = (tow_v[slot].astype(F32) + tcr_v[slot].astype(F32)).astype(BF16)
            t_y(k).wait_recv()
            at = pl.ds(pl.multiple_of(tp * quarter_rows + k * 128, 128), 128)
            gtok_ref[pl.ds(k * 128, 128), :] = (
                gattn_v[at, :].astype(F32) + (mine.astype(F32) + tyr_v[k].astype(F32))
            ).astype(BF16)
        small_outs[2].start()

    steps.update(
        {107: vector_step1, 108: vector_step2, 109: input_step, 110: vector_step3, 111: layer_step}
    )
    for n, u in late:
        run_step(n, u)

    for u in range(len(plan)):
        out_copy(u).wait()
    lay_out.wait()
    for copy in small_outs:
        copy.wait()
    for kind in range(3):
        proj_copy(kind).wait_send()
        for i in range(sentences):
            heads_copy(kind, i).wait_send()
    for i in range(sentences):
        core_copy(FFN, i).wait_send()
        y_copy(FFN, i).wait_send()
        core_copy(HID, i).wait_send()
        y_copy(HID, i).wait_send()
        gather_copy(G_HID, hid_v, i).wait_send()
        gather_copy(G_RES, lay_v, i).wait_send()
        gather_copy(G_ATTN, gattn_v, i).wait_send()
    for slot in range(6):
        t_core(slot).wait_send()
    for k in range(3):
        t_y(k).wait_send()
    for u in range(len(plan)):
        for n in range(len(stages[u])):
            for copy in stages[u][n]["sends"]:
                copy().wait_send()
    for k in range(quads - 1):
        vq_copy(k).wait_send()


def layer_call(batch_size, tp_size, args):
    (
        tokens,
        w_query,
        b_query,
        w_key,
        w_value,
        b_value,
        w_attn_out,
        b_attn_out,
        gain_one,
        bias_one,
        w_in,
        b_in,
        w_out,
        b_out,
        gain_two,
        bias_two,
        lengths,
        grad_out,
    ) = args
    rows, width = tokens.shape
    sentences = lengths.shape[0]
    qw = w_attn_out.shape[0]
    ff = w_in.shape[1]
    quads = batch_size // 4
    piece = -(-width // batch_size)
    piece = -(-piece // 16) * 16
    chunk = piece * batch_size
    if batch_size == 8:
        plan, early, late = UNITS, EARLY, LATE
    else:
        high = list(range(2, batch_size.bit_length() - 1))
        plan = [(c * chunk, chunk, [[0], [1], high], [high, [1], [0]]) for c in range(3)]
        early = {}
        late = [(n, u) for n in range(1, 7) for u in range(3)]
        late = late[:3] + [(n, 0) for n in range(107, 112)] + late[3:]
    copies = sum(2 ** len(g) - 1 for unit in plan for g in unit[2] + unit[3])
    quarter = rows // tp_size
    anyspec = pl.BlockSpec(memory_space=pl.ANY)
    dma = pltpu.SemaphoreType.DMA
    V = pltpu.VMEM
    kept = rows // 2
    return pl.pallas_call(
        lambda *refs: layer_kernel(batch_size, plan, early, late, *refs),
        out_shape=(
            jax.ShapeDtypeStruct((quarter, width), BF16),
            jax.ShapeDtypeStruct((sentences, width * 9 // 4), F32),
            jax.ShapeDtypeStruct((quarter, width), BF16),
            jax.ShapeDtypeStruct((3 * chunk, width), BF16),
            jax.ShapeDtypeStruct((8, width), F32),
        ),
        in_specs=[anyspec] * 18,
        out_specs=(anyspec,) * 5,
        scratch_shapes=[
            pltpu.SMEM((sentences,), jnp.int32),
            V((qw,), F32),
            V((qw,), F32),
            V((ff,), F32),
            V((width,), F32),
            V((width,), F32),
            V((width,), F32),
            V((width,), F32),
            V((width,), F32),
            V((width,), F32),
            V((sentences, width * 9 // 4), F32),
            V((quarter, width), BF16),
            V((8, width), F32),
            dma((10,)),
            V((rows, width), BF16),
            V((3 * qw, width), BF16),
            V((qw, width), BF16),
            V((width, width), BF16),
            V((width, ff), BF16),
            V((ff, width), BF16),
            V((kept, width), BF16),
            V((3 * qw, rows), BF16),
            V((qw, rows), BF16),
            V((8, rows), F32),
            V((rows, width), BF16),
            V((rows, ff), BF16),
            V((rows, ff), BF16),
            V((kept, width), F32),
            V((kept, 128), F32),
            V((kept, width), F32),
            V((rows, width), BF16),
            V((rows, width), BF16),
            V((3 * qw, rows), BF16),
            V((qw, SEQ_LEN), BF16),
            V((SEQ_LEN, 128), F32),
            V((HALF, width), F32),
            V((2 * sentences, HALF, width), BF16),
            V((2 * sentences, HALF, width), BF16),
            V((2 * sentences, HALF, width), BF16),
            V((2 * sentences, HALF, width), BF16),
            V((width, width), BF16),
            V((6, 128, width), BF16),
            V((6, 128, width), BF16),
            V((3, 128, width), BF16),
            V((3, 128, width), BF16),
            V((3 * chunk, width), BF16),
            V((3 * chunk, width), BF16),
            V((3 * chunk, width), BF16),
            V((ff, width), F32),
            V((8, width), F32),
            V((64, width), F32),
            V((8, width), F32),
            V((8, width), F32),
            V((4, 8, width), F32),
            V((quads, 8, width), F32),
            dma((2 * sentences + 6,)),
            dma((2 * sentences,)),
            dma((2 * sentences,)),
            dma((2 * sentences,)),
            dma((2 * sentences,)),
            dma((4 * sentences,)),
            dma((4 * sentences,)),
            dma((3 * sentences + 3,)),
            dma((3 * sentences + 3,)),
            dma((6,)),
            dma((6,)),
            dma((3,)),
            dma((3,)),
            dma((copies,)),
            dma((copies,)),
            dma((3,)),
            dma((3,)),
            dma((quads,)),
            dma((quads,)),
            dma((1 + len(plan),)),
        ],
        compiler_params=pltpu.CompilerParams(
            collective_id=0, has_side_effects=True, vmem_limit_bytes=63 << 20
        ),
    )(
        lengths,
        tokens,
        w_query.T,
        w_key.T,
        w_value.T,
        w_attn_out,
        w_in,
        w_out,
        grad_out,
        b_query,
        b_value,
        b_in,
        b_attn_out,
        gain_one,
        bias_one,
        b_out,
        gain_two,
        bias_two,
    )


def unpack_kernel(
    qw,
    gw_hbm,
    lay_in,
    gtok_in,
    pool_in,
    vec_in,
    lay_hbm,
    pool_hbm,
    gtok_hbm,
    wq_hbm,
    bq_ref,
    wk_hbm,
    wv_hbm,
    bv_ref,
    wo_hbm,
    battn_ref,
    gain1_ref,
    bias1_ref,
    win_hbm,
    bin_ref,
    wout_hbm,
    bout_ref,
    gain2_ref,
    bias2_ref,
    low_v,
    full_v,
    lay_v,
    gtok_v,
    pool_v,
    vec_v,
    bq_v,
    bv_v,
    v0,
    v1,
    v2,
    v3,
    v4,
    v5,
    v6,
    in_sem,
    out_sem,
    side_sem,
    vec_sem,
):
    chunk = low_v.shape[0] // 3
    width = low_v.shape[1]
    pieces = [
        (c * chunk + r, c * width + r, dst.at[pl.ds(r, 192)])
        for c, dst in ((0, wout_hbm), (1, win_hbm))
        for r in range(0, width, 192)
    ]
    pieces += [
        (2 * chunk + k * qw, 2 * width + k * qw, dst)
        for k, dst in enumerate((wq_hbm, wk_hbm, wv_hbm, wo_hbm))
    ]
    ins = [
        pltpu.make_async_copy(
            gw_hbm.at[pl.ds(src, 192)], low_v.at[pl.ds(src, 192)], in_sem.at[k]
        )
        for k, (src, _, _) in enumerate(pieces)
    ]
    for copy in ins:
        copy.start()
    lay_copy = pltpu.make_async_copy(lay_in, lay_v, side_sem.at[0])
    gtok_copy = pltpu.make_async_copy(gtok_in, gtok_v, side_sem.at[1])
    pool_copy = pltpu.make_async_copy(pool_in, pool_v, side_sem.at[2])
    vec_copy = pltpu.make_async_copy(vec_in, vec_v, side_sem.at[5])
    lay_copy.start()
    gtok_copy.start()
    pool_copy.start()
    vec_copy.start()
    outs = []
    for k, (src, at, dst) in enumerate(pieces):
        ins[k].wait()
        full_v[pl.ds(at, 192), :] = low_v[pl.ds(src, 192), :].astype(F32)
        copy = pltpu.make_async_copy(full_v.at[pl.ds(at, 192)], dst, out_sem.at[k])
        copy.start()
        outs.append(copy)
    lay_copy.wait()
    outs.append(pltpu.make_async_copy(lay_v, lay_hbm, side_sem.at[3]))
    outs[-1].start()
    gtok_copy.wait()
    outs.append(pltpu.make_async_copy(gtok_v, gtok_hbm, side_sem.at[4]))
    outs[-1].start()
    vec_copy.wait()
    short = (bq_v, bv_v, v0, v1, v2, v3, v4, v5, v6)
    bq_v[...] = vec_v[0, pl.ds(0, qw)]
    bv_v[...] = vec_v[0, pl.ds(256, qw)]
    for k in range(7):
        short[2 + k][...] = vec_v[1 + k, :]
    dsts = (bq_ref, bv_ref, bin_ref, battn_ref, gain1_ref, bias1_ref, bout_ref, gain2_ref, bias2_ref)
    for k, dst in enumerate(dsts):
        outs.append(pltpu.make_async_copy(short[k], dst, vec_sem.at[k]))
        outs[-1].start()
    pool_copy.wait()
    outs.append(pltpu.make_async_copy(pool_v, pool_hbm, vec_sem.at[9]))
    outs[-1].start()
    for copy in outs:
        copy.wait()


def unpack_call(qw, lay, pooled, gtok, gw, vec):
    width = gw.shape[1]
    anyspec = pl.BlockSpec(memory_space=pl.ANY)
    like = lambda v: jax.ShapeDtypeStruct(v.shape, v.dtype)
    mat = lambda n: jax.ShapeDtypeStruct((n, width), F32)
    one = lambda n: jax.ShapeDtypeStruct((n,), F32)
    outs = pl.pallas_call(
        lambda *refs: unpack_kernel(qw, *refs),
        out_shape=(
            like(lay),
            like(pooled),
            like(gtok),
            mat(qw),
            one(qw),
            mat(qw),
            mat(qw),
            one(qw),
            mat(qw),
            one(width),
            one(width),
            one(width),
            mat(width),
            one(width),
            mat(width),
            one(width),
            one(width),
            one(width),
        ),
        in_specs=[anyspec] * 5,
        out_specs=(anyspec,) * 18,
        scratch_shapes=[
            pltpu.VMEM(gw.shape, BF16),
            pltpu.VMEM((3 * width, width), F32),
            pltpu.VMEM(lay.shape, BF16),
            pltpu.VMEM(gtok.shape, BF16),
            pltpu.VMEM(pooled.shape, F32),
            pltpu.VMEM(vec.shape, F32),
            pltpu.VMEM((qw,), F32),
            pltpu.VMEM((qw,), F32),
            pltpu.VMEM((width,), F32),
            pltpu.VMEM((width,), F32),
            pltpu.VMEM((width,), F32),
            pltpu.VMEM((width,), F32),
            pltpu.VMEM((width,), F32),
            pltpu.VMEM((width,), F32),
            pltpu.VMEM((width,), F32),
            pltpu.SemaphoreType.DMA((12,)),
            pltpu.SemaphoreType.DMA((12,)),
            pltpu.SemaphoreType.DMA((6,)),
            pltpu.SemaphoreType.DMA((10,)),
        ],
        compiler_params=pltpu.CompilerParams(vmem_limit_bytes=63 << 20),
    )(gw, lay, gtok, pooled, vec)
    return tuple(v.T if k in (3, 5, 6) else v for k, v in enumerate(outs))


def shards(*args):
    batch_size = lax.axis_size("batch")
    tp_size = lax.axis_size("tp")
    return unpack_call(args[6].shape[0], *layer_call(batch_size, tp_size, args))


def solution(mesh):
    placed = (
        P("batch", None),
        P(None, "tp"),
        P("tp"),
        P(None, "tp"),
        P(None, "tp"),
        P("tp"),
        P("tp", None),
        P(),
        P(),
        P(),
        P(None, "tp"),
        P("tp"),
        P("tp", None),
        P(),
        P(),
        P(),
        P("batch"),
        P("batch", None),
    )
    return jax.shard_map(
        shards,
        mesh=mesh,
        in_specs=placed,
        out_specs=(
            P(("batch", "tp"), None),
            P("batch", None),
            P(("batch", "tp"), None),
            P(None, "tp"),
            P("tp"),
            P(None, "tp"),
            P(None, "tp"),
            P("tp"),
            P("tp", None),
            P(),
            P(),
            P(),
            P(None, "tp"),
            P("tp"),
            P("tp", None),
            P(),
            P(),
            P(),
        ),
        check_vma=False,
    )
```

```python
import math

import jax
import jax.numpy as jnp
from jax import lax
from jax.experimental import pallas as pl
from jax.experimental.pallas import tpu as pltpu
from jax.sharding import PartitionSpec as P

HEAD = 64
SEQ_LEN = 512
HALF = SEQ_LEN // 2
EPSILON = 1e-06
BLOCK = 256
F32 = jnp.float32
BF16 = jnp.bfloat16
MESH = pl.DeviceIdType.MESH

NN = (((1,), (0,)), ((), ()))
NT = (((1,), (1,)), ((), ()))
TN = (((0,), (0,)), ((), ()))

FFN, HID = 0, 1
G_HID, G_FFN, G_RES, G_ATTN = 0, 1, 2, 3


UNITS = [
    (0, 256, [[0], [1, 2]], [[1, 2], [0]]),
    (256, 256, [[0], [1, 2]], [[2], [1], [0]]),
    (512, 256, [[1], [0], [2]], [[2], [0], [1]]),
    (768, 128, [[0], [1], [2]], [[2], [1], [0]]),
    (896, 128, [[0], [1], [2]], [[1, 2], [0]]),
    (1024, 256, [[0], [1], [2]], [[2], [1], [0]]),
    (1280, 256, [[1], [0], [2]], [[2], [0], [1]]),
    (1536, 128, [[1], [0], [2]], [[2], [0], [1]]),
    (1664, 128, [[0], [1, 2]], [[1, 2], [0]]),
    (1792, 128, [[0], [1, 2]], [[1, 2], [0]]),
    (1920, 128, [[0], [1], [2]], [[1, 2], [0]]),
    (2048, 128, [[0], [1], [2]], [[1, 2], [0]]),
    (2176, 128, [[0], [1], [2]], [[1, 2], [0]]),
]
EARLY = {
    (0, 2): [(1, 0), (1, 2)],
    (0, 4): [(1, 1)],
    (0, 5): [(1, 6), (1, 3)],
    (1, 2): [(1, 4), (2, 0)],
    (1, 4): [(1, 5), (2, 3)],
    (1, 5): [(2, 4), (2, 2), (2, 1)],
    (2, 1): [(2, 6)],
    (2, 2): [(3, 0), (2, 5)],
    (2, 3): [(3, 3), (3, 4)],
    (2, 5): [(3, 2), (3, 1)],
}
LATE = [
    (4, 0),
    (3, 6),
    (1, 8),
    (3, 5),
    (1, 7),
    (4, 3),
    (1, 9),
    (4, 1),
    (4, 4),
    (1, 10),
    (4, 2),
    (1, 11),
    (4, 6),
    (5, 3),
    (1, 12),
    (107, 0),
    (2, 7),
    (2, 8),
    (2, 10),
    (4, 5),
    (2, 11),
    (2, 12),
    (108, 0),
    (109, 0),
    (5, 1),
    (2, 9),
    (3, 7),
    (5, 4),
    (3, 8),
    (3, 10),
    (5, 5),
    (5, 2),
    (3, 11),
    (3, 12),
    (5, 6),
    (110, 0),
    (6, 3),
    (3, 9),
    (4, 7),
    (4, 8),
    (111, 0),
    (4, 10),
    (6, 2),
    (6, 5),
    (4, 11),
    (4, 9),
    (5, 7),
    (4, 12),
    (5, 10),
    (6, 6),
    (5, 11),
    (6, 7),
    (5, 12),
]


def mm(left, right, dims):
    return lax.dot_general(left, right, dims, preferred_element_type=F32)


def fold8(block):
    rows, width = block.shape
    return jnp.sum(block.reshape(rows // 8, 8, width), axis=0)


def row_mean(block):
    return jnp.mean(block, axis=-1, keepdims=True)


def layer_kernel(
    batch_size,
    plan,
    early,
    late,
    len_hbm,
    tok_hbm,
    wq_hbm,
    wk_hbm,
    wv_hbm,
    wo_hbm,
    win_hbm,
    wout_hbm,
    gout_hbm,
    bq_hbm,
    bv_hbm,
    bin_hbm,
    battn_hbm,
    gain1_hbm,
    bias1_hbm,
    bout_hbm,
    gain2_hbm,
    bias2_hbm,
    lay_hbm,
    pool_hbm,
    gtok_hbm,
    gw_hbm,
    vec_hbm,
    len_ref,
    bq_ref,
    bv_ref,
    bin_ref,
    battn_ref,
    gain1_ref,
    bias1_ref,
    bout_ref,
    gain2_ref,
    bias2_ref,
    pool_ref,
    gtok_ref,
    vec_ref,
    small_sem,
    tok_v,
    wqkv_v,
    wo_v,
    wof_v,
    win_v,
    wout_v,
    gout_v,
    qkv_v,
    ctx_v,
    lse_v,
    hid_v,
    act_v,
    slope_v,
    norm1_v,
    inv1_v,
    res2_v,
    gffn_v,
    lay_v,
    gt_v,
    do_v,
    mask_v,
    part_v,
    cs_v,
    cr_v,
    ys_v,
    yr_v,
    all_v,
    tcr_v,
    tow_v,
    tys_v,
    tyr_v,
    gw_v,
    sum_v,
    rv_v,
    wacc_v,
    par_v,
    acc_v,
    vec_v,
    vc_v,
    vx_v,
    vq_v,
    in_sem,
    cs_sem,
    cr_sem,
    ys_sem,
    yr_sem,
    as_sem,
    ar_sem,
    hs_sem,
    hr_sem,
    tcs_sem,
    tcr_sem,
    tys_sem,
    tyr_sem,
    ws_sem,
    wr_sem,
    vs_sem,
    vr_sem,
    vqs_sem,
    vqr_sem,
    out_sem,
):
    rows_all, width = tok_v.shape
    sentences = rows_all // SEQ_LEN
    qw = wo_v.shape[0]
    heads = qw // HEAD
    quads = batch_size // 4
    bits = batch_size.bit_length() - 1

    gattn_v = gffn_v
    din_v = slope_v

    tp = lax.axis_index("tp")
    ba = lax.axis_index("batch")
    core = lax.rem(tp, 2)
    other = 1 - core
    chip = tp // 2
    quad = ba // 4
    bit = [lax.rem(ba // 2**k, 2) for k in range(bits)]
    core_id = {"tp": chip * 2 + other}
    y_id = {"tp": (1 - chip) * 2 + core}

    def flip_id(flips):
        at = ba
        for k in flips:
            at = at + (1 - 2 * bit[k]) * 2**k
        return {"batch": at}

    def flip_quad(flips):
        at = quad
        for k in flips:
            at = at + (1 - 2 * bit[k]) * 2 ** (k - 2)
        return at

    def subsets(group):
        return [
            [k for j, k in enumerate(group) if n >> j & 1] for n in range(1, 2 ** len(group))
        ]

    quad_flips = subsets(range(2, bits))
    batch_peers = []
    for _, _, down, up in plan:
        for group in down + up:
            batch_peers += [f for f in subsets(group) if f not in batch_peers]
    for f in [[0], [1]] + quad_flips:
        if f not in batch_peers:
            batch_peers.append(f)

    def remote(src, dst, send, recv, dev):
        return pltpu.make_async_remote_copy(
            src_ref=src,
            dst_ref=dst,
            send_sem=send,
            recv_sem=recv,
            device_id=dev,
            device_id_type=MESH,
        )

    def order(i):
        return lax.rem(2 * i, sentences)

    def tok_copy(i):
        rows = pl.ds(pl.multiple_of(order(i) * SEQ_LEN, SEQ_LEN), SEQ_LEN)
        return pltpu.make_async_copy(tok_hbm.at[rows], tok_v.at[rows], in_sem.at[i])

    w_copies = [
        pltpu.make_async_copy(src, dst, in_sem.at[sentences + k])
        for k, (src, dst) in enumerate(
            [
                (wq_hbm, wqkv_v.at[pl.ds(0, qw)]),
                (wk_hbm, wqkv_v.at[pl.ds(qw, qw)]),
                (wv_hbm, wqkv_v.at[pl.ds(2 * qw, qw)]),
                (wo_hbm, wo_v),
                (win_hbm, win_v),
                (wout_hbm, wout_v),
            ]
        )
    ]

    small_copies = [
        pltpu.make_async_copy(src, dst, small_sem.at[k])
        for k, (src, dst) in enumerate(
            [
                (len_hbm, len_ref),
                (bq_hbm, bq_ref),
                (bv_hbm, bv_ref),
                (bin_hbm, bin_ref),
                (battn_hbm, battn_ref),
                (gain1_hbm, gain1_ref),
                (bias1_hbm, bias1_ref),
                (bout_hbm, bout_ref),
                (gain2_hbm, gain2_ref),
                (bias2_hbm, bias2_ref),
            ]
        )
    ]

    def gout_copy(i):
        src = pl.ds(pl.multiple_of(order(i) * SEQ_LEN + core * HALF, HALF), HALF)
        dst = pl.ds(pl.multiple_of(i * HALF, HALF), HALF)
        return pltpu.make_async_copy(
            gout_hbm.at[src], gout_v.at[dst], in_sem.at[sentences + 6 + i]
        )

    barrier = pltpu.get_barrier_semaphore()
    cross_id = {"tp": (1 - chip) * 2 + other}
    peers = [core_id, y_id, cross_id] + [flip_id(f) for f in batch_peers]
    for dev in peers:
        pl.semaphore_signal(barrier, inc=1, device_id=dev, device_id_type=MESH)

    w_copies[3].start()
    for k in range(3):
        w_copies[k].start()
    for k in range(3):
        small_copies[k].start()
    tok_copy(0).start()
    for i in range(1, sentences):
        tok_copy(i).start()
    for k in range(4, 6):
        w_copies[k].start()
    for k in range(3, 10):
        small_copies[k].start()
    for i in range(sentences):
        gout_copy(i).start()

    acc_v[...] = jnp.zeros_like(acc_v)
    bin_row, battn_row, gain1_row, bias1_row, bout_row, gain2_row, bias2_row = [
        par_v.at[pl.ds(k, 1)] for k in range(7)
    ]

    def core_copy(ph, i):
        k = ph * sentences + i
        slot = k
        return remote(cs_v.at[slot], cr_v.at[slot], cs_sem.at[k], cr_sem.at[k], core_id)

    def y_copy(ph, i):
        k = ph * sentences + i
        slot = k
        return remote(ys_v.at[slot], yr_v.at[slot], ys_sem.at[k], yr_sem.at[k], y_id)

    ctx_all = all_v
    own_heads = pl.ds(pl.multiple_of(tp * qw, 16), qw)
    far_heads = pl.ds(pl.multiple_of(((1 - chip) * 2 + core) * qw, 16), qw)

    def heads_copy(kind, i):
        half = core if kind == 0 else other
        at = pl.multiple_of(order(i) * SEQ_LEN + half * HALF, HALF)
        dev = (y_id, core_id, cross_id)[kind]
        return remote(
            ctx_v.at[:, pl.ds(at, HALF)],
            ctx_all.at[own_heads, pl.ds(pl.multiple_of(i * HALF, HALF), HALF)],
            hs_sem.at[kind * sentences + i],
            hr_sem.at[kind * sentences + i],
            dev,
        )

    def proj_copy(kind):
        k = 3 * sentences + kind
        src = wof_v.at[far_heads] if kind == 2 else wo_v
        dst = wof_v.at[far_heads if kind == 2 else own_heads]
        return remote(src, dst, hs_sem.at[k], hr_sem.at[k], y_id if kind == 0 else core_id)

    def gather_copy(which, ref, i):
        k = which * sentences + i
        rows = pl.ds(pl.multiple_of(order(i) * SEQ_LEN + core * HALF, HALF), HALF)
        return remote(ref.at[rows], ref.at[rows], as_sem.at[k], ar_sem.at[k], core_id)

    def chip_sum(ph, i):
        slot = ph * sentences + i
        core_copy(ph, i).wait_recv()

        @pl.loop(0, HALF // BLOCK)
        def _(j):
            rows = pl.ds(pl.multiple_of(j * BLOCK, BLOCK), BLOCK)
            ys_v[slot, rows, :] = (part_v[rows, :] + cr_v[slot, rows, :].astype(F32)).astype(BF16)

        y_copy(ph, i).start()

    def total_rows(ph, i, rows):
        slot = ph * sentences + i
        return ys_v[slot, rows, :].astype(F32) + yr_v[slot, rows, :].astype(F32)

    def add_acc(k, value):
        rows = pl.ds(8 * k, 8)
        acc_v[rows, :] = acc_v[rows, :] + fold8(value)

    def fill_mask(s):
        limit = len_ref[s]
        key = lax.broadcasted_iota(jnp.int32, mask_v.shape, 0)
        mask_v[...] = jnp.where(key < limit, 0.0, -1e30)

    def masked_scores(k_t, q_t):
        mask = mask_v[...]
        return mm(k_t, q_t, TN) + jnp.concatenate([mask] * (q_t.shape[1] // 128), axis=1)

    def column(row_ref):
        row = row_ref[...].reshape(1, qw)
        return jnp.transpose(jnp.broadcast_to(row, (8, qw)))[:, :1]

    w_copies[3].wait()
    pl.semaphore_wait(barrier, len(peers))
    proj_copy(0).start()
    proj_copy(1).start()
    for k in range(3):
        w_copies[k].wait()

    def project(i):
        s = order(i)
        cols = pl.ds(pl.multiple_of(s * SEQ_LEN, SEQ_LEN), SEQ_LEN)
        tok_copy(i).wait()
        x = tok_v[cols, :]
        qkv_v[pl.ds(0, qw), cols] = (
            mm(wqkv_v[pl.ds(0, qw), :], x, NT) + column(bq_ref)
        ).astype(BF16) * jnp.asarray(HEAD ** (-0.5), BF16)
        qkv_v[pl.ds(qw, qw), cols] = mm(wqkv_v[pl.ds(qw, qw), :], x, NT).astype(BF16)
        qkv_v[pl.ds(2 * qw, qw), cols] = (
            mm(wqkv_v[pl.ds(2 * qw, qw), :], x, NT) + column(bv_ref)
        ).astype(BF16)
        fill_mask(s)

    def attend(i, half):
        r0 = pl.multiple_of(order(i) * SEQ_LEN, SEQ_LEN)
        cols = pl.ds(r0, SEQ_LEN)
        qcols = pl.ds(pl.multiple_of(r0 + half * HALF, HALF), HALF)
        for h in range(heads):
            k_t = qkv_v[pl.ds(qw + h * HEAD, HEAD), cols]
            v_t = qkv_v[pl.ds(2 * qw + h * HEAD, HEAD), cols]
            scores = masked_scores(k_t, qkv_v[pl.ds(h * HEAD, HEAD), qcols])
            top = jnp.max(scores, axis=0, keepdims=True)
            expo = jnp.exp(scores - top)
            total = jnp.sum(expo, axis=0, keepdims=True)
            shares = (expo * (1.0 / total)).astype(BF16)
            ctx_v[pl.ds(h * HEAD, HEAD), qcols] = mm(v_t, shares, NN).astype(BF16)
            lse_v[pl.ds(h, 1), qcols] = top + jnp.log(total)

    for k in range(3):
        small_copies[k].wait()
    project(0)
    attend(0, other)

    @pl.loop(0, sentences)
    def _(i):
        heads_copy(2, i).start()
        heads_copy(1, i).start()
        attend(i, core)
        heads_copy(0, i).start()
        own = pl.ds(pl.multiple_of(order(i) * SEQ_LEN + core * HALF, HALF), HALF)
        ctx_all[own_heads, pl.ds(pl.multiple_of(i * HALF, HALF), HALF)] = ctx_v[:, own]

        @pl.when(i + 1 < sentences)
        def _():
            project(i + 1)
            attend(i + 1, other)

    wof_v[own_heads, :] = wo_v[...]
    proj_copy(0).wait_recv()
    proj_copy(2).start()

    w_copies[4].wait()
    w_copies[5].wait()
    for k in range(3, 10):
        small_copies[k].wait()
    for k, ref in enumerate(
        (bin_ref, battn_ref, gain1_ref, bias1_ref, bout_ref, gain2_ref, bias2_ref)
    ):
        par_v[pl.ds(k, 1), :] = ref[...].reshape(1, width)
    proj_copy(1).wait_recv()
    proj_copy(2).wait_recv()

    @pl.loop(0, sentences)
    def _(i):
        r0 = pl.multiple_of(order(i) * SEQ_LEN, SEQ_LEN)
        own0 = pl.multiple_of(r0 + core * HALF, HALF)
        oth0 = pl.multiple_of(r0 + other * HALF, HALF)
        for kind in range(3):
            heads_copy(kind, i).wait_recv()
        heard = ctx_all[:, pl.ds(pl.multiple_of(i * HALF, HALF), HALF)]
        part_v[...] = mm(heard, wof_v[...], TN)

        @pl.loop(0, HALF // BLOCK)
        def _(j):
            rows = pl.ds(pl.multiple_of(j * BLOCK, BLOCK), BLOCK)
            full = pl.ds(pl.multiple_of(own0 + j * BLOCK, BLOCK), BLOCK)
            kept = pl.ds(pl.multiple_of(i * HALF + j * BLOCK, BLOCK), BLOCK)
            resid = tok_v[full, :].astype(F32) + (part_v[rows, :] + battn_row[...])
            centred = resid - row_mean(resid)
            inv = lax.rsqrt(row_mean(centred * centred) + EPSILON)
            normed = centred * inv
            norm1_v[kept, :] = normed
            inv1_v[kept, :] = jnp.broadcast_to(inv, (BLOCK, 128))
            hid_v[full, :] = (normed * gain1_row[...] + bias1_row[...]).astype(BF16)

        gather_copy(G_HID, hid_v, i).start()

        def feed(base):
            full = pl.ds(base, HALF)
            pre = mm(hid_v[full, :], win_v[...], NN) + bin_row[...]
            cdf = 0.5 * (1.0 + lax.erf(pre * 0.5**0.5))
            act_v[full, :] = (pre * cdf).astype(BF16)
            slope_v[full, :] = (
                cdf + pre * (jnp.exp(-0.5 * pre * pre) * (2.0 * math.pi) ** (-0.5))
            ).astype(slope_v.dtype)
            return mm(act_v[pl.ds(base, HALF), :], wout_v[...], NN)

        part_v[...] = feed(own0)
        gather_copy(G_HID, hid_v, i).wait_recv()
        cs_v[i] = feed(oth0).astype(BF16)
        core_copy(FFN, i).start()
        chip_sum(FFN, i)

    chunk_rows = gw_v.shape[0] // 3

    def store_rows(j, t, block):
        gw_v[pl.ds(j * chunk_rows + t * 384, 384), :] = block.astype(BF16)

    stages = []
    used = 0
    for base, rows, down, up in plan:
        where, size, unit, spare = base, rows, [], base
        for group in down:
            unit_stage = {"sends": [], "waits": [], "adds": []}
            size = size // 2 ** len(group)

            def place(flips, group=group, where=where, size=size):
                at = where
                for j, k in enumerate(group):
                    side = 1 - bit[k] if k in flips else bit[k]
                    at = at + side * (size * 2 ** (len(group) - 1 - j))
                return at

            own = place([])
            unit_stage["order"] = [place(flips) for flips in subsets(group)] + [own]
            unit_stage["size"] = size
            for flips in subsets(group):
                src = gw_v.at[pl.ds(pl.multiple_of(place(flips), 16), size)]
                dst = rv_v.at[pl.ds(spare, size)]
                args = (src, dst, ws_sem.at[used], wr_sem.at[used], flip_id(flips))
                unit_stage["sends"].append(lambda args=args: remote(*args))
                unit_stage["waits"].append(lambda args=args: remote(*args))
                unit_stage["adds"].append((own, spare, size))
                spare += size
                used += 1
            unit.append(unit_stage)
            where = own
        final = (where, size)
        for group in up:
            unit_stage = {"sends": [], "waits": [], "adds": []}
            order_bits = [k for g in down for k in g]
            weight = {}
            width_of = rows
            for k in order_bits:
                width_of = width_of // 2
                weight[k] = width_of
            held = [k for g in up[: up.index(group)] for k in g]
            mine = base
            span = rows
            for k in order_bits:
                if k not in held:
                    mine = mine + bit[k] * weight[k]
                    span = span // 2
            for flips in subsets(group):
                theirs = mine
                for k in flips:
                    theirs = theirs + (1 - 2 * bit[k]) * weight[k]
                here = sum_v.at[pl.ds(pl.multiple_of(mine, 16), span)]
                there = sum_v.at[pl.ds(pl.multiple_of(theirs, 16), span)]
                sems = (ws_sem.at[used], wr_sem.at[used], flip_id(flips))
                unit_stage["sends"].append(lambda r=here, t=sems: remote(r, r, *t))
                unit_stage["waits"].append(lambda r=there, t=sems: remote(r, r, *t))
                used += 1
            unit.append(unit_stage)
        for unit_stage in unit:
            unit_stage["final"] = final
            unit_stage["last_down"] = len(down) - 1
        stages.append(unit)

    def start_stage(u, n):
        for copy in stages[u][n]["sends"]:
            copy().start()

    def out_copy(u):
        base, rows = plan[u][:2]
        at = pl.ds(base, rows)
        return pltpu.make_async_copy(sum_v.at[at], gw_hbm.at[at], out_sem.at[1 + u])

    def step(n, u):
        done = stages[u][n - 1]
        for copy in done["waits"]:
            copy().wait_recv()
        more = n < len(stages[u])
        if done["adds"]:
            own, _, size = done["adds"][0]
            blocks, part = [own], size
            if more and "order" in stages[u][n]:
                blocks, part = stages[u][n]["order"], stages[u][n]["size"]
            for at in blocks:
                if at is blocks[-1] and len(blocks) > 1:
                    start_stage(u, n)
                rows = pl.ds(pl.multiple_of(at, 16), part)
                total = gw_v[rows, :].astype(F32)
                for _, spare, _ in done["adds"]:
                    here = pl.ds(pl.multiple_of(spare + at - own, 16), part)
                    total = total + rv_v[here, :].astype(F32)
                if n - 1 == done["last_down"]:
                    sum_v[rows, :] = total.astype(BF16)
                else:
                    gw_v[rows, :] = total.astype(BF16)
            if len(blocks) > 1:
                return
        if more:
            start_stage(u, n)
        else:
            out_copy(u).start()

    def start_rows(c, t):
        for u, (base, rows, _, _) in enumerate(plan):
            last_tile = min((base % chunk_rows + rows - 1) // 384, width // 384 - 1)
            if base // chunk_rows == c and last_tile == t:
                start_stage(u, 0)

    wacc_v[...] = jnp.zeros_like(wacc_v)

    @pl.loop(0, sentences)
    def _(i):
        r0 = pl.multiple_of(order(i) * SEQ_LEN, SEQ_LEN)
        own0 = pl.multiple_of(r0 + core * HALF, HALF)
        oth0 = pl.multiple_of(r0 + other * HALF, HALF)
        gout_copy(i).wait()
        y_copy(FFN, i).wait_recv()

        @pl.loop(0, HALF // BLOCK)
        def _(j):
            rows = pl.ds(pl.multiple_of(j * BLOCK, BLOCK), BLOCK)
            full = pl.ds(pl.multiple_of(own0 + j * BLOCK, BLOCK), BLOCK)
            kept = pl.ds(pl.multiple_of(i * HALF + j * BLOCK, BLOCK), BLOCK)
            hidden = norm1_v[kept, :] * gain1_row[...] + bias1_row[...]
            resid = hidden + (total_rows(FFN, i, rows) + bout_row[...])
            centred = resid - row_mean(resid)
            inv = lax.rsqrt(row_mean(centred * centred) + EPSILON)
            normed = centred * inv
            lay_v[full, :] = (normed * gain2_row[...] + bias2_row[...]).astype(BF16)
            up = gout_v[kept, :].astype(F32)
            scaled = up * gain2_row[...]
            grad = inv * (scaled - row_mean(scaled) - normed * row_mean(scaled * normed))
            res2_v[kept, :] = grad
            gffn_v[full, :] = grad.astype(BF16)
            add_acc(4, grad)
            add_acc(5, up * normed)
            add_acc(6, up)

        gather_copy(G_FFN, gffn_v, i).start()
        gather_copy(G_RES, lay_v, i).start()

        def back(base):
            full = pl.ds(base, HALF)
            inner = (
                mm(gffn_v[full, :], wout_v[...], NT) * slope_v[full, :].astype(F32)
            ).astype(BF16)
            din_v[full, :] = inner
            add_acc(0, inner.astype(F32))
            return mm(din_v[pl.ds(base, HALF), :], win_v[...], NT)

        def grow(base, t):
            at = pl.ds(t * 384, 384)
            half = pl.ds(base, HALF)
            wacc_v[at, :] = wacc_v[at, :] + mm(act_v[half, at], gffn_v[half, :], TN)

        for t in range(width // 384):
            grow(own0, t)
        gather_copy(G_FFN, gffn_v, i).wait_recv()
        for t in range(width // 384):
            grow(oth0, t)

            @pl.when(i == sentences - 1)
            def _():
                store_rows(0, t, wacc_v[pl.ds(t * 384, 384), :])
                start_rows(0, t)

        part_v[...] = back(own0)
        cs_v[sentences + i] = back(oth0).astype(BF16)
        core_copy(HID, i).start()
        chip_sum(HID, i)

    for t in range(width // 384):
        store_rows(1, t, mm(hid_v[:, pl.ds(t * 384, 384)], din_v[...], TN))
        start_rows(1, t)

    steps = {}

    def run_step(n, u):
        if n in steps:
            steps[n]()
        else:
            step(n, u)

    def serve(i, point):
        for (turn, place), todo in early.items():
            if place == point:

                @pl.when(i == turn)
                def _():
                    for n, u in todo:
                        run_step(n, u)

    wacc_v[...] = jnp.zeros_like(wacc_v)

    @pl.loop(0, sentences)
    def _(i):
        s = order(i)
        r0 = pl.multiple_of(s * SEQ_LEN, SEQ_LEN)
        cols = pl.ds(r0, SEQ_LEN)
        own0 = pl.multiple_of(r0 + core * HALF, HALF)
        y_copy(HID, i).wait_recv()
        gather_copy(G_FFN, gffn_v, i).wait_send()

        @pl.loop(0, HALF // BLOCK)
        def _(j):
            rows = pl.ds(pl.multiple_of(j * BLOCK, BLOCK), BLOCK)
            full = pl.ds(pl.multiple_of(own0 + j * BLOCK, BLOCK), BLOCK)
            kept = pl.ds(pl.multiple_of(i * HALF + j * BLOCK, BLOCK), BLOCK)
            grad_hidden = res2_v[kept, :] + total_rows(HID, i, rows)
            normed = norm1_v[kept, :]
            inv = inv1_v[kept, :][:, :1]
            scaled = grad_hidden * gain1_row[...]
            grad = inv * (scaled - row_mean(scaled) - normed * row_mean(scaled * normed))
            gattn_v[full, :] = grad.astype(BF16)
            add_acc(1, grad)
            add_acc(2, grad_hidden * normed)
            add_acc(3, grad_hidden)

        gather_copy(G_ATTN, gattn_v, i).start()
        fill_mask(s)
        serve(i, 1)
        gather_copy(G_ATTN, gattn_v, i).wait_recv()
        do_v[...] = mm(wo_v[...], gattn_v[cols, :], NT).astype(BF16)
        for h in range(heads):
            k_t = qkv_v[pl.ds(qw + h * HEAD, HEAD), cols]
            v_t = qkv_v[pl.ds(2 * qw + h * HEAD, HEAD), cols]
            q_t = qkv_v[pl.ds(h * HEAD, HEAD), cols]
            d_t = do_v[pl.ds(h * HEAD, HEAD), :]
            c_t = ctx_v[pl.ds(h * HEAD, HEAD), cols]
            delta = jnp.sum(d_t.astype(F32) * c_t.astype(F32), axis=0, keepdims=True)
            shares = jnp.exp(masked_scores(k_t, q_t) - lse_v[pl.ds(h, 1), cols])
            grad_shares = mm(v_t, d_t, TN)
            grad_scores = (shares * (grad_shares - delta)).astype(BF16)
            gt_v[pl.ds(h * HEAD, HEAD), cols] = (
                mm(k_t, grad_scores, NN) * HEAD ** (-0.5)
            ).astype(BF16)
            gt_v[pl.ds(qw + h * HEAD, HEAD), cols] = mm(q_t, grad_scores, NT).astype(BF16)
            gt_v[pl.ds(2 * qw + h * HEAD, HEAD), cols] = mm(
                d_t, shares.astype(BF16), NT
            ).astype(BF16)
            serve(i, 2 + h)

        flat = pl.ds(0, 3 * qw)
        wacc_v[flat, :] = wacc_v[flat, :] + mm(gt_v[:, cols], tok_v[cols, :], NN)
        flat = pl.ds(3 * qw, qw)
        wacc_v[flat, :] = wacc_v[flat, :] + mm(ctx_v[:, cols], gattn_v[cols, :], NN)

        @pl.when(i == sentences - 1)
        def _():
            for t in range(width // 384):
                store_rows(2, t, wacc_v[pl.ds(t * 384, 384), :])
                start_rows(2, t)

        @pl.loop(0, 2)
        def _(j2):
            hcols = pl.ds(pl.multiple_of(r0 + j2 * 256, 256), 256)
            half_part = mm(gt_v[:, hcols], wqkv_v[...], TN).astype(BF16)
            for j1 in range(2):
                blk = s * (SEQ_LEN // 128) + j2 * 2 + j1
                quarter = blk // 3
                place = lax.rem(blk, 3)
                slot = (quarter // 2) * 3 + place
                part = half_part[j1 * 128 : j1 * 128 + 128]

                @pl.when(lax.rem(quarter, 2) == core)
                def _():
                    tow_v[slot] = part

                @pl.when(lax.rem(quarter, 2) == other)
                def _():
                    all_v[pl.ds(pl.multiple_of(slot * 128, 128), 128), :] = part
                    remote(
                        all_v.at[pl.ds(pl.multiple_of(slot * 128, 128), 128)],
                        tcr_v.at[slot],
                        tcs_sem.at[slot],
                        tcr_sem.at[slot],
                        core_id,
                    ).start()

        serve(i, 5)

    ones = jnp.ones((8, rows_all), BF16)
    vec_v[...] = jnp.zeros_like(vec_v)
    vec_v[pl.ds(0, 1), pl.ds(0, qw)] = mm(ones, gt_v[pl.ds(0, qw), :], NT)[:1]
    vec_v[pl.ds(0, 1), pl.ds(256, qw)] = mm(ones, gt_v[pl.ds(2 * qw, qw), :], NT)[:1]
    for k in range(7):
        vec_v[pl.ds(1 + k, 1), :] = jnp.sum(acc_v[pl.ds(8 * k, 8), :], axis=0, keepdims=True)
    v_core = remote(vec_v, vc_v, vs_sem.at[0], vr_sem.at[0], core_id)
    v_core.start()

    v_core.wait()
    row_id = lax.broadcasted_iota(jnp.int32, vec_v.shape, 0)
    vx_v[0] = vec_v[...] + jnp.where(row_id >= 2, vc_v[...], 0.0)
    v_x = remote(vx_v.at[0], vx_v.at[1], vs_sem.at[1], vr_sem.at[1], flip_id([0]))
    v_x.start()

    def t_core(slot):
        return remote(
            all_v.at[pl.ds(slot * 128, 128)],
            tcr_v.at[slot],
            tcs_sem.at[slot],
            tcr_sem.at[slot],
            core_id,
        )

    def t_y(k):
        return remote(tys_v.at[k], tyr_v.at[k], tys_sem.at[k], tyr_sem.at[k], y_id)

    for k in range(3):
        slot = (1 - chip) * 3 + k
        t_core(slot).wait_recv()
        tys_v[k] = (tow_v[slot].astype(F32) + tcr_v[slot].astype(F32)).astype(BF16)
        t_y(k).start()

    v_p = remote(vx_v.at[2], vx_v.at[3], vs_sem.at[2], vr_sem.at[2], flip_id([1]))

    small_outs = [
        pltpu.make_async_copy(src, dst, small_sem.at[k])
        for k, (src, dst) in enumerate(
            [(vec_ref, vec_hbm), (pool_ref, pool_hbm), (gtok_ref, gtok_hbm)]
        )
    ]

    def vector_step1():
        v_x.wait()
        vx_v[2] = vx_v[0] + vx_v[1]
        v_p.start()

    def vq_copy(k):
        return remote(
            vq_v.at[quad], vq_v.at[quad], vqs_sem.at[k], vqr_sem.at[quad], flip_id(quad_flips[k])
        )

    def vq_from(k):
        q = flip_quad(quad_flips[k])
        return remote(vq_v.at[q], vq_v.at[q], vqs_sem.at[k], vqr_sem.at[q], flip_id(quad_flips[k]))

    def vector_step2():
        v_p.wait()
        vq_v[quad] = vx_v[2] + vx_v[3]
        for k in range(quads - 1):
            vq_copy(k).start()

    def vector_step3():
        for k in range(quads - 1):
            vq_from(k).wait_recv()
        total = vq_v[0]
        for q in range(1, quads):
            total = total + vq_v[q]
        vec_ref[...] = total
        small_outs[0].start()

    quarter_rows = rows_all // 4
    lay_out = pltpu.make_async_copy(
        lay_v.at[pl.ds(pl.multiple_of(tp * quarter_rows, quarter_rows), quarter_rows)],
        lay_hbm,
        out_sem.at[0],
    )

    def layer_step():
        for i in range(sentences):
            gather_copy(G_RES, lay_v, i).wait_recv()
        lay_out.start()
        for s in range(sentences):
            key = lax.broadcasted_iota(jnp.int32, (8, SEQ_LEN), 1)
            member = jnp.where(key < len_ref[s], 1.0, 0.0).astype(BF16)
            total = mm(member, lay_v[pl.ds(s * SEQ_LEN, SEQ_LEN), :], NN)[:1]
            average = total / len_ref[s].astype(F32)
            at = 0
            for cut in (width, width * 2 // 3, width // 3, width // 6, width // 12):
                prefix = average[:, :cut]
                centred = prefix - row_mean(prefix)
                pool_ref[pl.ds(s, 1), pl.ds(at, cut)] = centred * lax.rsqrt(
                    row_mean(centred * centred) + EPSILON
                )
                at += cut
        small_outs[1].start()

    def input_step():
        for k in range(3):
            slot = chip * 3 + k
            t_core(slot).wait_recv()
            mine = (tow_v[slot].astype(F32) + tcr_v[slot].astype(F32)).astype(BF16)
            t_y(k).wait_recv()
            at = pl.ds(pl.multiple_of(tp * quarter_rows + k * 128, 128), 128)
            gtok_ref[pl.ds(k * 128, 128), :] = (
                gattn_v[at, :].astype(F32) + (mine.astype(F32) + tyr_v[k].astype(F32))
            ).astype(BF16)
        small_outs[2].start()

    steps.update(
        {107: vector_step1, 108: vector_step2, 109: input_step, 110: vector_step3, 111: layer_step}
    )
    for n, u in late:
        run_step(n, u)

    for u in range(len(plan)):
        out_copy(u).wait()
    lay_out.wait()
    for copy in small_outs:
        copy.wait()
    for kind in range(3):
        proj_copy(kind).wait_send()
        for i in range(sentences):
            heads_copy(kind, i).wait_send()
    for i in range(sentences):
        core_copy(FFN, i).wait_send()
        y_copy(FFN, i).wait_send()
        core_copy(HID, i).wait_send()
        y_copy(HID, i).wait_send()
        gather_copy(G_HID, hid_v, i).wait_send()
        gather_copy(G_RES, lay_v, i).wait_send()
        gather_copy(G_ATTN, gattn_v, i).wait_send()
    for slot in range(6):
        t_core(slot).wait_send()
    for k in range(3):
        t_y(k).wait_send()
    for u in range(len(plan)):
        for n in range(len(stages[u])):
            for copy in stages[u][n]["sends"]:
                copy().wait_send()
    for k in range(quads - 1):
        vq_copy(k).wait_send()


def layer_call(batch_size, tp_size, args):
    (
        tokens,
        w_query,
        b_query,
        w_key,
        w_value,
        b_value,
        w_attn_out,
        b_attn_out,
        gain_one,
        bias_one,
        w_in,
        b_in,
        w_out,
        b_out,
        gain_two,
        bias_two,
        lengths,
        grad_out,
    ) = args
    rows, width = tokens.shape
    sentences = lengths.shape[0]
    qw = w_attn_out.shape[0]
    ff = w_in.shape[1]
    quads = batch_size // 4
    piece = -(-width // batch_size)
    piece = -(-piece // 16) * 16
    chunk = piece * batch_size
    if batch_size == 8:
        plan, early, late = UNITS, EARLY, LATE
    else:
        high = list(range(2, batch_size.bit_length() - 1))
        plan = [(c * chunk, chunk, [[0], [1], high], [high, [1], [0]]) for c in range(3)]
        early = {}
        late = [(n, u) for n in range(1, 7) for u in range(3)]
        late = late[:3] + [(n, 0) for n in range(107, 112)] + late[3:]
    copies = sum(2 ** len(g) - 1 for unit in plan for g in unit[2] + unit[3])
    quarter = rows // tp_size
    anyspec = pl.BlockSpec(memory_space=pl.ANY)
    dma = pltpu.SemaphoreType.DMA
    V = pltpu.VMEM
    kept = rows // 2
    return pl.pallas_call(
        lambda *refs: layer_kernel(batch_size, plan, early, late, *refs),
        out_shape=(
            jax.ShapeDtypeStruct((quarter, width), BF16),
            jax.ShapeDtypeStruct((sentences, width * 9 // 4), F32),
            jax.ShapeDtypeStruct((quarter, width), BF16),
            jax.ShapeDtypeStruct((3 * chunk, width), BF16),
            jax.ShapeDtypeStruct((8, width), F32),
        ),
        in_specs=[anyspec] * 18,
        out_specs=(anyspec,) * 5,
        scratch_shapes=[
            pltpu.SMEM((sentences,), jnp.int32),
            V((qw,), F32),
            V((qw,), F32),
            V((ff,), F32),
            V((width,), F32),
            V((width,), F32),
            V((width,), F32),
            V((width,), F32),
            V((width,), F32),
            V((width,), F32),
            V((sentences, width * 9 // 4), F32),
            V((quarter, width), BF16),
            V((8, width), F32),
            dma((10,)),
            V((rows, width), BF16),
            V((3 * qw, width), BF16),
            V((qw, width), BF16),
            V((width, width), BF16),
            V((width, ff), BF16),
            V((ff, width), BF16),
            V((kept, width), BF16),
            V((3 * qw, rows), BF16),
            V((qw, rows), BF16),
            V((8, rows), F32),
            V((rows, width), BF16),
            V((rows, ff), BF16),
            V((rows, ff), BF16),
            V((kept, width), F32),
            V((kept, 128), F32),
            V((kept, width), F32),
            V((rows, width), BF16),
            V((rows, width), BF16),
            V((3 * qw, rows), BF16),
            V((qw, SEQ_LEN), BF16),
            V((SEQ_LEN, 128), F32),
            V((HALF, width), F32),
            V((2 * sentences, HALF, width), BF16),
            V((2 * sentences, HALF, width), BF16),
            V((2 * sentences, HALF, width), BF16),
            V((2 * sentences, HALF, width), BF16),
            V((width, width), BF16),
            V((6, 128, width), BF16),
            V((6, 128, width), BF16),
            V((3, 128, width), BF16),
            V((3, 128, width), BF16),
            V((3 * chunk, width), BF16),
            V((3 * chunk, width), BF16),
            V((3 * chunk, width), BF16),
            V((ff, width), F32),
            V((8, width), F32),
            V((64, width), F32),
            V((8, width), F32),
            V((8, width), F32),
            V((4, 8, width), F32),
            V((quads, 8, width), F32),
            dma((2 * sentences + 6,)),
            dma((2 * sentences,)),
            dma((2 * sentences,)),
            dma((2 * sentences,)),
            dma((2 * sentences,)),
            dma((4 * sentences,)),
            dma((4 * sentences,)),
            dma((3 * sentences + 3,)),
            dma((3 * sentences + 3,)),
            dma((6,)),
            dma((6,)),
            dma((3,)),
            dma((3,)),
            dma((copies,)),
            dma((copies,)),
            dma((3,)),
            dma((3,)),
            dma((quads,)),
            dma((quads,)),
            dma((1 + len(plan),)),
        ],
        compiler_params=pltpu.CompilerParams(
            collective_id=0, has_side_effects=True, vmem_limit_bytes=63 << 20
        ),
    )(
        lengths,
        tokens,
        w_query.T,
        w_key.T,
        w_value.T,
        w_attn_out,
        w_in,
        w_out,
        grad_out,
        b_query,
        b_value,
        b_in,
        b_attn_out,
        gain_one,
        bias_one,
        b_out,
        gain_two,
        bias_two,
    )


def unpack_kernel(
    qw,
    gw_hbm,
    lay_in,
    gtok_in,
    pool_in,
    vec_in,
    lay_hbm,
    pool_hbm,
    gtok_hbm,
    wq_hbm,
    bq_ref,
    wk_hbm,
    wv_hbm,
    bv_ref,
    wo_hbm,
    battn_ref,
    gain1_ref,
    bias1_ref,
    win_hbm,
    bin_ref,
    wout_hbm,
    bout_ref,
    gain2_ref,
    bias2_ref,
    low_v,
    full_v,
    lay_v,
    gtok_v,
    pool_v,
    vec_v,
    bq_v,
    bv_v,
    v0,
    v1,
    v2,
    v3,
    v4,
    v5,
    v6,
    in_sem,
    out_sem,
    side_sem,
    vec_sem,
):
    chunk = low_v.shape[0] // 3
    width = low_v.shape[1]
    pieces = [
        (c * chunk + r, c * width + r, dst.at[pl.ds(r, 192)])
        for c, dst in ((0, wout_hbm), (1, win_hbm))
        for r in range(0, width, 192)
    ]
    pieces += [
        (2 * chunk + k * qw, 2 * width + k * qw, dst)
        for k, dst in enumerate((wq_hbm, wk_hbm, wv_hbm, wo_hbm))
    ]
    ins = [
        pltpu.make_async_copy(
            gw_hbm.at[pl.ds(src, 192)], low_v.at[pl.ds(src, 192)], in_sem.at[k]
        )
        for k, (src, _, _) in enumerate(pieces)
    ]
    for copy in ins:
        copy.start()
    lay_copy = pltpu.make_async_copy(lay_in, lay_v, side_sem.at[0])
    gtok_copy = pltpu.make_async_copy(gtok_in, gtok_v, side_sem.at[1])
    pool_copy = pltpu.make_async_copy(pool_in, pool_v, side_sem.at[2])
    vec_copy = pltpu.make_async_copy(vec_in, vec_v, side_sem.at[5])
    lay_copy.start()
    gtok_copy.start()
    pool_copy.start()
    vec_copy.start()
    outs = []
    for k, (src, at, dst) in enumerate(pieces):
        ins[k].wait()
        full_v[pl.ds(at, 192), :] = low_v[pl.ds(src, 192), :].astype(F32)
        copy = pltpu.make_async_copy(full_v.at[pl.ds(at, 192)], dst, out_sem.at[k])
        copy.start()
        outs.append(copy)
    lay_copy.wait()
    outs.append(pltpu.make_async_copy(lay_v, lay_hbm, side_sem.at[3]))
    outs[-1].start()
    gtok_copy.wait()
    outs.append(pltpu.make_async_copy(gtok_v, gtok_hbm, side_sem.at[4]))
    outs[-1].start()
    vec_copy.wait()
    short = (bq_v, bv_v, v0, v1, v2, v3, v4, v5, v6)
    bq_v[...] = vec_v[0, pl.ds(0, qw)]
    bv_v[...] = vec_v[0, pl.ds(256, qw)]
    for k in range(7):
        short[2 + k][...] = vec_v[1 + k, :]
    dsts = (bq_ref, bv_ref, bin_ref, battn_ref, gain1_ref, bias1_ref, bout_ref, gain2_ref, bias2_ref)
    for k, dst in enumerate(dsts):
        outs.append(pltpu.make_async_copy(short[k], dst, vec_sem.at[k]))
        outs[-1].start()
    pool_copy.wait()
    outs.append(pltpu.make_async_copy(pool_v, pool_hbm, vec_sem.at[9]))
    outs[-1].start()
    for copy in outs:
        copy.wait()


def unpack_call(qw, lay, pooled, gtok, gw, vec):
    width = gw.shape[1]
    anyspec = pl.BlockSpec(memory_space=pl.ANY)
    like = lambda v: jax.ShapeDtypeStruct(v.shape, v.dtype)
    mat = lambda n: jax.ShapeDtypeStruct((n, width), F32)
    one = lambda n: jax.ShapeDtypeStruct((n,), F32)
    outs = pl.pallas_call(
        lambda *refs: unpack_kernel(qw, *refs),
        out_shape=(
            like(lay),
            like(pooled),
            like(gtok),
            mat(qw),
            one(qw),
            mat(qw),
            mat(qw),
            one(qw),
            mat(qw),
            one(width),
            one(width),
            one(width),
            mat(width),
            one(width),
            mat(width),
            one(width),
            one(width),
            one(width),
        ),
        in_specs=[anyspec] * 5,
        out_specs=(anyspec,) * 18,
        scratch_shapes=[
            pltpu.VMEM(gw.shape, BF16),
            pltpu.VMEM((3 * width, width), F32),
            pltpu.VMEM(lay.shape, BF16),
            pltpu.VMEM(gtok.shape, BF16),
            pltpu.VMEM(pooled.shape, F32),
            pltpu.VMEM(vec.shape, F32),
            pltpu.VMEM((qw,), F32),
            pltpu.VMEM((qw,), F32),
            pltpu.VMEM((width,), F32),
            pltpu.VMEM((width,), F32),
            pltpu.VMEM((width,), F32),
            pltpu.VMEM((width,), F32),
            pltpu.VMEM((width,), F32),
            pltpu.VMEM((width,), F32),
            pltpu.VMEM((width,), F32),
            pltpu.SemaphoreType.DMA((12,)),
            pltpu.SemaphoreType.DMA((12,)),
            pltpu.SemaphoreType.DMA((6,)),
            pltpu.SemaphoreType.DMA((10,)),
        ],
        compiler_params=pltpu.CompilerParams(vmem_limit_bytes=63 << 20),
    )(gw, lay, gtok, pooled, vec)
    return tuple(v.T if k in (3, 5, 6) else v for k, v in enumerate(outs))


def shards(*args):
    batch_size = lax.axis_size("batch")
    tp_size = lax.axis_size("tp")
    return unpack_call(args[6].shape[0], *layer_call(batch_size, tp_size, args))


def solution(mesh):
    placed = (
        P("batch", None),
        P(None, "tp"),
        P("tp"),
        P(None, "tp"),
        P(None, "tp"),
        P("tp"),
        P("tp", None),
        P(),
        P(),
        P(),
        P(None, "tp"),
        P("tp"),
        P("tp", None),
        P(),
        P(),
        P(),
        P("batch"),
        P("batch", None),
    )
    return jax.shard_map(
        shards,
        mesh=mesh,
        in_specs=placed,
        out_specs=(
            P(("batch", "tp"), None),
            P("batch", None),
            P(("batch", "tp"), None),
            P(None, "tp"),
            P("tp"),
            P(None, "tp"),
            P(None, "tp"),
            P("tp"),
            P("tp", None),
            P(),
            P(),
            P(),
            P(None, "tp"),
            P("tp"),
            P("tp", None),
            P(),
            P(),
            P(),
        ),
        check_vma=False,
    )
```

```python
import math

import jax
import jax.numpy as jnp
from jax import lax
from jax.experimental import pallas as pl
from jax.experimental.pallas import tpu as pltpu
from jax.sharding import PartitionSpec as P

HEAD = 64
SEQ_LEN = 512
HALF = SEQ_LEN // 2
EPSILON = 1e-06
BLOCK = 256
F32 = jnp.float32
BF16 = jnp.bfloat16
MESH = pl.DeviceIdType.MESH

NN = (((1,), (0,)), ((), ()))
NT = (((1,), (1,)), ((), ()))
TN = (((0,), (0,)), ((), ()))

FFN, HID = 0, 1
G_HID, G_FFN, G_RES, G_ATTN = 0, 1, 2, 3


UNITS = [
    (0, 256, [[0], [1, 2]], [[1, 2], [0]]),
    (256, 256, [[0], [1, 2]], [[2], [1], [0]]),
    (512, 256, [[1], [0], [2]], [[2], [0], [1]]),
    (768, 128, [[0], [1], [2]], [[2], [1], [0]]),
    (896, 128, [[0], [1], [2]], [[1, 2], [0]]),
    (1024, 256, [[0], [1], [2]], [[2], [1], [0]]),
    (1280, 256, [[1], [0], [2]], [[2], [0], [1]]),
    (1536, 128, [[1], [0], [2]], [[2], [0], [1]]),
    (1664, 128, [[0], [1, 2]], [[1, 2], [0]]),
    (1792, 128, [[0], [1, 2]], [[1, 2], [0]]),
    (1920, 128, [[0], [1], [2]], [[1, 2], [0]]),
    (2048, 128, [[0], [1], [2]], [[1, 2], [0]]),
    (2176, 128, [[0], [1], [2]], [[1, 2], [0]]),
]
EARLY = {
    (0, 2): [(1, 0), (1, 2)],
    (0, 4): [(1, 1)],
    (0, 5): [(1, 6), (1, 3)],
    (1, 2): [(1, 4), (2, 0)],
    (1, 4): [(1, 5), (2, 3)],
    (1, 5): [(2, 4), (2, 2), (2, 1)],
    (2, 1): [(2, 6)],
    (2, 2): [(3, 0), (2, 5)],
    (2, 3): [(3, 3), (3, 4)],
    (2, 5): [(3, 2), (3, 1)],
}
LATE = [
    (4, 0),
    (3, 6),
    (1, 8),
    (3, 5),
    (1, 7),
    (4, 3),
    (1, 9),
    (4, 1),
    (4, 4),
    (1, 10),
    (4, 2),
    (1, 11),
    (4, 6),
    (5, 3),
    (1, 12),
    (107, 0),
    (2, 7),
    (2, 8),
    (2, 10),
    (4, 5),
    (2, 11),
    (2, 12),
    (108, 0),
    (109, 0),
    (5, 1),
    (2, 9),
    (3, 7),
    (5, 4),
    (3, 8),
    (3, 10),
    (5, 5),
    (5, 2),
    (3, 11),
    (3, 12),
    (5, 6),
    (110, 0),
    (6, 3),
    (3, 9),
    (4, 7),
    (4, 8),
    (111, 0),
    (4, 10),
    (6, 2),
    (6, 5),
    (4, 11),
    (4, 9),
    (5, 7),
    (4, 12),
    (5, 10),
    (6, 6),
    (5, 11),
    (6, 7),
    (5, 12),
]


def mm(left, right, dims):
    return lax.dot_general(left, right, dims, preferred_element_type=F32)


def fold8(block):
    rows, width = block.shape
    return jnp.sum(block.reshape(rows // 8, 8, width), axis=0)


def row_mean(block):
    return jnp.mean(block, axis=-1, keepdims=True)


def layer_kernel(
    batch_size,
    plan,
    early,
    late,
    len_hbm,
    tok_hbm,
    wq_hbm,
    wk_hbm,
    wv_hbm,
    wo_hbm,
    win_hbm,
    wout_hbm,
    gout_hbm,
    bq_hbm,
    bv_hbm,
    bin_hbm,
    battn_hbm,
    gain1_hbm,
    bias1_hbm,
    bout_hbm,
    gain2_hbm,
    bias2_hbm,
    lay_hbm,
    pool_hbm,
    gtok_hbm,
    gw_hbm,
    vec_hbm,
    len_ref,
    bq_ref,
    bv_ref,
    bin_ref,
    battn_ref,
    gain1_ref,
    bias1_ref,
    bout_ref,
    gain2_ref,
    bias2_ref,
    pool_ref,
    gtok_ref,
    vec_ref,
    small_sem,
    tok_v,
    wqkv_v,
    wo_v,
    wof_v,
    win_v,
    wout_v,
    gout_v,
    qkv_v,
    ctx_v,
    lse_v,
    hid_v,
    act_v,
    slope_v,
    norm1_v,
    inv1_v,
    res2_v,
    gffn_v,
    lay_v,
    gt_v,
    do_v,
    mask_v,
    part_v,
    cs_v,
    cr_v,
    ys_v,
    yr_v,
    all_v,
    tcr_v,
    tow_v,
    tys_v,
    tyr_v,
    gw_v,
    sum_v,
    rv_v,
    wacc_v,
    par_v,
    acc_v,
    vec_v,
    vc_v,
    vx_v,
    vq_v,
    in_sem,
    cs_sem,
    cr_sem,
    ys_sem,
    yr_sem,
    as_sem,
    ar_sem,
    hs_sem,
    hr_sem,
    tcs_sem,
    tcr_sem,
    tys_sem,
    tyr_sem,
    ws_sem,
    wr_sem,
    vs_sem,
    vr_sem,
    vqs_sem,
    vqr_sem,
    out_sem,
):
    rows_all, width = tok_v.shape
    sentences = rows_all // SEQ_LEN
    qw = wo_v.shape[0]
    heads = qw // HEAD
    quads = batch_size // 4
    bits = batch_size.bit_length() - 1

    gattn_v = gffn_v
    din_v = slope_v

    tp = lax.axis_index("tp")
    ba = lax.axis_index("batch")
    core = lax.rem(tp, 2)
    other = 1 - core
    chip = tp // 2
    quad = ba // 4
    bit = [lax.rem(ba // 2**k, 2) for k in range(bits)]
    core_id = {"tp": chip * 2 + other}
    y_id = {"tp": (1 - chip) * 2 + core}

    def flip_id(flips):
        at = ba
        for k in flips:
            at = at + (1 - 2 * bit[k]) * 2**k
        return {"batch": at}

    def flip_quad(flips):
        at = quad
        for k in flips:
            at = at + (1 - 2 * bit[k]) * 2 ** (k - 2)
        return at

    def subsets(group):
        return [
            [k for j, k in enumerate(group) if n >> j & 1] for n in range(1, 2 ** len(group))
        ]

    quad_flips = subsets(range(2, bits))
    batch_peers = []
    for _, _, down, up in plan:
        for group in down + up:
            batch_peers += [f for f in subsets(group) if f not in batch_peers]
    for f in [[0], [1]] + quad_flips:
        if f not in batch_peers:
            batch_peers.append(f)

    def remote(src, dst, send, recv, dev):
        return pltpu.make_async_remote_copy(
            src_ref=src,
            dst_ref=dst,
            send_sem=send,
            recv_sem=recv,
            device_id=dev,
            device_id_type=MESH,
        )

    def order(i):
        return lax.rem(2 * i, sentences)

    def tok_copy(i):
        rows = pl.ds(pl.multiple_of(order(i) * SEQ_LEN, SEQ_LEN), SEQ_LEN)
        return pltpu.make_async_copy(tok_hbm.at[rows], tok_v.at[rows], in_sem.at[i])

    w_copies = [
        pltpu.make_async_copy(src, dst, in_sem.at[sentences + k])
        for k, (src, dst) in enumerate(
            [
                (wq_hbm, wqkv_v.at[pl.ds(0, qw)]),
                (wk_hbm, wqkv_v.at[pl.ds(qw, qw)]),
                (wv_hbm, wqkv_v.at[pl.ds(2 * qw, qw)]),
                (wo_hbm, wo_v),
                (win_hbm, win_v),
                (wout_hbm, wout_v),
            ]
        )
    ]

    small_copies = [
        pltpu.make_async_copy(src, dst, small_sem.at[k])
        for k, (src, dst) in enumerate(
            [
                (len_hbm, len_ref),
                (bq_hbm, bq_ref),
                (bv_hbm, bv_ref),
                (bin_hbm, bin_ref),
                (battn_hbm, battn_ref),
                (gain1_hbm, gain1_ref),
                (bias1_hbm, bias1_ref),
                (bout_hbm, bout_ref),
                (gain2_hbm, gain2_ref),
                (bias2_hbm, bias2_ref),
            ]
        )
    ]

    def gout_copy(i):
        src = pl.ds(pl.multiple_of(order(i) * SEQ_LEN + core * HALF, HALF), HALF)
        dst = pl.ds(pl.multiple_of(i * HALF, HALF), HALF)
        return pltpu.make_async_copy(
            gout_hbm.at[src], gout_v.at[dst], in_sem.at[sentences + 6 + i]
        )

    barrier = pltpu.get_barrier_semaphore()
    cross_id = {"tp": (1 - chip) * 2 + other}
    peers = [core_id, y_id, cross_id] + [flip_id(f) for f in batch_peers]
    for dev in peers:
        pl.semaphore_signal(barrier, inc=1, device_id=dev, device_id_type=MESH)

    w_copies[3].start()
    for k in range(3):
        w_copies[k].start()
    for k in range(3):
        small_copies[k].start()
    tok_copy(0).start()
    for i in range(1, sentences):
        tok_copy(i).start()
    for k in range(4, 6):
        w_copies[k].start()
    for k in range(3, 10):
        small_copies[k].start()
    for i in range(sentences):
        gout_copy(i).start()

    acc_v[...] = jnp.zeros_like(acc_v)
    bin_row, battn_row, gain1_row, bias1_row, bout_row, gain2_row, bias2_row = [
        par_v.at[pl.ds(k, 1)] for k in range(7)
    ]

    def core_copy(ph, i):
        k = ph * sentences + i
        slot = k
        return remote(cs_v.at[slot], cr_v.at[slot], cs_sem.at[k], cr_sem.at[k], core_id)

    def y_copy(ph, i):
        k = ph * sentences + i
        slot = k
        return remote(ys_v.at[slot], yr_v.at[slot], ys_sem.at[k], yr_sem.at[k], y_id)

    ctx_all = all_v
    own_heads = pl.ds(pl.multiple_of(tp * qw, 16), qw)
    far_heads = pl.ds(pl.multiple_of(((1 - chip) * 2 + core) * qw, 16), qw)

    def heads_copy(kind, i):
        half = core if kind == 0 else other
        at = pl.multiple_of(order(i) * SEQ_LEN + half * HALF, HALF)
        dev = (y_id, core_id, cross_id)[kind]
        return remote(
            ctx_v.at[:, pl.ds(at, HALF)],
            ctx_all.at[own_heads, pl.ds(pl.multiple_of(i * HALF, HALF), HALF)],
            hs_sem.at[kind * sentences + i],
            hr_sem.at[kind * sentences + i],
            dev,
        )

    def proj_copy(kind):
        k = 3 * sentences + kind
        src = wof_v.at[far_heads] if kind == 2 else wo_v
        dst = wof_v.at[far_heads if kind == 2 else own_heads]
        return remote(src, dst, hs_sem.at[k], hr_sem.at[k], y_id if kind == 0 else core_id)

    def gather_copy(which, ref, i):
        k = which * sentences + i
        rows = pl.ds(pl.multiple_of(order(i) * SEQ_LEN + core * HALF, HALF), HALF)
        return remote(ref.at[rows], ref.at[rows], as_sem.at[k], ar_sem.at[k], core_id)

    def chip_sum(ph, i):
        slot = ph * sentences + i
        core_copy(ph, i).wait_recv()

        @pl.loop(0, HALF // BLOCK)
        def _(j):
            rows = pl.ds(pl.multiple_of(j * BLOCK, BLOCK), BLOCK)
            ys_v[slot, rows, :] = (part_v[rows, :] + cr_v[slot, rows, :].astype(F32)).astype(BF16)

        y_copy(ph, i).start()

    def total_rows(ph, i, rows):
        slot = ph * sentences + i
        return ys_v[slot, rows, :].astype(F32) + yr_v[slot, rows, :].astype(F32)

    def add_acc(k, value):
        rows = pl.ds(8 * k, 8)
        acc_v[rows, :] = acc_v[rows, :] + fold8(value)

    def fill_mask(s):
        limit = len_ref[s]
        key = lax.broadcasted_iota(jnp.int32, mask_v.shape, 0)
        mask_v[...] = jnp.where(key < limit, 0.0, -1e30)

    def masked_scores(k_t, q_t):
        mask = mask_v[...]
        return mm(k_t, q_t, TN) + jnp.concatenate([mask] * (q_t.shape[1] // 128), axis=1)

    def column(row_ref):
        row = row_ref[...].reshape(1, qw)
        return jnp.transpose(jnp.broadcast_to(row, (8, qw)))[:, :1]

    w_copies[3].wait()
    pl.semaphore_wait(barrier, len(peers))
    proj_copy(0).start()
    proj_copy(1).start()
    for k in range(3):
        w_copies[k].wait()

    def project(i):
        s = order(i)
        cols = pl.ds(pl.multiple_of(s * SEQ_LEN, SEQ_LEN), SEQ_LEN)
        tok_copy(i).wait()
        x = tok_v[cols, :]
        qkv_v[pl.ds(0, qw), cols] = (
            mm(wqkv_v[pl.ds(0, qw), :], x, NT) + column(bq_ref)
        ).astype(BF16) * jnp.asarray(HEAD ** (-0.5), BF16)
        qkv_v[pl.ds(qw, qw), cols] = mm(wqkv_v[pl.ds(qw, qw), :], x, NT).astype(BF16)
        qkv_v[pl.ds(2 * qw, qw), cols] = (
            mm(wqkv_v[pl.ds(2 * qw, qw), :], x, NT) + column(bv_ref)
        ).astype(BF16)
        fill_mask(s)

    def attend(i, half):
        r0 = pl.multiple_of(order(i) * SEQ_LEN, SEQ_LEN)
        cols = pl.ds(r0, SEQ_LEN)
        qcols = pl.ds(pl.multiple_of(r0 + half * HALF, HALF), HALF)
        for h in range(heads):
            k_t = qkv_v[pl.ds(qw + h * HEAD, HEAD), cols]
            v_t = qkv_v[pl.ds(2 * qw + h * HEAD, HEAD), cols]
            scores = masked_scores(k_t, qkv_v[pl.ds(h * HEAD, HEAD), qcols])
            top = jnp.max(scores, axis=0, keepdims=True)
            expo = jnp.exp(scores - top)
            total = jnp.sum(expo, axis=0, keepdims=True)
            shares = (expo * (1.0 / total)).astype(BF16)
            ctx_v[pl.ds(h * HEAD, HEAD), qcols] = mm(v_t, shares, NN).astype(BF16)
            lse_v[pl.ds(h, 1), qcols] = top + jnp.log(total)

    for k in range(3):
        small_copies[k].wait()
    project(0)
    attend(0, other)

    @pl.loop(0, sentences)
    def _(i):
        heads_copy(2, i).start()
        heads_copy(1, i).start()
        attend(i, core)
        heads_copy(0, i).start()
        own = pl.ds(pl.multiple_of(order(i) * SEQ_LEN + core * HALF, HALF), HALF)
        ctx_all[own_heads, pl.ds(pl.multiple_of(i * HALF, HALF), HALF)] = ctx_v[:, own]

        @pl.when(i + 1 < sentences)
        def _():
            project(i + 1)
            attend(i + 1, other)

    wof_v[own_heads, :] = wo_v[...]
    proj_copy(0).wait_recv()
    proj_copy(2).start()

    w_copies[4].wait()
    w_copies[5].wait()
    for k in range(3, 10):
        small_copies[k].wait()
    for k, ref in enumerate(
        (bin_ref, battn_ref, gain1_ref, bias1_ref, bout_ref, gain2_ref, bias2_ref)
    ):
        par_v[pl.ds(k, 1), :] = ref[...].reshape(1, width)
    proj_copy(1).wait_recv()
    proj_copy(2).wait_recv()

    @pl.loop(0, sentences)
    def _(i):
        r0 = pl.multiple_of(order(i) * SEQ_LEN, SEQ_LEN)
        own0 = pl.multiple_of(r0 + core * HALF, HALF)
        oth0 = pl.multiple_of(r0 + other * HALF, HALF)
        for kind in range(3):
            heads_copy(kind, i).wait_recv()
        heard = ctx_all[:, pl.ds(pl.multiple_of(i * HALF, HALF), HALF)]
        part_v[...] = mm(heard, wof_v[...], TN)

        @pl.loop(0, HALF // BLOCK)
        def _(j):
            rows = pl.ds(pl.multiple_of(j * BLOCK, BLOCK), BLOCK)
            full = pl.ds(pl.multiple_of(own0 + j * BLOCK, BLOCK), BLOCK)
            kept = pl.ds(pl.multiple_of(i * HALF + j * BLOCK, BLOCK), BLOCK)
            resid = tok_v[full, :].astype(F32) + (part_v[rows, :] + battn_row[...])
            centred = resid - row_mean(resid)
            inv = lax.rsqrt(row_mean(centred * centred) + EPSILON)
            normed = centred * inv
            norm1_v[kept, :] = normed
            inv1_v[kept, :] = jnp.broadcast_to(inv, (BLOCK, 128))
            hid_v[full, :] = (normed * gain1_row[...] + bias1_row[...]).astype(BF16)

        gather_copy(G_HID, hid_v, i).start()

        def feed(base):
            full = pl.ds(base, HALF)
            pre = mm(hid_v[full, :], win_v[...], NN) + bin_row[...]
            cdf = 0.5 * (1.0 + lax.erf(pre * 0.5**0.5))
            act_v[full, :] = (pre * cdf).astype(BF16)
            slope_v[full, :] = (
                cdf + pre * (jnp.exp(-0.5 * pre * pre) * (2.0 * math.pi) ** (-0.5))
            ).astype(slope_v.dtype)
            return mm(act_v[pl.ds(base, HALF), :], wout_v[...], NN)

        part_v[...] = feed(own0)
        gather_copy(G_HID, hid_v, i).wait_recv()
        cs_v[i] = feed(oth0).astype(BF16)
        core_copy(FFN, i).start()
        chip_sum(FFN, i)

    chunk_rows = gw_v.shape[0] // 3

    def store_rows(j, t, block):
        gw_v[pl.ds(j * chunk_rows + t * 384, 384), :] = block.astype(BF16)

    stages = []
    used = 0
    for base, rows, down, up in plan:
        where, size, unit, spare = base, rows, [], base
        for group in down:
            unit_stage = {"sends": [], "waits": [], "adds": []}
            size = size // 2 ** len(group)

            def place(flips, group=group, where=where, size=size):
                at = where
                for j, k in enumerate(group):
                    side = 1 - bit[k] if k in flips else bit[k]
                    at = at + side * (size * 2 ** (len(group) - 1 - j))
                return at

            own = place([])
            unit_stage["order"] = [place(flips) for flips in subsets(group)] + [own]
            unit_stage["size"] = size
            for flips in subsets(group):
                src = gw_v.at[pl.ds(pl.multiple_of(place(flips), 16), size)]
                dst = rv_v.at[pl.ds(spare, size)]
                args = (src, dst, ws_sem.at[used], wr_sem.at[used], flip_id(flips))
                unit_stage["sends"].append(lambda args=args: remote(*args))
                unit_stage["waits"].append(lambda args=args: remote(*args))
                unit_stage["adds"].append((own, spare, size))
                spare += size
                used += 1
            unit.append(unit_stage)
            where = own
        final = (where, size)
        for group in up:
            unit_stage = {"sends": [], "waits": [], "adds": []}
            order_bits = [k for g in down for k in g]
            weight = {}
            width_of = rows
            for k in order_bits:
                width_of = width_of // 2
                weight[k] = width_of
            held = [k for g in up[: up.index(group)] for k in g]
            mine = base
            span = rows
            for k in order_bits:
                if k not in held:
                    mine = mine + bit[k] * weight[k]
                    span = span // 2
            for flips in subsets(group):
                theirs = mine
                for k in flips:
                    theirs = theirs + (1 - 2 * bit[k]) * weight[k]
                here = sum_v.at[pl.ds(pl.multiple_of(mine, 16), span)]
                there = sum_v.at[pl.ds(pl.multiple_of(theirs, 16), span)]
                sems = (ws_sem.at[used], wr_sem.at[used], flip_id(flips))
                unit_stage["sends"].append(lambda r=here, t=sems: remote(r, r, *t))
                unit_stage["waits"].append(lambda r=there, t=sems: remote(r, r, *t))
                used += 1
            unit.append(unit_stage)
        for unit_stage in unit:
            unit_stage["final"] = final
            unit_stage["last_down"] = len(down) - 1
        stages.append(unit)

    def start_stage(u, n):
        for copy in stages[u][n]["sends"]:
            copy().start()

    def out_copy(u):
        base, rows = plan[u][:2]
        at = pl.ds(base, rows)
        return pltpu.make_async_copy(sum_v.at[at], gw_hbm.at[at], out_sem.at[1 + u])

    def step(n, u):
        done = stages[u][n - 1]
        for copy in done["waits"]:
            copy().wait_recv()
        more = n < len(stages[u])
        if done["adds"]:
            own, _, size = done["adds"][0]
            blocks, part = [own], size
            if more and "order" in stages[u][n]:
                blocks, part = stages[u][n]["order"], stages[u][n]["size"]
            for at in blocks:
                if at is blocks[-1] and len(blocks) > 1:
                    start_stage(u, n)
                rows = pl.ds(pl.multiple_of(at, 16), part)
                total = gw_v[rows, :].astype(F32)
                for _, spare, _ in done["adds"]:
                    here = pl.ds(pl.multiple_of(spare + at - own, 16), part)
                    total = total + rv_v[here, :].astype(F32)
                if n - 1 == done["last_down"]:
                    sum_v[rows, :] = total.astype(BF16)
                else:
                    gw_v[rows, :] = total.astype(BF16)
            if len(blocks) > 1:
                return
        if more:
            start_stage(u, n)
        else:
            out_copy(u).start()

    def start_rows(c, t):
        for u, (base, rows, _, _) in enumerate(plan):
            last_tile = min((base % chunk_rows + rows - 1) // 384, width // 384 - 1)
            if base // chunk_rows == c and last_tile == t:
                start_stage(u, 0)

    wacc_v[...] = jnp.zeros_like(wacc_v)

    @pl.loop(0, sentences)
    def _(i):
        r0 = pl.multiple_of(order(i) * SEQ_LEN, SEQ_LEN)
        own0 = pl.multiple_of(r0 + core * HALF, HALF)
        oth0 = pl.multiple_of(r0 + other * HALF, HALF)
        gout_copy(i).wait()
        y_copy(FFN, i).wait_recv()

        @pl.loop(0, HALF // BLOCK)
        def _(j):
            rows = pl.ds(pl.multiple_of(j * BLOCK, BLOCK), BLOCK)
            full = pl.ds(pl.multiple_of(own0 + j * BLOCK, BLOCK), BLOCK)
            kept = pl.ds(pl.multiple_of(i * HALF + j * BLOCK, BLOCK), BLOCK)
            hidden = norm1_v[kept, :] * gain1_row[...] + bias1_row[...]
            resid = hidden + (total_rows(FFN, i, rows) + bout_row[...])
            centred = resid - row_mean(resid)
            inv = lax.rsqrt(row_mean(centred * centred) + EPSILON)
            normed = centred * inv
            lay_v[full, :] = (normed * gain2_row[...] + bias2_row[...]).astype(BF16)
            up = gout_v[kept, :].astype(F32)
            scaled = up * gain2_row[...]
            grad = inv * (scaled - row_mean(scaled) - normed * row_mean(scaled * normed))
            res2_v[kept, :] = grad
            gffn_v[full, :] = grad.astype(BF16)
            add_acc(4, grad)
            add_acc(5, up * normed)
            add_acc(6, up)

        gather_copy(G_FFN, gffn_v, i).start()
        gather_copy(G_RES, lay_v, i).start()

        def back(base):
            full = pl.ds(base, HALF)
            inner = (
                mm(gffn_v[full, :], wout_v[...], NT) * slope_v[full, :].astype(F32)
            ).astype(BF16)
            din_v[full, :] = inner
            add_acc(0, inner.astype(F32))
            return mm(din_v[pl.ds(base, HALF), :], win_v[...], NT)

        def grow(base, t):
            at = pl.ds(t * 384, 384)
            half = pl.ds(base, HALF)
            wacc_v[at, :] = wacc_v[at, :] + mm(act_v[half, at], gffn_v[half, :], TN)

        for t in range(width // 384):
            grow(own0, t)
        gather_copy(G_FFN, gffn_v, i).wait_recv()
        for t in range(width // 384):
            grow(oth0, t)

            @pl.when(i == sentences - 1)
            def _():
                store_rows(0, t, wacc_v[pl.ds(t * 384, 384), :])
                start_rows(0, t)

        part_v[...] = back(own0)
        cs_v[sentences + i] = back(oth0).astype(BF16)
        core_copy(HID, i).start()
        chip_sum(HID, i)

    for t in range(width // 384):
        store_rows(1, t, mm(hid_v[:, pl.ds(t * 384, 384)], din_v[...], TN))
        start_rows(1, t)

    steps = {}

    def run_step(n, u):
        if n in steps:
            steps[n]()
        else:
            step(n, u)

    def serve(i, point):
        for (turn, place), todo in early.items():
            if place == point:

                @pl.when(i == turn)
                def _():
                    for n, u in todo:
                        run_step(n, u)

    wacc_v[...] = jnp.zeros_like(wacc_v)

    @pl.loop(0, sentences)
    def _(i):
        s = order(i)
        r0 = pl.multiple_of(s * SEQ_LEN, SEQ_LEN)
        cols = pl.ds(r0, SEQ_LEN)
        own0 = pl.multiple_of(r0 + core * HALF, HALF)
        y_copy(HID, i).wait_recv()
        gather_copy(G_FFN, gffn_v, i).wait_send()

        @pl.loop(0, HALF // BLOCK)
        def _(j):
            rows = pl.ds(pl.multiple_of(j * BLOCK, BLOCK), BLOCK)
            full = pl.ds(pl.multiple_of(own0 + j * BLOCK, BLOCK), BLOCK)
            kept = pl.ds(pl.multiple_of(i * HALF + j * BLOCK, BLOCK), BLOCK)
            grad_hidden = res2_v[kept, :] + total_rows(HID, i, rows)
            normed = norm1_v[kept, :]
            inv = inv1_v[kept, :][:, :1]
            scaled = grad_hidden * gain1_row[...]
            grad = inv * (scaled - row_mean(scaled) - normed * row_mean(scaled * normed))
            gattn_v[full, :] = grad.astype(BF16)
            add_acc(1, grad)
            add_acc(2, grad_hidden * normed)
            add_acc(3, grad_hidden)

        gather_copy(G_ATTN, gattn_v, i).start()
        fill_mask(s)
        serve(i, 1)
        gather_copy(G_ATTN, gattn_v, i).wait_recv()
        do_v[...] = mm(wo_v[...], gattn_v[cols, :], NT).astype(BF16)
        for h in range(heads):
            k_t = qkv_v[pl.ds(qw + h * HEAD, HEAD), cols]
            v_t = qkv_v[pl.ds(2 * qw + h * HEAD, HEAD), cols]
            q_t = qkv_v[pl.ds(h * HEAD, HEAD), cols]
            d_t = do_v[pl.ds(h * HEAD, HEAD), :]
            c_t = ctx_v[pl.ds(h * HEAD, HEAD), cols]
            delta = jnp.sum(d_t.astype(F32) * c_t.astype(F32), axis=0, keepdims=True)
            shares = jnp.exp(masked_scores(k_t, q_t) - lse_v[pl.ds(h, 1), cols])
            grad_shares = mm(v_t, d_t, TN)
            grad_scores = (shares * (grad_shares - delta)).astype(BF16)
            gt_v[pl.ds(h * HEAD, HEAD), cols] = (
                mm(k_t, grad_scores, NN) * HEAD ** (-0.5)
            ).astype(BF16)
            gt_v[pl.ds(qw + h * HEAD, HEAD), cols] = mm(q_t, grad_scores, NT).astype(BF16)
            gt_v[pl.ds(2 * qw + h * HEAD, HEAD), cols] = mm(
                d_t, shares.astype(BF16), NT
            ).astype(BF16)
            serve(i, 2 + h)

        flat = pl.ds(0, 3 * qw)
        wacc_v[flat, :] = wacc_v[flat, :] + mm(gt_v[:, cols], tok_v[cols, :], NN)
        flat = pl.ds(3 * qw, qw)
        wacc_v[flat, :] = wacc_v[flat, :] + mm(ctx_v[:, cols], gattn_v[cols, :], NN)

        @pl.when(i == sentences - 1)
        def _():
            for t in range(width // 384):
                store_rows(2, t, wacc_v[pl.ds(t * 384, 384), :])
                start_rows(2, t)

        @pl.loop(0, 2)
        def _(j2):
            hcols = pl.ds(pl.multiple_of(r0 + j2 * 256, 256), 256)
            half_part = mm(gt_v[:, hcols], wqkv_v[...], TN).astype(BF16)
            for j1 in range(2):
                blk = s * (SEQ_LEN // 128) + j2 * 2 + j1
                quarter = blk // 3
                place = lax.rem(blk, 3)
                slot = (quarter // 2) * 3 + place
                part = half_part[j1 * 128 : j1 * 128 + 128]

                @pl.when(lax.rem(quarter, 2) == core)
                def _():
                    tow_v[slot] = part

                @pl.when(lax.rem(quarter, 2) == other)
                def _():
                    all_v[pl.ds(pl.multiple_of(slot * 128, 128), 128), :] = part
                    remote(
                        all_v.at[pl.ds(pl.multiple_of(slot * 128, 128), 128)],
                        tcr_v.at[slot],
                        tcs_sem.at[slot],
                        tcr_sem.at[slot],
                        core_id,
                    ).start()

        serve(i, 5)

    ones = jnp.ones((8, rows_all), BF16)
    vec_v[...] = jnp.zeros_like(vec_v)
    vec_v[pl.ds(0, 1), pl.ds(0, qw)] = mm(ones, gt_v[pl.ds(0, qw), :], NT)[:1]
    vec_v[pl.ds(0, 1), pl.ds(256, qw)] = mm(ones, gt_v[pl.ds(2 * qw, qw), :], NT)[:1]
    for k in range(7):
        vec_v[pl.ds(1 + k, 1), :] = jnp.sum(acc_v[pl.ds(8 * k, 8), :], axis=0, keepdims=True)
    v_core = remote(vec_v, vc_v, vs_sem.at[0], vr_sem.at[0], core_id)
    v_core.start()

    v_core.wait()
    row_id = lax.broadcasted_iota(jnp.int32, vec_v.shape, 0)
    vx_v[0] = vec_v[...] + jnp.where(row_id >= 2, vc_v[...], 0.0)
    v_x = remote(vx_v.at[0], vx_v.at[1], vs_sem.at[1], vr_sem.at[1], flip_id([0]))
    v_x.start()

    def t_core(slot):
        return remote(
            all_v.at[pl.ds(slot * 128, 128)],
            tcr_v.at[slot],
            tcs_sem.at[slot],
            tcr_sem.at[slot],
            core_id,
        )

    def t_y(k):
        return remote(tys_v.at[k], tyr_v.at[k], tys_sem.at[k], tyr_sem.at[k], y_id)

    for k in range(3):
        slot = (1 - chip) * 3 + k
        t_core(slot).wait_recv()
        tys_v[k] = (tow_v[slot].astype(F32) + tcr_v[slot].astype(F32)).astype(BF16)
        t_y(k).start()

    v_p = remote(vx_v.at[2], vx_v.at[3], vs_sem.at[2], vr_sem.at[2], flip_id([1]))

    small_outs = [
        pltpu.make_async_copy(src, dst, small_sem.at[k])
        for k, (src, dst) in enumerate(
            [(vec_ref, vec_hbm), (pool_ref, pool_hbm), (gtok_ref, gtok_hbm)]
        )
    ]

    def vector_step1():
        v_x.wait()
        vx_v[2] = vx_v[0] + vx_v[1]
        v_p.start()

    def vq_copy(k):
        return remote(
            vq_v.at[quad], vq_v.at[quad], vqs_sem.at[k], vqr_sem.at[quad], flip_id(quad_flips[k])
        )

    def vq_from(k):
        q = flip_quad(quad_flips[k])
        return remote(vq_v.at[q], vq_v.at[q], vqs_sem.at[k], vqr_sem.at[q], flip_id(quad_flips[k]))

    def vector_step2():
        v_p.wait()
        vq_v[quad] = vx_v[2] + vx_v[3]
        for k in range(quads - 1):
            vq_copy(k).start()

    def vector_step3():
        for k in range(quads - 1):
            vq_from(k).wait_recv()
        total = vq_v[0]
        for q in range(1, quads):
            total = total + vq_v[q]
        vec_ref[...] = total
        small_outs[0].start()

    quarter_rows = rows_all // 4
    lay_out = pltpu.make_async_copy(
        lay_v.at[pl.ds(pl.multiple_of(tp * quarter_rows, quarter_rows), quarter_rows)],
        lay_hbm,
        out_sem.at[0],
    )

    def layer_step():
        for i in range(sentences):
            gather_copy(G_RES, lay_v, i).wait_recv()
        lay_out.start()
        for s in range(sentences):
            key = lax.broadcasted_iota(jnp.int32, (8, SEQ_LEN), 1)
            member = jnp.where(key < len_ref[s], 1.0, 0.0).astype(BF16)
            total = mm(member, lay_v[pl.ds(s * SEQ_LEN, SEQ_LEN), :], NN)[:1]
            average = total / len_ref[s].astype(F32)
            at = 0
            for cut in (width, width * 2 // 3, width // 3, width // 6, width // 12):
                prefix = average[:, :cut]
                centred = prefix - row_mean(prefix)
                pool_ref[pl.ds(s, 1), pl.ds(at, cut)] = centred * lax.rsqrt(
                    row_mean(centred * centred) + EPSILON
                )
                at += cut
        small_outs[1].start()

    def input_step():
        for k in range(3):
            slot = chip * 3 + k
            t_core(slot).wait_recv()
            mine = (tow_v[slot].astype(F32) + tcr_v[slot].astype(F32)).astype(BF16)
            t_y(k).wait_recv()
            at = pl.ds(pl.multiple_of(tp * quarter_rows + k * 128, 128), 128)
            gtok_ref[pl.ds(k * 128, 128), :] = (
                gattn_v[at, :].astype(F32) + (mine.astype(F32) + tyr_v[k].astype(F32))
            ).astype(BF16)
        small_outs[2].start()

    steps.update(
        {107: vector_step1, 108: vector_step2, 109: input_step, 110: vector_step3, 111: layer_step}
    )
    for n, u in late:
        run_step(n, u)

    for u in range(len(plan)):
        out_copy(u).wait()
    lay_out.wait()
    for copy in small_outs:
        copy.wait()
    for kind in range(3):
        proj_copy(kind).wait_send()
        for i in range(sentences):
            heads_copy(kind, i).wait_send()
    for i in range(sentences):
        core_copy(FFN, i).wait_send()
        y_copy(FFN, i).wait_send()
        core_copy(HID, i).wait_send()
        y_copy(HID, i).wait_send()
        gather_copy(G_HID, hid_v, i).wait_send()
        gather_copy(G_RES, lay_v, i).wait_send()
        gather_copy(G_ATTN, gattn_v, i).wait_send()
    for slot in range(6):
        t_core(slot).wait_send()
    for k in range(3):
        t_y(k).wait_send()
    for u in range(len(plan)):
        for n in range(len(stages[u])):
            for copy in stages[u][n]["sends"]:
                copy().wait_send()
    for k in range(quads - 1):
        vq_copy(k).wait_send()


def layer_call(batch_size, tp_size, args):
    (
        tokens,
        w_query,
        b_query,
        w_key,
        w_value,
        b_value,
        w_attn_out,
        b_attn_out,
        gain_one,
        bias_one,
        w_in,
        b_in,
        w_out,
        b_out,
        gain_two,
        bias_two,
        lengths,
        grad_out,
    ) = args
    rows, width = tokens.shape
    sentences = lengths.shape[0]
    qw = w_attn_out.shape[0]
    ff = w_in.shape[1]
    quads = batch_size // 4
    piece = -(-width // batch_size)
    piece = -(-piece // 16) * 16
    chunk = piece * batch_size
    if batch_size == 8:
        plan, early, late = UNITS, EARLY, LATE
    else:
        high = list(range(2, batch_size.bit_length() - 1))
        plan = [(c * chunk, chunk, [[0], [1], high], [high, [1], [0]]) for c in range(3)]
        early = {}
        late = [(n, u) for n in range(1, 7) for u in range(3)]
        late = late[:3] + [(n, 0) for n in range(107, 112)] + late[3:]
    copies = sum(2 ** len(g) - 1 for unit in plan for g in unit[2] + unit[3])
    quarter = rows // tp_size
    anyspec = pl.BlockSpec(memory_space=pl.ANY)
    dma = pltpu.SemaphoreType.DMA
    V = pltpu.VMEM
    kept = rows // 2
    return pl.pallas_call(
        lambda *refs: layer_kernel(batch_size, plan, early, late, *refs),
        out_shape=(
            jax.ShapeDtypeStruct((quarter, width), BF16),
            jax.ShapeDtypeStruct((sentences, width * 9 // 4), F32),
            jax.ShapeDtypeStruct((quarter, width), BF16),
            jax.ShapeDtypeStruct((3 * chunk, width), BF16),
            jax.ShapeDtypeStruct((8, width), F32),
        ),
        in_specs=[anyspec] * 18,
        out_specs=(anyspec,) * 5,
        scratch_shapes=[
            pltpu.SMEM((sentences,), jnp.int32),
            V((qw,), F32),
            V((qw,), F32),
            V((ff,), F32),
            V((width,), F32),
            V((width,), F32),
            V((width,), F32),
            V((width,), F32),
            V((width,), F32),
            V((width,), F32),
            V((sentences, width * 9 // 4), F32),
            V((quarter, width), BF16),
            V((8, width), F32),
            dma((10,)),
            V((rows, width), BF16),
            V((3 * qw, width), BF16),
            V((qw, width), BF16),
            V((width, width), BF16),
            V((width, ff), BF16),
            V((ff, width), BF16),
            V((kept, width), BF16),
            V((3 * qw, rows), BF16),
            V((qw, rows), BF16),
            V((8, rows), F32),
            V((rows, width), BF16),
            V((rows, ff), BF16),
            V((rows, ff), BF16),
            V((kept, width), F32),
            V((kept, 128), F32),
            V((kept, width), F32),
            V((rows, width), BF16),
            V((rows, width), BF16),
            V((3 * qw, rows), BF16),
            V((qw, SEQ_LEN), BF16),
            V((SEQ_LEN, 128), F32),
            V((HALF, width), F32),
            V((2 * sentences, HALF, width), BF16),
            V((2 * sentences, HALF, width), BF16),
            V((2 * sentences, HALF, width), BF16),
            V((2 * sentences, HALF, width), BF16),
            V((width, width), BF16),
            V((6, 128, width), BF16),
            V((6, 128, width), BF16),
            V((3, 128, width), BF16),
            V((3, 128, width), BF16),
            V((3 * chunk, width), BF16),
            V((3 * chunk, width), BF16),
            V((3 * chunk, width), BF16),
            V((ff, width), F32),
            V((8, width), F32),
            V((64, width), F32),
            V((8, width), F32),
            V((8, width), F32),
            V((4, 8, width), F32),
            V((quads, 8, width), F32),
            dma((2 * sentences + 6,)),
            dma((2 * sentences,)),
            dma((2 * sentences,)),
            dma((2 * sentences,)),
            dma((2 * sentences,)),
            dma((4 * sentences,)),
            dma((4 * sentences,)),
            dma((3 * sentences + 3,)),
            dma((3 * sentences + 3,)),
            dma((6,)),
            dma((6,)),
            dma((3,)),
            dma((3,)),
            dma((copies,)),
            dma((copies,)),
            dma((3,)),
            dma((3,)),
            dma((quads,)),
            dma((quads,)),
            dma((1 + len(plan),)),
        ],
        compiler_params=pltpu.CompilerParams(
            collective_id=0, has_side_effects=True, vmem_limit_bytes=63 << 20
        ),
    )(
        lengths,
        tokens,
        w_query.T,
        w_key.T,
        w_value.T,
        w_attn_out,
        w_in,
        w_out,
        grad_out,
        b_query,
        b_value,
        b_in,
        b_attn_out,
        gain_one,
        bias_one,
        b_out,
        gain_two,
        bias_two,
    )


def unpack_kernel(
    qw,
    gw_hbm,
    lay_in,
    gtok_in,
    pool_in,
    vec_in,
    lay_hbm,
    pool_hbm,
    gtok_hbm,
    wq_hbm,
    bq_ref,
    wk_hbm,
    wv_hbm,
    bv_ref,
    wo_hbm,
    battn_ref,
    gain1_ref,
    bias1_ref,
    win_hbm,
    bin_ref,
    wout_hbm,
    bout_ref,
    gain2_ref,
    bias2_ref,
    low_v,
    full_v,
    lay_v,
    gtok_v,
    pool_v,
    vec_v,
    bq_v,
    bv_v,
    v0,
    v1,
    v2,
    v3,
    v4,
    v5,
    v6,
    in_sem,
    out_sem,
    side_sem,
    vec_sem,
):
    chunk = low_v.shape[0] // 3
    width = low_v.shape[1]
    ins = []
    pieces = []
    for c, dst in ((0, wout_hbm), (1, win_hbm)):
        for r in range(0, width, 256):
            pieces.append((c * chunk + r, c * width + r, dst.at[pl.ds(r, 256)], 256))
    for k, dst in enumerate((wq_hbm, wk_hbm, wv_hbm, wo_hbm)):
        pieces.append((2 * chunk + k * qw, 2 * width + k * qw, dst, qw))
    ins = [
        pltpu.make_async_copy(gw_hbm.at[pl.ds(src, n)], low_v.at[pl.ds(src, n)], in_sem.at[k])
        for k, (src, _, _, n) in enumerate(pieces)
    ]
    for copy in ins:
        copy.start()
    lay_copy = pltpu.make_async_copy(lay_in, lay_v, side_sem.at[0])
    gtok_copy = pltpu.make_async_copy(gtok_in, gtok_v, side_sem.at[1])
    pool_copy = pltpu.make_async_copy(pool_in, pool_v, side_sem.at[2])
    vec_copy = pltpu.make_async_copy(vec_in, vec_v, side_sem.at[5])
    lay_copy.start()
    gtok_copy.start()
    pool_copy.start()
    vec_copy.start()
    outs = []
    for k, (src, at, dst, n) in enumerate(pieces):
        ins[k].wait()
        full_v[pl.ds(at, n), :] = low_v[pl.ds(src, n), :].astype(F32)
        copy = pltpu.make_async_copy(full_v.at[pl.ds(at, n)], dst, out_sem.at[k])
        copy.start()
        outs.append(copy)
    lay_copy.wait()
    outs.append(pltpu.make_async_copy(lay_v, lay_hbm, side_sem.at[3]))
    outs[-1].start()
    gtok_copy.wait()
    outs.append(pltpu.make_async_copy(gtok_v, gtok_hbm, side_sem.at[4]))
    outs[-1].start()
    vec_copy.wait()
    short = (bq_v, bv_v, v0, v1, v2, v3, v4, v5, v6)
    bq_v[...] = vec_v[0, pl.ds(0, qw)]
    bv_v[...] = vec_v[0, pl.ds(256, qw)]
    for k in range(7):
        short[2 + k][...] = vec_v[1 + k, :]
    dsts = (bq_ref, bv_ref, bin_ref, battn_ref, gain1_ref, bias1_ref, bout_ref, gain2_ref, bias2_ref)
    for k, dst in enumerate(dsts):
        outs.append(pltpu.make_async_copy(short[k], dst, vec_sem.at[k]))
        outs[-1].start()
    pool_copy.wait()
    outs.append(pltpu.make_async_copy(pool_v, pool_hbm, vec_sem.at[9]))
    outs[-1].start()
    for copy in outs:
        copy.wait()


def unpack_call(qw, lay, pooled, gtok, gw, vec):
    width = gw.shape[1]
    anyspec = pl.BlockSpec(memory_space=pl.ANY)
    like = lambda v: jax.ShapeDtypeStruct(v.shape, v.dtype)
    mat = lambda n: jax.ShapeDtypeStruct((n, width), F32)
    one = lambda n: jax.ShapeDtypeStruct((n,), F32)
    outs = pl.pallas_call(
        lambda *refs: unpack_kernel(qw, *refs),
        out_shape=(
            like(lay),
            like(pooled),
            like(gtok),
            mat(qw),
            one(qw),
            mat(qw),
            mat(qw),
            one(qw),
            mat(qw),
            one(width),
            one(width),
            one(width),
            mat(width),
            one(width),
            mat(width),
            one(width),
            one(width),
            one(width),
        ),
        in_specs=[anyspec] * 5,
        out_specs=(anyspec,) * 18,
        scratch_shapes=[
            pltpu.VMEM(gw.shape, BF16),
            pltpu.VMEM((3 * width, width), F32),
            pltpu.VMEM(lay.shape, BF16),
            pltpu.VMEM(gtok.shape, BF16),
            pltpu.VMEM(pooled.shape, F32),
            pltpu.VMEM(vec.shape, F32),
            pltpu.VMEM((qw,), F32),
            pltpu.VMEM((qw,), F32),
            pltpu.VMEM((width,), F32),
            pltpu.VMEM((width,), F32),
            pltpu.VMEM((width,), F32),
            pltpu.VMEM((width,), F32),
            pltpu.VMEM((width,), F32),
            pltpu.VMEM((width,), F32),
            pltpu.VMEM((width,), F32),
            pltpu.SemaphoreType.DMA((12,)),
            pltpu.SemaphoreType.DMA((12,)),
            pltpu.SemaphoreType.DMA((6,)),
            pltpu.SemaphoreType.DMA((10,)),
        ],
        compiler_params=pltpu.CompilerParams(vmem_limit_bytes=63 << 20),
    )(gw, lay, gtok, pooled, vec)
    return tuple(v.T if k in (3, 5, 6) else v for k, v in enumerate(outs))


def shards(*args):
    batch_size = lax.axis_size("batch")
    tp_size = lax.axis_size("tp")
    return unpack_call(args[6].shape[0], *layer_call(batch_size, tp_size, args))


def solution(mesh):
    placed = (
        P("batch", None),
        P(None, "tp"),
        P("tp"),
        P(None, "tp"),
        P(None, "tp"),
        P("tp"),
        P("tp", None),
        P(),
        P(),
        P(),
        P(None, "tp"),
        P("tp"),
        P("tp", None),
        P(),
        P(),
        P(),
        P("batch"),
        P("batch", None),
    )
    return jax.shard_map(
        shards,
        mesh=mesh,
        in_specs=placed,
        out_specs=(
            P(("batch", "tp"), None),
            P("batch", None),
            P(("batch", "tp"), None),
            P(None, "tp"),
            P("tp"),
            P(None, "tp"),
            P(None, "tp"),
            P("tp"),
            P("tp", None),
            P(),
            P(),
            P(),
            P(None, "tp"),
            P("tp"),
            P("tp", None),
            P(),
            P(),
            P(),
        ),
        check_vma=False,
    )
```
